32 devices in a mesh: draws: 2 (over x), spec: 16 (over z, y, core).
Axes of the slice: x: 2, y: 2, z: 4, core: 2. Of those that a mesh axis runs over, the one named last changes fastest.
Arguments:
- coefficients: bfloat16 [1280, 2, 320, 128], P('draws', None, 'spec'), parts along dimension 0, may hold values from -6 to 6
- legendre: float32 [640, 2, 320, 16], P('spec'), as said below
- row_counts: int32 [16], P('spec'), may hold values from 640 to 1280, as said below
- basis: float32 [64, 128], replicated, may hold values from -0.75 to 0.75
- absorb: float32 [128], replicated, may hold values from 0.00390625 to 0.0625
- peak_level: int32 [512], replicated, may hold values from 0 to 127
- width: float32 [512], replicated, may hold values from 1.5 to 12
Outputs:
- radiance: float32 [32, 2, 1280, 512], P(('draws', 'spec')), parts along dimension 0
The draws below stay inside these ranges and needn't reach their ends.
There are 2 independent parts, one for each index of `draws`. The reference program is written for one: setup_inputs(seed, part) draws one part's arguments, and reference() takes and returns one part's arrays. A program takes and returns all parts, laid end to end along the dimension named above; an argument that names none is the same for every part. Nothing has to cross between parts.
Inputs may be any that keep to these rules, and one draw needn't show every extreme that they name: `legendre`: entry [m, p, s, j] is the associated Legendre function of order m and degree m + 2 s + p, normalised to unit square integral over [-1, 1], at the cosine of a drawn colatitude of row j in the northern hemisphere; it is zero where the degree exceeds 640 - 1. `row_counts`: every count is a multiple of 4; row 0 has 1280 longitudes and row 1 has 640.
All inputs are finite; a program needn't handle non-finite values.
Results may differ from the reference program's by a relative error of at most 0.0003.
Values sent between devices are 32-bit elements; how exact they have to be, the bound alone decides.
A program may use at most 128 MiB of HBM per device.

```python
import math
import jax
import jax.numpy as jnp
from jax import lax

MW = 640
NE = 320
NLON = 1280
NCH = 512
LEV = 128
K = 64
PR = 16


def draw_legendre(key, part):
    jitter = jax.random.uniform(key, (PR,), jnp.float32)
    colatitude = 0.5 * math.pi * (jnp.arange(PR, dtype=jnp.float32) + 0.2 + 0.6 * jitter) / PR
    cosine = jnp.cos(colatitude)
    log_sine = jnp.log(jnp.sin(colatitude))
    orders = jnp.arange(MW, dtype=jnp.float32)
    growth = jnp.concatenate((jnp.zeros((1,), jnp.float32), 0.5 * jnp.log((2.0 * orders[1:] + 1.0) / (2.0 * orders[1:]))))
    log_start = 0.5 * math.log(0.5) + jnp.cumsum(growth)
    diagonal_start = jnp.exp(log_start[:, None] + orders[:, None] * log_sine[None, :])

    def advance(carry, offset):
        previous, current = carry
        degree = orders + offset
        below = degree - 1.0
        coupling_now = jnp.sqrt(jnp.maximum((degree * degree - orders * orders) / (4.0 * degree * degree - 1.0), 0.0))
        coupling_prev = jnp.sqrt(jnp.maximum((below * below - orders * orders) / (4.0 * below * below - 1.0), 0.0))
        following = (cosine[None, :] * current - coupling_prev[:, None] * previous) / coupling_now[:, None]
        return ((current, following), following)
    offsets = jnp.arange(1, MW, dtype=jnp.float32)
    carried, values = lax.scan(advance, (jnp.zeros_like(diagonal_start), diagonal_start), offsets)
    whole = jnp.concatenate((diagonal_start[None], values), axis=0)
    degree_offset = jnp.arange(MW, dtype=jnp.int32)[:, None, None]
    order_index = jnp.arange(MW, dtype=jnp.int32)[None, :, None]
    whole = jnp.where(degree_offset + order_index < MW, whole, jnp.zeros_like(whole))
    arranged = whole.reshape(MW // 2, 2, MW, PR)
    return jnp.transpose(arranged, (2, 1, 0, 3)).astype(jnp.float32)


def draw_row_counts(key, part):
    increments = jax.random.randint(key, (PR,), 0, NLON // 8 + 1)
    counts = NLON // 2 + 4 * increments
    counts = counts.at[0].set(NLON).at[1].set(NLON // 2)
    return counts.astype(jnp.int32)


def set_ends(values, rng, low, high):
    index_at = [jax.random.randint(jax.random.fold_in(rng, axis), (), 0, length) for axis, length in enumerate(values.shape)]
    main_axis = values.shape.index(max(values.shape))
    next_to = index_at[:main_axis] + [(index_at[main_axis] + 1) % values.shape[main_axis]] + index_at[main_axis + 1:]
    return values.at[tuple(index_at)].set(low).at[tuple(next_to)].set(high)


def shard_levels(own_key, extent, cuts, smallest, top_value):
    gain, own = 1.0, jax.random.fold_in(own_key, 6)
    for position, parts in cuts:
        draws = jnp.exp(jax.random.uniform(jax.random.fold_in(own, position), (parts,), jnp.float32, smallest / len(cuts), top_value / len(cuts)))
        gain = gain * jnp.repeat(draws, extent[position] // parts).reshape([-1 if axis == position else 1 for axis in range(len(extent))])
    return gain


def centred(own_key, extent, scale, most, cuts=(), kind=jnp.bfloat16):
    entries = scale * jax.random.normal(own_key, extent, jnp.float32)
    if cuts:
        entries = entries * shard_levels(own_key, extent, cuts, -0.22, 0.18)
    return jnp.clip(entries, -most, most).astype(kind)


def setup_inputs(seed: int = 0, part: int = 0) -> dict:
    streams_of = jax.random.split(jax.random.key(seed), 8)
    part_splits = jax.random.split(jax.random.fold_in(streams_of[7], part), 8)
    coefficients = centred(part_splits[0], (MW, 2, NE, 2 * K), 1.0, 6.0, ((2, 16),))
    legendre = draw_legendre(jax.random.fold_in(streams_of[7], 71), part)
    row_counts = draw_row_counts(jax.random.fold_in(streams_of[7], 71), part)
    basis = centred(streams_of[3], (K, LEV), K ** -0.5, 0.75, (), jnp.float32)
    absorb = jnp.clip(jnp.exp(jax.random.uniform(streams_of[4], (LEV,), jnp.float32, math.log(0.00390625), math.log(0.0625))), 0.00390625, 0.0625)
    peak_level = set_ends(jax.random.randint(streams_of[5], (NCH,), 0, LEV), jax.random.fold_in(streams_of[5], 1), 0, LEV - 1).astype(jnp.int32)
    width = jnp.clip(jnp.exp(jax.random.uniform(streams_of[6], (NCH,), jnp.float32, math.log(1.5), math.log(12.0))), 1.5, 12.0)
    return {"coefficients": coefficients, "legendre": legendre, "row_counts": row_counts, "basis": basis, "absorb": absorb, "peak_level": peak_level, "width": width}


PRECISE = lax.Precision.HIGHEST

def prior_scale(shard, first):
    waves = shard.shape[0]
    slots = shard.shape[2]
    orders = jnp.arange(waves, dtype=jnp.int32)[:, None, None]
    parity = jnp.arange(2, dtype=jnp.int32)[None, :, None]
    slot_index = first + jnp.arange(slots, dtype=jnp.int32)[None, None, :]
    degree = orders + 2 * slot_index + parity
    spread = lax.rsqrt((degree + 1).astype(jnp.float32) * waves)
    spread = jnp.where(degree < waves, spread, jnp.zeros_like(spread))
    return shard.astype(jnp.float32) * spread[..., None]

def expand_levels(values, modes_basis):
    lead = values.shape[:-1]
    halves = values.reshape(lead + (2, modes_basis.shape[0]))
    expanded = jnp.einsum('abcqk,kl->abcql', halves, modes_basis, precision=PRECISE)
    return expanded.reshape(lead + (2 * modes_basis.shape[1],))

def channel_kernel(peak_level, width, levels):
    height = jnp.arange(levels, dtype=jnp.float32)[:, None]
    offsets = (height - peak_level.astype(jnp.float32)[None, :]) / width[None, :]
    weights = jnp.exp(-offsets * offsets)
    return weights / lax.optimization_barrier(jnp.sum(weights, axis=0, keepdims=True))

def radiate(temps, absorb, kernel):
    levels = temps.shape[-1]
    strict_upper = (jnp.arange(levels)[:, None] < jnp.arange(levels)[None, :]).astype(jnp.float32)
    source = jnp.exp(0.5 * temps)
    layers = absorb[None, :] * source
    overhead = jnp.dot(layers, strict_upper, precision=PRECISE, preferred_element_type=jnp.float32)
    emitted = source * jnp.exp(-overhead) * -jnp.expm1(-layers)
    return jnp.dot(emitted, kernel, precision=PRECISE, preferred_element_type=jnp.float32)

def fourier_lookup(row_count, waves, points):
    orders = jnp.arange(waves, dtype=jnp.int32)
    places = jnp.arange(points, dtype=jnp.int32)
    phases = places[:, None] * orders[None, :] % row_count
    angles = 2.0 * math.pi * phases.astype(jnp.float32) / row_count.astype(jnp.float32)
    weights = jnp.where(orders == 0, 1.0, 2.0) * (2 * orders < row_count).astype(jnp.float32)
    return jnp.stack((weights * jnp.cos(angles), -weights * jnp.sin(angles)), axis=-1)

def synthesize_row(spectra, row_count, modes_basis, absorb, kernel, points):
    waves, hemis, columns = spectra.shape
    lookup = fourier_lookup(row_count, waves, points)
    split_parts = spectra.reshape(waves, hemis, 2, columns // 2)
    fields = jnp.einsum('kmq,mhqc->hkc', lookup, split_parts, precision=PRECISE)
    if modes_basis is not None:
        fields = jnp.einsum('hkc,cl->hkl', fields, modes_basis, precision=PRECISE)
    levels = fields.shape[-1]
    bright = radiate(fields.reshape(hemis * points, levels), absorb, kernel)
    bright = bright.reshape(hemis, points, kernel.shape[1])
    inside = (jnp.arange(points, dtype=jnp.int32) < row_count).astype(jnp.float32)
    return bright * inside[None, :, None]

def reference(coefficients, legendre, row_counts, basis, absorb, peak_level, width):
    scaled = prior_scale(coefficients, 0)
    spectral = expand_levels(scaled, basis)
    even_odd = jnp.einsum('mpsj,mpsc->mpjc', legendre, spectral, precision=PRECISE)
    fourier = jnp.stack((even_odd[:, 0] + even_odd[:, 1], even_odd[:, 0] - even_odd[:, 1]), axis=1)
    kernel = channel_kernel(peak_level, width, LEV)

    def one_row(inputs):
        spectra, row_count = inputs
        return synthesize_row(spectra, row_count, None, absorb, kernel, NLON)
    return lax.map(one_row, (jnp.moveaxis(fourier, 2, 0), row_counts))
```

```python
import math

import jax
import jax.numpy as jnp
from jax import lax
from jax.experimental import pallas as pl
from jax.experimental.pallas import tpu as pltpu
from jax.sharding import PartitionSpec as P

NLON = 1280
FINE = 256
LANES = 128

PRECISE = lax.Precision.HIGHEST
F32 = jnp.float32
BF16 = jnp.bfloat16


def prior_spread(orders, slots, waves):
    parity = jnp.arange(2, dtype=jnp.int32)[None, :, None]
    degree = orders[:, None, None] + 2 * slots[None, None, :] + parity
    spread = lax.rsqrt((degree + 1).astype(F32) * waves)
    return jnp.where(degree < waves, spread, jnp.zeros_like(spread))


def split(x):
    high = x.astype(BF16)
    return high, (x - high.astype(F32)).astype(BF16)


def dot(a, b):
    return jnp.dot(a, b, preferred_element_type=F32)


def dot3(a, b):
    ah, al = split(a)
    bh, bl = split(b)
    return dot(ah, bh) + dot(al, bh) + dot(ah, bl)


def place_in_ring(n):
    me = lax.axis_index("spec")
    core = me % 2
    side = (me // 2) % 2
    layer = me // 4
    return me, core, side, layer


def trig_tile(tile, count, spectra_ref, basis_ref, fcos_ref, fsin_ref, temps_ref):
    points, lanes = fcos_ref.shape
    steps = temps_ref.shape[0] // points
    tiny = 16
    middle = points // tiny
    coarse = -(-steps // 8) * 8
    whole = count.astype(F32)
    table = (tiny + middle + coarse, lanes)
    index = lax.broadcasted_iota(jnp.int32, table, 0)
    order = lax.broadcasted_iota(jnp.int32, table, 1) + tile * lanes
    places = jnp.where(index < tiny, index, (index - tiny) * tiny)
    places = jnp.where(index < tiny + middle, places, (index - tiny - middle) * points)
    phases = (places * order).astype(F32)
    phases = phases - jnp.floor(phases / whole) * whole
    angles = 2.0 * math.pi * phases / whole
    cosine, sine = jnp.cos(angles), jnp.sin(angles)
    weights = jnp.where(order == 0, 1.0, 2.0) * jnp.where(2 * order < count, 1.0, 0.0)
    first = tiny + middle
    base_c, base_s = (cosine * weights)[first:], (sine * weights)[first:]
    for b in range(middle):
        turn_c, turn_s = cosine[tiny + b:tiny + b + 1], sine[tiny + b:tiny + b + 1]
        fcos_ref[pl.ds(b * tiny, tiny), :] = cosine[:tiny] * turn_c - sine[:tiny] * turn_s
        fsin_ref[pl.ds(b * tiny, tiny), :] = sine[:tiny] * turn_c + cosine[:tiny] * turn_s

    even = spectra_ref[pl.ds(2 * lanes * tile, lanes, stride=2), :]
    odd = spectra_ref[pl.ds(2 * lanes * tile + 1, lanes, stride=2), :]
    half = even.shape[1] // 2
    real = jnp.concatenate((even[:, :half], odd[:, :half]), axis=1)
    imag = jnp.concatenate((even[:, half:], odd[:, half:]), axis=1)
    basis = basis_ref[...]
    top = jnp.concatenate((basis, basis), axis=1)
    wide = jnp.concatenate((top, jnp.concatenate((basis, -basis), axis=1)), axis=0)
    high, low = split(dot3(jnp.concatenate((real, imag), axis=0), wide))
    fine_c, fine_s = fcos_ref[...], fsin_ref[...]
    for step in range(steps):
        turn_c, turn_s = base_c[step:step + 1], base_s[step:step + 1]
        lookup_c = turn_c * fine_c - turn_s * fine_s
        lookup_s = -(turn_s * fine_c + turn_c * fine_s)
        lookup_high, lookup_low = split(jnp.concatenate((lookup_c, lookup_s), axis=1))
        temps = dot(jnp.concatenate((lookup_high, lookup_low), axis=0), high)
        temps = temps[:points] + temps[points:] + dot(lookup_high, low)
        at = pl.ds(step * points, points)
        if tile == 0:
            temps_ref[at, :] = temps
        else:
            temps_ref[at, :] += temps


def exchange_kernel(
    n, waves, count_ref, coef_hbm, leg_ref, basis_ref, temps_ref, coef_ref, turn_ref, raw_ref, send_ref, seed_ref,
    wide_ref, sums_ref, near_ref, side_ref, far_ref, spectra_ref, fcos_ref, fsin_ref, coef_sem, seed_send, seed_recv,
    near_send, near_recv, side_send, side_recv, far_send, far_recv, diag_send,
):
    me, core, side, layer = place_in_ring(n)
    layers = n // 4
    chunks = n
    chip = me // 2
    rows = n
    columns = coef_hbm.shape[1]
    every = leg_ref.shape[1]
    slots = every // n
    lanes = LANES
    pairs = lanes // rows
    per = pairs // 2
    own = waves // n
    groups = own // per
    depth = per * slots * 2
    part = groups * pairs
    room = seed_ref.shape[1] // 2
    partner = me + 1 - 2 * core
    across = me + 2 - 4 * side

    def spot(z, y, c):
        return (z * 2 + y) * 2 + c

    def remote(src, dst, send_sem, recv_sem, target):
        return pltpu.make_async_remote_copy(
            src_ref=src, dst_ref=dst, send_sem=send_sem, recv_sem=recv_sem,
            device_id={"spec": target}, device_id_type=pl.DeviceIdType.MESH,
        )

    def seed_copy(source, target):
        return remote(send_ref.at[target], seed_ref.at[source], seed_send.at[target], seed_recv.at[source], target)

    def near_copy(q):
        return remote(sums_ref.at[q, 1 - core], near_ref.at[q], near_send.at[q], near_recv.at[q], partner)

    def side_copy(q, z):
        return remote(
            sums_ref.at[q, core, 1 - side, z], side_ref.at[q, z], side_send.at[q, z], side_recv.at[q, z], across
        )

    def far_copy(q, source, target):
        return remote(
            sums_ref.at[q, core, side, target], far_ref.at[source, q],
            far_send.at[target, q], far_recv.at[source, q], spot(target, side, core),
        )

    def diag_copy(q, target):
        return remote(
            sums_ref.at[q, core, 1 - side, target], far_ref.at[layer, q],
            diag_send.at[target, q], far_recv.at[layer, q], spot(target, 1 - side, core),
        )

    def signal(target):
        pl.semaphore_signal(barrier, inc=1, device_id={"spec": target}, device_id_type=pl.DeviceIdType.MESH)

    corners = [(dy, dc) for dy in range(2) for dc in range(2)]

    def corner(z, offset):
        dy, dc = offset
        return spot(z, (side + dy) % 2, (core + dc) % 2)

    coef_copy = pltpu.make_async_copy(coef_hbm, coef_ref, coef_sem)
    coef_copy.start()
    barrier = pltpu.get_barrier_semaphore()
    for offset in corners[1:]:
        signal(corner(layer, offset))

    @pl.when(layer > 0)
    def _():
        for dz in range(1, layers - 1):
            for offset in corners:
                signal(corner(1 + (layer - 1 + dz) % (layers - 1), offset))

    row = lax.broadcasted_iota(jnp.int32, (lanes, lanes), 0)
    lane = lax.broadcasted_iota(jnp.int32, (lanes, lanes), 1)
    row_at = row % rows
    ordered = ((row_at % 2) * 2 + (row_at // 2) % 2) * layers + row_at // 4
    moves = jnp.where(ordered * pairs + row // rows == lane, 1.0, 0.0).astype(BF16)

    raw_ref[...] = jnp.zeros(raw_ref.shape, F32)
    for g in range(groups):
        turn_ref[...] = jnp.transpose(leg_ref[pl.ds(g * lanes, lanes), :])
        raw_ref[pl.ds(g, n, stride=2 * room), :] = turn_ref[pl.ds(0, n, stride=slots), :]
        raw_ref[pl.ds(room + g, n, stride=2 * room), :] = turn_ref[pl.ds(1, n, stride=slots), :]
    start = jnp.broadcast_to(raw_ref[pl.ds(0, 1), :], (8, lanes))
    cosine = pltpu.roll(start, lanes - rows, 1) / start
    sine = pltpu.roll(start, lanes - 2 * rows, 1) / start
    sine = sine * sine * (2.0 / 3.0)
    square = jnp.where(sine < 0.5, 1.0 - sine, cosine * cosine * (1.0 / 3.0))
    square = jnp.where(lax.broadcasted_iota(jnp.int32, (8, lanes), 1) < rows, square, 0.0)
    shift = rows
    while shift < lanes:
        square = square + pltpu.roll(square, shift, 1)
        shift *= 2
    square = jnp.where(me == 0, square, 0.0)
    raw_ref[pl.ds(groups, n, stride=2 * room), :] = jnp.broadcast_to(square[:1], (n, lanes))
    raw = raw_ref[...]
    high = raw.astype(BF16)
    rest = raw - high.astype(F32)
    middle = rest.astype(BF16)
    low = (rest - middle.astype(F32)).astype(BF16)
    send_ref[...] = (dot(high, moves) + (dot(middle, moves) + dot(low, moves))).reshape(send_ref.shape)
    seed_ref[me] = send_ref[me]

    def give_seeds(z, offset):
        target = corner(z, offset)

        @pl.when(me + target < n)
        def _():
            seed_copy(me, target).start()

    @pl.when(layer == 0)
    def _():
        pl.semaphore_wait(barrier, len(corners) - 1)
        for dz in range(1, layers):
            for offset in corners:
                signal(corner(dz, offset))
        for offset in corners[1:]:
            give_seeds(layer, offset)

    @pl.when(layer > 0)
    def _():
        pl.semaphore_wait(barrier, n - 1)
        for offset in corners:
            signal(corner(0, offset))
        for offset in corners[1:]:
            give_seeds(layer, offset)
        for dz in range(1, layers):
            for offset in corners:
                give_seeds((layer + dz) % layers, offset)

    def meet():
        @pl.when(layer == 0)
        def _():
            pl.semaphore_wait(barrier, n - len(corners))
            for dz in range(1, layers):
                for offset in corners:
                    give_seeds(dz, offset)

    coef_copy.wait()

    expand_row = lax.broadcasted_iota(jnp.int32, (depth, lanes), 0)
    expand_lane = lax.broadcasted_iota(jnp.int32, (depth, lanes), 1) % pairs
    keep = (expand_row // (2 * slots)) * 2 + expand_row % 2 == expand_lane
    pair_at = lax.broadcasted_iota(jnp.int32, (room, lanes), 1) % pairs
    order_part = lax.broadcasted_iota(jnp.int32, (room, lanes), 0) * per + pair_at // 2

    def recur(owner):
        order = order_part + owner * own
        first = order + pair_at % 2 + me * (2 * slots)
        m = order.astype(F32)
        square = seed_ref[0, pl.ds(groups, 1), :]

        def coupling(d):
            return ((d - m) * (d + m)) / ((2.0 * d - 1.0) * (2.0 * d + 1.0))

        def place(s, value):
            degree = first + 2 * s
            spread = lax.rsqrt((degree + 1).astype(F32) * float(waves))
            value = value * jnp.where(degree < waves, spread, 0.0)
            wide_ref[pl.ds(2 * s, room, stride=2 * slots), :] = value
            wide_ref[pl.ds(2 * s + 1, room, stride=2 * slots), :] = value

        before = seed_ref[owner, pl.ds(0, room), :]
        now = seed_ref[owner, pl.ds(room, room), :]
        place(0, before)
        place(1, now)
        degree = first.astype(F32)
        last = coupling(degree + 2.0)
        weight = jnp.sqrt(coupling(degree + 1.0) * last)
        for s in range(1, slots - 1):
            degree = degree + 2.0
            one, two = coupling(degree + 1.0), coupling(degree + 2.0)
            product = one * two
            inverse = lax.rsqrt(product)
            before, now = now, ((square - (one + last)) * now - weight * before) * inverse
            weight = product * inverse
            last = two
            place(s + 1, now)

    def partial(owner):
        @pl.when(me + owner < n)
        def _():
            @pl.when(owner != me)
            def _():
                seed_copy(owner, me).wait_recv()

            recur(owner)

            @pl.loop(0, groups // 2)
            def _(double):
                for half in range(2):
                    g = double * 2 + half
                    at = owner * groups + g
                    values = coef_ref[pl.ds(pl.multiple_of(at * depth, depth), depth), :]
                    one = wide_ref[pl.ds(pl.multiple_of(g * 2 * slots, 2 * slots), 2 * slots), :]
                    tiled = jnp.where(keep, jnp.concatenate([one] * per, axis=0), 0.0)
                    both = jnp.concatenate(split(tiled), axis=1)
                    sums = lax.dot_general(both, values, (((0,), (0,)), ((), ())), preferred_element_type=F32)
                    sums = (sums[:lanes] + sums[lanes:]).reshape(2, 2, layers, pairs, columns)
                    sums_ref[owner, :, :, :, pl.ds(pl.multiple_of(g * pairs, pairs), pairs), :] = sums

        @pl.when(me + owner >= n)
        def _():
            sums_ref[owner] = jnp.zeros((2, 2, layers, part, columns), F32)

    def held(q, place):
        return q + 2 * place < chunks

    def compute(q):
        @pl.when(held(q, chip))
        def _():
            partial(q)
            near_copy(q).start()

    def merge_near(q):
        shared = jnp.logical_and(held(q, chip), held(q, across // 2))
        alone = jnp.logical_and(held(q, chip), jnp.logical_not(held(q, across // 2)))

        @pl.when(held(q, chip))
        def _():
            near_copy(q).wait_recv()

            for y in (0, 1):
                @pl.loop(0, layers)
                def _(z):
                    sums_ref[q, core, y, z] += near_ref[q, y, z]

        @pl.when(shared)
        def _():
            for dz in range(1, layers):
                side_copy(q, (layer + dz) % layers).start()

        @pl.when(alone)
        def _():
            for dz in range(1, layers):
                far_copy(q, layer, (layer + dz) % layers).start()
                diag_copy(q, (layer + dz) % layers).start()

    def merge_side(q):
        @pl.when(jnp.logical_and(held(q, chip), held(q, across // 2)))
        def _():
            for dz in range(1, layers):
                z = (layer + dz) % layers
                side_copy(q, z).wait_recv()
                sums_ref[q, core, side, z] += side_ref[q, z]
                far_copy(q, layer, z).start()

    lag = 3

    @pl.loop(0, chunks + lag)
    def _(t):
        @pl.when(t < chunks)
        def _():
            compute(t)

        @pl.when(t == 1)
        def _():
            meet()

        @pl.when(jnp.logical_and(t >= 1, t <= chunks))
        def _():
            merge_near(t - 1)

        @pl.when(t == chunks)
        def _():
            @pl.loop(0, chunks)
            def _(q):
                @pl.when(held(q, chip))
                def _():
                    side_copy(q, layer).start()

        @pl.when(t >= lag)
        def _():
            merge_side(t - lag)

    def finish(q):
        at = pl.ds(pl.multiple_of(q * part, part), part)

        @pl.when(held(q, chip))
        def _():
            spectra_ref[at, :] = sums_ref[q, core, side, layer]

        @pl.when(jnp.logical_not(held(q, chip)))
        def _():
            spectra_ref[at, :] = jnp.zeros((part, columns), F32)

        for dz in range(1, layers):
            source = (layer + dz) % layers

            @pl.when(q + 4 * source < chunks)
            def _():
                far_copy(q, source, layer).wait_recv()
                spectra_ref[at, :] += far_ref[source, q]

        @pl.when(held(q, across // 2))
        def _():
            side_copy(q, layer).wait_recv()
            spectra_ref[at, :] += side_ref[q, layer]

    tiles = waves // lanes
    done = 0
    for tile in range(tiles):
        until = -(-(tile + 1) * lanes // own)

        @pl.loop(done, until)
        def _(q):
            finish(q)

        done = until
        trig_tile(tile, count_ref[0], spectra_ref, basis_ref, fcos_ref, fsin_ref, temps_ref)

    @pl.loop(0, n)
    def _(target):
        @pl.when(jnp.logical_and(target != me, me + target < n))
        def _():
            seed_copy(me, target).wait_send()

    @pl.loop(0, chunks)
    def _(q):
        @pl.when(held(q, chip))
        def _():
            near_copy(q).wait_send()
            side_copy(q, layer).wait_send()
            for dz in range(1, layers):
                z = (layer + dz) % layers
                far_copy(q, layer, z).wait_send()

                @pl.when(held(q, across // 2))
                def _():
                    side_copy(q, z).wait_send()

                @pl.when(jnp.logical_not(held(q, across // 2)))
                def _():
                    diag_copy(q, z).wait_send()


def exchanged_temps(coefficients, legendre, row_counts, basis, n, points):
    waves, _, slots, columns = coefficients.shape
    own, _, every, rows = legendre.shape
    dense = jnp.transpose(coefficients, (0, 2, 1, 3)).reshape(waves * slots * 2, columns)
    legs = jnp.transpose(legendre, (0, 1, 3, 2)).reshape(own * 2 * rows, every)
    layers, chunks = n // 4, n
    pairs = LANES // rows
    groups = own * 2 // pairs
    width = groups * pairs
    room = -(-(groups + 1) // 8) * 8
    dma = pltpu.SemaphoreType.DMA

    def body(*refs):
        exchange_kernel(n, waves, *refs)

    vmem = pl.BlockSpec(memory_space=pltpu.VMEM)
    return pl.pallas_call(
        body,
        out_shape=jax.ShapeDtypeStruct((points, 2 * basis.shape[1]), F32),
        in_specs=[pl.BlockSpec(memory_space=pltpu.SMEM), pl.BlockSpec(memory_space=pl.ANY), vmem, vmem],
        out_specs=vmem,
        scratch_shapes=[
            pltpu.VMEM(dense.shape, BF16),
            pltpu.VMEM((every, LANES), F32),
            pltpu.VMEM((n * 2 * room, LANES), F32),
            pltpu.VMEM((n, 2 * room, LANES), F32),
            pltpu.VMEM((n, 2 * room, LANES), F32),
            pltpu.VMEM((room * 2 * slots, LANES), F32),
            pltpu.VMEM((chunks, 2, 2, layers, width, columns), F32),
            pltpu.VMEM((chunks, 2, layers, width, columns), F32),
            pltpu.VMEM((chunks, layers, width, columns), F32),
            pltpu.VMEM((layers, chunks, width, columns), F32),
            pltpu.VMEM((2 * waves, columns), F32),
            pltpu.VMEM((FINE, LANES), F32),
            pltpu.VMEM((FINE, LANES), F32),
            dma, dma((n,)), dma((n,)),
            dma((chunks,)), dma((chunks,)),
            dma((chunks, layers)), dma((chunks, layers)),
            dma((layers, chunks)), dma((layers, chunks)), dma((layers, chunks)),
        ],
        compiler_params=pltpu.CompilerParams(
            collective_id=0, has_side_effects=True, vmem_limit_bytes=58 * 1024 * 1024
        ),
        name="exchanged_temps",
    )(row_counts, dense, legs, basis)


def plain_temps(spectra, row_counts, basis, points):
    tiles = spectra.shape[0] // (2 * LANES)

    def body(count_ref, spectra_ref, basis_ref, temps_ref, fcos_ref, fsin_ref):
        for tile in range(tiles):
            trig_tile(tile, count_ref[0], spectra_ref, basis_ref, fcos_ref, fsin_ref, temps_ref)

    vmem = pl.BlockSpec(memory_space=pltpu.VMEM)
    return pl.pallas_call(
        body,
        out_shape=jax.ShapeDtypeStruct((points, 2 * basis.shape[1]), F32),
        in_specs=[pl.BlockSpec(memory_space=pltpu.SMEM), vmem, vmem],
        out_specs=vmem,
        scratch_shapes=[pltpu.VMEM((FINE, LANES), F32), pltpu.VMEM((FINE, LANES), F32)],
        name="plain_temps",
    )(row_counts, spectra, basis)


def row_kernel(count_ref, temps_ref, absorb_ref, peak_ref, width_ref, out_ref, rhigh_ref, rlow_ref):
    step = pl.program_id(0)
    levels = absorb_ref.shape[1]
    points = temps_ref.shape[0]

    @pl.when(step == 0)
    def _():
        height = lax.broadcasted_iota(jnp.int32, rlow_ref.shape, 0)
        offsets = (height - peak_ref[...]).astype(F32) / width_ref[...]
        shape = jnp.exp(-offsets * offsets)
        high, low = split(shape / jnp.sum(shape, axis=0, keepdims=True))
        rhigh_ref[pl.ds(0, levels), :] = high
        rhigh_ref[pl.ds(levels, levels), :] = high
        rlow_ref[...] = low

    temps = temps_ref[...]
    temps = jnp.concatenate((temps[:, :levels], temps[:, levels:]), axis=0)

    source = jnp.exp(0.5 * temps)
    layers = absorb_ref[...] * source
    before = lax.broadcasted_iota(jnp.int32, (2 * levels, levels), 0) % levels
    after = lax.broadcasted_iota(jnp.int32, (2 * levels, levels), 1)
    upper = jnp.where(before < after, 1.0, 0.0).astype(BF16)
    layers_high, layers_low = split(layers)
    above = dot(jnp.concatenate((layers_high, layers_low), axis=1), upper)
    emitted = source * jnp.exp(-above) * (1.0 - jnp.exp(-layers))
    place = step * points + lax.broadcasted_iota(jnp.int32, (2 * points, levels), 0) % points
    emitted = jnp.where(place < count_ref[0], emitted, 0.0)
    emitted_high, emitted_low = split(emitted)
    bright = dot(jnp.concatenate((emitted_high, emitted_low), axis=1), rhigh_ref[...])
    bright = bright + dot(emitted_high, rlow_ref[...])
    out_ref[0, 0] = bright[:points]
    out_ref[0, 1] = bright[points:]


def radiate_row(temps, row_counts, absorb, peak_level, width):
    points = temps.shape[0]
    levels, channels = absorb.shape[0], width.shape[0]

    def whole(*shape):
        return pl.BlockSpec(shape, lambda i, *_: (0,) * len(shape))

    return pl.pallas_call(
        row_kernel,
        out_shape=jax.ShapeDtypeStruct((1, 2, points, channels), F32),
        grid_spec=pltpu.PrefetchScalarGridSpec(
            num_scalar_prefetch=1,
            grid=(points // FINE,),
            in_specs=[
                pl.BlockSpec((FINE, 2 * levels), lambda i, *_: (i, 0)),
                whole(1, levels),
                whole(1, channels),
                whole(1, channels),
            ],
            out_specs=pl.BlockSpec((1, 2, FINE, channels), lambda i, *_: (0, 0, i, 0)),
            scratch_shapes=[
                pltpu.VMEM((2 * levels, channels), BF16),
                pltpu.VMEM((levels, channels), BF16),
            ],
        ),
        name="row_radiance",
    )(row_counts, temps, absorb[None, :], peak_level[None, :], width[None, :])


def moved_coefficients(coefficients, legendre):
    waves, _, slots, _ = coefficients.shape
    first = lax.axis_index("spec") * slots
    spread = prior_spread(jnp.arange(waves, dtype=jnp.int32), first + jnp.arange(slots, dtype=jnp.int32), waves)
    scaled = coefficients.astype(F32) * spread[..., None]
    spectral = lax.all_to_all(scaled, "spec", split_axis=0, concat_axis=2, tiled=True)
    sums = jnp.einsum("mpsj,mpsc->mpjc", legendre, spectral, precision=PRECISE)
    sums = lax.all_to_all(sums, "spec", split_axis=2, concat_axis=0, tiled=True)
    return sums.reshape(2 * waves, sums.shape[-1])


def on_device(coefficients, legendre, row_counts, basis, absorb, peak_level, width):
    own, _, every, rows = legendre.shape
    waves, _, slots, columns = coefficients.shape
    n = waves // own
    fits = n == rows and n % 8 == 0 and LANES % n == 0 and every == n * slots and columns == LANES
    fits = fits and (LANES // n) % 8 == 0 and own % (LANES // n) == 0 and slots % 4 == 0 and waves % LANES == 0
    if fits and (slots * LANES // n) % 16 == 0 and 2 * waves >= 2 * slots * n:
        temps = exchanged_temps(coefficients, legendre, row_counts, basis, n, NLON)
    else:
        spectra = moved_coefficients(coefficients, legendre)
        temps = plain_temps(spectra, row_counts, basis, NLON)
    return radiate_row(temps, row_counts, absorb, peak_level, width)


def solution(mesh):
    placed = (
        P("draws", None, "spec", None),
        P("spec", None, None, None),
        P("spec"),
        P(),
        P(),
        P(),
        P(),
    )
    return jax.shard_map(
        on_device,
        mesh=mesh,
        in_specs=placed,
        out_specs=P(("draws", "spec"), None, None, None),
        check_vma=False,
    )
```

```python
import math

import jax
import jax.numpy as jnp
from jax import lax
from jax.experimental import pallas as pl
from jax.experimental.pallas import tpu as pltpu
from jax.sharding import PartitionSpec as P

NLON = 1280
FINE = 256
LANES = 128

PRECISE = lax.Precision.HIGHEST
F32 = jnp.float32
BF16 = jnp.bfloat16


def prior_spread(orders, slots, waves):
    parity = jnp.arange(2, dtype=jnp.int32)[None, :, None]
    degree = orders[:, None, None] + 2 * slots[None, None, :] + parity
    spread = lax.rsqrt((degree + 1).astype(F32) * waves)
    return jnp.where(degree < waves, spread, jnp.zeros_like(spread))


def split(x):
    high = x.astype(BF16)
    return high, (x - high.astype(F32)).astype(BF16)


def dot(a, b):
    return jnp.dot(a, b, preferred_element_type=F32)


def dot3(a, b):
    ah, al = split(a)
    bh, bl = split(b)
    return dot(ah, bh) + dot(al, bh) + dot(ah, bl)


def place_in_ring(n):
    me = lax.axis_index("spec")
    core = me % 2
    side = (me // 2) % 2
    layer = me // 4
    return me, core, side, layer


def trig_tile(tile, count, spectra_ref, basis_ref, fcos_ref, fsin_ref, temps_ref):
    points, lanes = fcos_ref.shape
    steps = temps_ref.shape[0] // points
    tiny = 16
    middle = points // tiny
    coarse = -(-steps // 8) * 8
    whole = count.astype(F32)
    table = (tiny + middle + coarse, lanes)
    index = lax.broadcasted_iota(jnp.int32, table, 0)
    order = lax.broadcasted_iota(jnp.int32, table, 1) + tile * lanes
    places = jnp.where(index < tiny, index, (index - tiny) * tiny)
    places = jnp.where(index < tiny + middle, places, (index - tiny - middle) * points)
    phases = (places * order).astype(F32)
    phases = phases - jnp.floor(phases / whole) * whole
    angles = 2.0 * math.pi * phases / whole
    cosine, sine = jnp.cos(angles), jnp.sin(angles)
    weights = jnp.where(order == 0, 1.0, 2.0) * jnp.where(2 * order < count, 1.0, 0.0)
    first = tiny + middle
    base_c, base_s = (cosine * weights)[first:], (sine * weights)[first:]
    for b in range(middle):
        turn_c, turn_s = cosine[tiny + b:tiny + b + 1], sine[tiny + b:tiny + b + 1]
        fcos_ref[pl.ds(b * tiny, tiny), :] = cosine[:tiny] * turn_c - sine[:tiny] * turn_s
        fsin_ref[pl.ds(b * tiny, tiny), :] = sine[:tiny] * turn_c + cosine[:tiny] * turn_s

    even = spectra_ref[pl.ds(2 * lanes * tile, lanes, stride=2), :]
    odd = spectra_ref[pl.ds(2 * lanes * tile + 1, lanes, stride=2), :]
    half = even.shape[1] // 2
    real = jnp.concatenate((even[:, :half], odd[:, :half]), axis=1)
    imag = jnp.concatenate((even[:, half:], odd[:, half:]), axis=1)
    basis = basis_ref[...]
    top = jnp.concatenate((basis, basis), axis=1)
    wide = jnp.concatenate((top, jnp.concatenate((basis, -basis), axis=1)), axis=0)
    high, low = split(dot3(jnp.concatenate((real, imag), axis=0), wide))
    fine_c, fine_s = fcos_ref[...], fsin_ref[...]
    for step in range(steps):
        turn_c, turn_s = base_c[step:step + 1], base_s[step:step + 1]
        lookup_c = turn_c * fine_c - turn_s * fine_s
        lookup_s = -(turn_s * fine_c + turn_c * fine_s)
        lookup_high, lookup_low = split(jnp.concatenate((lookup_c, lookup_s), axis=1))
        temps = dot(jnp.concatenate((lookup_high, lookup_low), axis=0), high)
        temps = temps[:points] + temps[points:] + dot(lookup_high, low)
        at = pl.ds(step * points, points)
        if tile == 0:
            temps_ref[at, :] = temps
        else:
            temps_ref[at, :] += temps


def exchange_kernel(
    n, waves, count_ref, coef_hbm, leg_ref, basis_ref, temps_ref, coef_ref, turn_ref, raw_ref, send_ref, seed_ref,
    wide_ref, sums_ref, near_ref, side_ref, far_ref, up_ref, spectra_ref, fcos_ref, fsin_ref, coef_sem, seed_send, seed_recv,
    near_send, near_recv, side_send, side_recv, far_send, far_recv, up_recv, diag_send,
):
    me, core, side, layer = place_in_ring(n)
    layers = n // 4
    chunks = n
    chip = me // 2
    rows = n
    columns = coef_hbm.shape[1]
    every = leg_ref.shape[1]
    slots = every // n
    lanes = LANES
    pairs = lanes // rows
    per = pairs // 2
    own = waves // n
    groups = own // per
    depth = per * slots * 2
    part = groups * pairs
    room = seed_ref.shape[1] // 2
    partner = me + 1 - 2 * core
    across = me + 2 - 4 * side

    def spot(z, y, c):
        return (z * 2 + y) * 2 + c

    def remote(src, dst, send_sem, recv_sem, target):
        return pltpu.make_async_remote_copy(
            src_ref=src, dst_ref=dst, send_sem=send_sem, recv_sem=recv_sem,
            device_id={"spec": target}, device_id_type=pl.DeviceIdType.MESH,
        )

    def seed_copy(source, target):
        return remote(send_ref.at[target], seed_ref.at[source], seed_send.at[target], seed_recv.at[source], target)

    def near_copy(q):
        return remote(sums_ref.at[q, 1 - core], near_ref.at[q], near_send.at[q], near_recv.at[q], partner)

    def side_copy(q, z):
        return remote(
            sums_ref.at[q, core, 1 - side, z], side_ref.at[q, z], side_send.at[q, z], side_recv.at[q, z], across
        )

    def far_copy(q, source, target):
        return remote(
            sums_ref.at[q, core, side, target], far_ref.at[source, q],
            far_send.at[target, q], far_recv.at[source, q], spot(target, side, core),
        )

    def up_copy(q, target):
        return remote(
            sums_ref.at[q, core, side, target], up_ref.at[q, target],
            far_send.at[target, q], up_recv.at[q, target], spot((layer + 1) % layers, side, core),
        )

    def diag_copy(q, target):
        return remote(
            sums_ref.at[q, core, 1 - side, target], far_ref.at[layer, q],
            diag_send.at[target, q], far_recv.at[layer, q], spot(target, 1 - side, core),
        )

    def signal(target):
        pl.semaphore_signal(barrier, inc=1, device_id={"spec": target}, device_id_type=pl.DeviceIdType.MESH)

    corners = [(dy, dc) for dy in range(2) for dc in range(2)]

    def corner(z, offset):
        dy, dc = offset
        return spot(z, (side + dy) % 2, (core + dc) % 2)

    coef_copy = pltpu.make_async_copy(coef_hbm, coef_ref, coef_sem)
    coef_copy.start()
    barrier = pltpu.get_barrier_semaphore()
    for offset in corners[1:]:
        signal(corner(layer, offset))

    @pl.when(layer > 0)
    def _():
        for dz in range(1, layers - 1):
            for offset in corners:
                signal(corner(1 + (layer - 1 + dz) % (layers - 1), offset))

    row = lax.broadcasted_iota(jnp.int32, (lanes, lanes), 0)
    lane = lax.broadcasted_iota(jnp.int32, (lanes, lanes), 1)
    row_at = row % rows
    ordered = ((row_at % 2) * 2 + (row_at // 2) % 2) * layers + row_at // 4
    moves = jnp.where(ordered * pairs + row // rows == lane, 1.0, 0.0).astype(BF16)

    raw_ref[...] = jnp.zeros(raw_ref.shape, F32)
    for g in range(groups):
        turn_ref[...] = jnp.transpose(leg_ref[pl.ds(g * lanes, lanes), :])
        raw_ref[pl.ds(g, n, stride=2 * room), :] = turn_ref[pl.ds(0, n, stride=slots), :]
        raw_ref[pl.ds(room + g, n, stride=2 * room), :] = turn_ref[pl.ds(1, n, stride=slots), :]
    start = jnp.broadcast_to(raw_ref[pl.ds(0, 1), :], (8, lanes))
    cosine = pltpu.roll(start, lanes - rows, 1) / start
    sine = pltpu.roll(start, lanes - 2 * rows, 1) / start
    sine = sine * sine * (2.0 / 3.0)
    square = jnp.where(sine < 0.5, 1.0 - sine, cosine * cosine * (1.0 / 3.0))
    square = jnp.where(lax.broadcasted_iota(jnp.int32, (8, lanes), 1) < rows, square, 0.0)
    shift = rows
    while shift < lanes:
        square = square + pltpu.roll(square, shift, 1)
        shift *= 2
    square = jnp.where(me == 0, square, 0.0)
    raw_ref[pl.ds(groups, n, stride=2 * room), :] = jnp.broadcast_to(square[:1], (n, lanes))
    raw = raw_ref[...]
    high = raw.astype(BF16)
    rest = raw - high.astype(F32)
    middle = rest.astype(BF16)
    low = (rest - middle.astype(F32)).astype(BF16)
    send_ref[...] = (dot(high, moves) + (dot(middle, moves) + dot(low, moves))).reshape(send_ref.shape)
    seed_ref[me] = send_ref[me]

    def give_seeds(z, offset):
        target = corner(z, offset)

        @pl.when(me + target < n)
        def _():
            seed_copy(me, target).start()

    @pl.when(layer == 0)
    def _():
        pl.semaphore_wait(barrier, len(corners) - 1)
        for dz in range(1, layers):
            for offset in corners:
                signal(corner(dz, offset))
        for offset in corners[1:]:
            give_seeds(layer, offset)

    @pl.when(layer > 0)
    def _():
        pl.semaphore_wait(barrier, n - 1)
        for offset in corners:
            signal(corner(0, offset))
        for offset in corners[1:]:
            give_seeds(layer, offset)
        for dz in range(1, layers):
            for offset in corners:
                give_seeds((layer + dz) % layers, offset)

    def meet():
        @pl.when(layer == 0)
        def _():
            pl.semaphore_wait(barrier, n - len(corners))
            for dz in range(1, layers):
                for offset in corners:
                    give_seeds(dz, offset)

    coef_copy.wait()

    expand_row = lax.broadcasted_iota(jnp.int32, (depth, lanes), 0)
    expand_lane = lax.broadcasted_iota(jnp.int32, (depth, lanes), 1) % pairs
    keep = (expand_row // (2 * slots)) * 2 + expand_row % 2 == expand_lane
    pair_at = lax.broadcasted_iota(jnp.int32, (room, lanes), 1) % pairs
    order_part = lax.broadcasted_iota(jnp.int32, (room, lanes), 0) * per + pair_at // 2

    def recur(owner):
        order = order_part + owner * own
        first = order + pair_at % 2 + me * (2 * slots)
        m = order.astype(F32)
        square = seed_ref[0, pl.ds(groups, 1), :]

        def coupling(d):
            return ((d - m) * (d + m)) / ((2.0 * d - 1.0) * (2.0 * d + 1.0))

        def place(s, value):
            degree = first + 2 * s
            spread = lax.rsqrt((degree + 1).astype(F32) * float(waves))
            value = value * jnp.where(degree < waves, spread, 0.0)
            wide_ref[pl.ds(2 * s, room, stride=2 * slots), :] = value
            wide_ref[pl.ds(2 * s + 1, room, stride=2 * slots), :] = value

        before = seed_ref[owner, pl.ds(0, room), :]
        now = seed_ref[owner, pl.ds(room, room), :]
        place(0, before)
        place(1, now)
        degree = first.astype(F32)
        last = coupling(degree + 2.0)
        weight = jnp.sqrt(coupling(degree + 1.0) * last)
        for s in range(1, slots - 1):
            degree = degree + 2.0
            one, two = coupling(degree + 1.0), coupling(degree + 2.0)
            product = one * two
            inverse = lax.rsqrt(product)
            before, now = now, ((square - (one + last)) * now - weight * before) * inverse
            weight = product * inverse
            last = two
            place(s + 1, now)

    def partial(owner):
        @pl.when(me + owner < n)
        def _():
            @pl.when(owner != me)
            def _():
                seed_copy(owner, me).wait_recv()

            recur(owner)

            @pl.loop(0, groups // 2)
            def _(double):
                for half in range(2):
                    g = double * 2 + half
                    at = owner * groups + g
                    values = coef_ref[pl.ds(pl.multiple_of(at * depth, depth), depth), :]
                    one = wide_ref[pl.ds(pl.multiple_of(g * 2 * slots, 2 * slots), 2 * slots), :]
                    tiled = jnp.where(keep, jnp.concatenate([one] * per, axis=0), 0.0)
                    both = jnp.concatenate(split(tiled), axis=1)
                    sums = lax.dot_general(both, values, (((0,), (0,)), ((), ())), preferred_element_type=F32)
                    sums = (sums[:lanes] + sums[lanes:]).reshape(2, 2, layers, pairs, columns)
                    sums_ref[owner, :, :, :, pl.ds(pl.multiple_of(g * pairs, pairs), pairs), :] = sums

        @pl.when(me + owner >= n)
        def _():
            sums_ref[owner] = jnp.zeros((2, 2, layers, part, columns), F32)

    def held(q, place):
        return q + 2 * place < chunks

    def compute(q):
        @pl.when(held(q, chip))
        def _():
            partial(q)
            near_copy(q).start()

    def merge_near(q):
        shared = jnp.logical_and(held(q, chip), held(q, across // 2))

        @pl.when(held(q, chip))
        def _():
            near_copy(q).wait_recv()

            for y in (0, 1):
                @pl.loop(0, layers)
                def _(z):
                    sums_ref[q, core, y, z] += near_ref[q, y, z]

        @pl.when(shared)
        def _():
            for dz in reversed(range(1, layers)):
                side_copy(q, (layer + dz) % layers).start()

    def pass_on(q):
        shared = held(q, across // 2)

        @pl.when(held(q, chip))
        def _():
            for dz in reversed(range(1, layers)):
                z = (layer + dz) % layers
                upward = jnp.logical_and(z > layer + 1, held(q, chip + 2))

                @pl.when(shared)
                def _():
                    side_copy(q, z).wait_recv()
                    sums_ref[q, core, side, z] += side_ref[q, z]

                @pl.when(jnp.logical_and(layer > 0, z > layer))
                def _():
                    up_copy(q, z).wait_recv()
                    sums_ref[q, core, side, z] += up_ref[q, z]

                @pl.when(upward)
                def _():
                    up_copy(q, z).start()

                @pl.when(jnp.logical_not(upward))
                def _():
                    far_copy(q, layer, z).start()

                @pl.when(jnp.logical_not(shared))
                def _():
                    diag_copy(q, z).start()

    lag = 3

    @pl.loop(0, chunks + lag)
    def _(t):
        @pl.when(t < chunks)
        def _():
            compute(t)

        @pl.when(t == 1)
        def _():
            meet()

        @pl.when(jnp.logical_and(t >= 1, t <= chunks))
        def _():
            merge_near(t - 1)

        @pl.when(t == chunks - 2 * chip)
        def _():
            @pl.loop(0, chunks)
            def _(q):
                @pl.when(held(q, chip))
                def _():
                    side_copy(q, layer).start()

        @pl.when(t >= lag)
        def _():
            pass_on(t - lag)

    def finish(q):
        at = pl.ds(pl.multiple_of(q * part, part), part)

        @pl.when(held(q, chip))
        def _():
            spectra_ref[at, :] = sums_ref[q, core, side, layer]

        @pl.when(jnp.logical_not(held(q, chip)))
        def _():
            spectra_ref[at, :] = jnp.zeros((part, columns), F32)

        for dz in range(1, layers):
            source = (layer + dz) % layers

            passed = jnp.logical_and(source + 1 < layer, held(q, 2 * (source + 1) + side))

            @pl.when(jnp.logical_and(held(q, 2 * source), jnp.logical_not(passed)))
            def _():
                far_copy(q, source, layer).wait_recv()
                spectra_ref[at, :] += far_ref[source, q]

        @pl.when(held(q, across // 2))
        def _():
            side_copy(q, layer).wait_recv()
            spectra_ref[at, :] += side_ref[q, layer]

    tiles = waves // lanes
    done = 0
    for tile in range(tiles):
        until = -(-(tile + 1) * lanes // own)

        @pl.loop(done, until)
        def _(q):
            finish(q)

        done = until
        trig_tile(tile, count_ref[0], spectra_ref, basis_ref, fcos_ref, fsin_ref, temps_ref)

    @pl.loop(0, n)
    def _(target):
        @pl.when(jnp.logical_and(target != me, me + target < n))
        def _():
            seed_copy(me, target).wait_send()

    @pl.loop(0, chunks)
    def _(q):
        @pl.when(held(q, chip))
        def _():
            near_copy(q).wait_send()
            side_copy(q, layer).wait_send()
            for dz in range(1, layers):
                z = (layer + dz) % layers
                far_copy(q, layer, z).wait_send()

                @pl.when(held(q, across // 2))
                def _():
                    side_copy(q, z).wait_send()

                @pl.when(jnp.logical_not(held(q, across // 2)))
                def _():
                    diag_copy(q, z).wait_send()


def exchanged_temps(coefficients, legendre, row_counts, basis, n, points):
    waves, _, slots, columns = coefficients.shape
    own, _, every, rows = legendre.shape
    dense = jnp.transpose(coefficients, (0, 2, 1, 3)).reshape(waves * slots * 2, columns)
    legs = jnp.transpose(legendre, (0, 1, 3, 2)).reshape(own * 2 * rows, every)
    layers, chunks = n // 4, n
    pairs = LANES // rows
    groups = own * 2 // pairs
    width = groups * pairs
    room = -(-(groups + 1) // 8) * 8
    dma = pltpu.SemaphoreType.DMA

    def body(*refs):
        exchange_kernel(n, waves, *refs)

    vmem = pl.BlockSpec(memory_space=pltpu.VMEM)
    return pl.pallas_call(
        body,
        out_shape=jax.ShapeDtypeStruct((points, 2 * basis.shape[1]), F32),
        in_specs=[pl.BlockSpec(memory_space=pltpu.SMEM), pl.BlockSpec(memory_space=pl.ANY), vmem, vmem],
        out_specs=vmem,
        scratch_shapes=[
            pltpu.VMEM(dense.shape, BF16),
            pltpu.VMEM((every, LANES), F32),
            pltpu.VMEM((n * 2 * room, LANES), F32),
            pltpu.VMEM((n, 2 * room, LANES), F32),
            pltpu.VMEM((n, 2 * room, LANES), F32),
            pltpu.VMEM((room * 2 * slots, LANES), F32),
            pltpu.VMEM((chunks, 2, 2, layers, width, columns), F32),
            pltpu.VMEM((chunks, 2, layers, width, columns), F32),
            pltpu.VMEM((chunks, layers, width, columns), F32),
            pltpu.VMEM((layers, chunks, width, columns), F32),
            pltpu.VMEM((chunks, layers, width, columns), F32),
            pltpu.VMEM((2 * waves, columns), F32),
            pltpu.VMEM((FINE, LANES), F32),
            pltpu.VMEM((FINE, LANES), F32),
            dma, dma((n,)), dma((n,)),
            dma((chunks,)), dma((chunks,)),
            dma((chunks, layers)), dma((chunks, layers)),
            dma((layers, chunks)), dma((layers, chunks)), dma((chunks, layers)), dma((layers, chunks)),
        ],
        compiler_params=pltpu.CompilerParams(
            collective_id=0, has_side_effects=True, vmem_limit_bytes=58 * 1024 * 1024
        ),
        name="exchanged_temps",
    )(row_counts, dense, legs, basis)


def plain_temps(spectra, row_counts, basis, points):
    tiles = spectra.shape[0] // (2 * LANES)

    def body(count_ref, spectra_ref, basis_ref, temps_ref, fcos_ref, fsin_ref):
        for tile in range(tiles):
            trig_tile(tile, count_ref[0], spectra_ref, basis_ref, fcos_ref, fsin_ref, temps_ref)

    vmem = pl.BlockSpec(memory_space=pltpu.VMEM)
    return pl.pallas_call(
        body,
        out_shape=jax.ShapeDtypeStruct((points, 2 * basis.shape[1]), F32),
        in_specs=[pl.BlockSpec(memory_space=pltpu.SMEM), vmem, vmem],
        out_specs=vmem,
        scratch_shapes=[pltpu.VMEM((FINE, LANES), F32), pltpu.VMEM((FINE, LANES), F32)],
        name="plain_temps",
    )(row_counts, spectra, basis)


def row_kernel(count_ref, temps_ref, absorb_ref, peak_ref, width_ref, out_ref, rhigh_ref, rlow_ref):
    step = pl.program_id(0)
    levels = absorb_ref.shape[1]
    points = temps_ref.shape[0]

    @pl.when(step == 0)
    def _():
        height = lax.broadcasted_iota(jnp.int32, rlow_ref.shape, 0)
        offsets = (height - peak_ref[...]).astype(F32) / width_ref[...]
        shape = jnp.exp(-offsets * offsets)
        high, low = split(shape / jnp.sum(shape, axis=0, keepdims=True))
        rhigh_ref[pl.ds(0, levels), :] = high
        rhigh_ref[pl.ds(levels, levels), :] = high
        rlow_ref[...] = low

    temps = temps_ref[...]
    temps = jnp.concatenate((temps[:, :levels], temps[:, levels:]), axis=0)

    source = jnp.exp(0.5 * temps)
    layers = absorb_ref[...] * source
    before = lax.broadcasted_iota(jnp.int32, (2 * levels, levels), 0) % levels
    after = lax.broadcasted_iota(jnp.int32, (2 * levels, levels), 1)
    upper = jnp.where(before < after, 1.0, 0.0).astype(BF16)
    layers_high, layers_low = split(layers)
    above = dot(jnp.concatenate((layers_high, layers_low), axis=1), upper)
    emitted = source * jnp.exp(-above) * (1.0 - jnp.exp(-layers))
    place = step * points + lax.broadcasted_iota(jnp.int32, (2 * points, levels), 0) % points
    emitted = jnp.where(place < count_ref[0], emitted, 0.0)
    emitted_high, emitted_low = split(emitted)
    bright = dot(jnp.concatenate((emitted_high, emitted_low), axis=1), rhigh_ref[...])
    bright = bright + dot(emitted_high, rlow_ref[...])
    out_ref[0, 0] = bright[:points]
    out_ref[0, 1] = bright[points:]


def radiate_row(temps, row_counts, absorb, peak_level, width):
    points = temps.shape[0]
    levels, channels = absorb.shape[0], width.shape[0]

    def whole(*shape):
        return pl.BlockSpec(shape, lambda i, *_: (0,) * len(shape))

    return pl.pallas_call(
        row_kernel,
        out_shape=jax.ShapeDtypeStruct((1, 2, points, channels), F32),
        grid_spec=pltpu.PrefetchScalarGridSpec(
            num_scalar_prefetch=1,
            grid=(points // FINE,),
            in_specs=[
                pl.BlockSpec((FINE, 2 * levels), lambda i, *_: (i, 0)),
                whole(1, levels),
                whole(1, channels),
                whole(1, channels),
            ],
            out_specs=pl.BlockSpec((1, 2, FINE, channels), lambda i, *_: (0, 0, i, 0)),
            scratch_shapes=[
                pltpu.VMEM((2 * levels, channels), BF16),
                pltpu.VMEM((levels, channels), BF16),
            ],
        ),
        name="row_radiance",
    )(row_counts, temps, absorb[None, :], peak_level[None, :], width[None, :])


def moved_coefficients(coefficients, legendre):
    waves, _, slots, _ = coefficients.shape
    first = lax.axis_index("spec") * slots
    spread = prior_spread(jnp.arange(waves, dtype=jnp.int32), first + jnp.arange(slots, dtype=jnp.int32), waves)
    scaled = coefficients.astype(F32) * spread[..., None]
    spectral = lax.all_to_all(scaled, "spec", split_axis=0, concat_axis=2, tiled=True)
    sums = jnp.einsum("mpsj,mpsc->mpjc", legendre, spectral, precision=PRECISE)
    sums = lax.all_to_all(sums, "spec", split_axis=2, concat_axis=0, tiled=True)
    return sums.reshape(2 * waves, sums.shape[-1])


def on_device(coefficients, legendre, row_counts, basis, absorb, peak_level, width):
    own, _, every, rows = legendre.shape
    waves, _, slots, columns = coefficients.shape
    n = waves // own
    fits = n == rows and n % 8 == 0 and LANES % n == 0 and every == n * slots and columns == LANES
    fits = fits and (LANES // n) % 8 == 0 and own % (LANES // n) == 0 and slots % 4 == 0 and waves % LANES == 0
    if fits and (slots * LANES // n) % 16 == 0 and 2 * waves >= 2 * slots * n:
        temps = exchanged_temps(coefficients, legendre, row_counts, basis, n, NLON)
    else:
        spectra = moved_coefficients(coefficients, legendre)
        temps = plain_temps(spectra, row_counts, basis, NLON)
    return radiate_row(temps, row_counts, absorb, peak_level, width)


def solution(mesh):
    placed = (
        P("draws", None, "spec", None),
        P("spec", None, None, None),
        P("spec"),
        P(),
        P(),
        P(),
        P(),
    )
    return jax.shard_map(
        on_device,
        mesh=mesh,
        in_specs=placed,
        out_specs=P(("draws", "spec"), None, None, None),
        check_vma=False,
    )
```

```python
import math

import jax
import jax.numpy as jnp
from jax import lax
from jax.experimental import pallas as pl
from jax.experimental.pallas import tpu as pltpu
from jax.sharding import PartitionSpec as P

NLON = 1280
FINE = 256
LANES = 128

PRECISE = lax.Precision.HIGHEST
F32 = jnp.float32
BF16 = jnp.bfloat16


def prior_spread(orders, slots, waves):
    parity = jnp.arange(2, dtype=jnp.int32)[None, :, None]
    degree = orders[:, None, None] + 2 * slots[None, None, :] + parity
    spread = lax.rsqrt((degree + 1).astype(F32) * waves)
    return jnp.where(degree < waves, spread, jnp.zeros_like(spread))


def split(x):
    high = x.astype(BF16)
    return high, (x - high.astype(F32)).astype(BF16)


def dot(a, b):
    return jnp.dot(a, b, preferred_element_type=F32)


def dot3(a, b):
    ah, al = split(a)
    bh, bl = split(b)
    return dot(ah, bh) + dot(al, bh) + dot(ah, bl)


def place_in_ring(n):
    me = lax.axis_index("spec")
    core = me % 2
    side = (me // 2) % 2
    layer = me // 4
    return me, core, side, layer


def fill_lookup(tile, count, fcos_ref, fsin_ref, high_ref, low_ref):
    points, lanes = fcos_ref.shape
    steps = high_ref.shape[0] // points
    tiny = 16
    middle = points // tiny
    coarse = -(-steps // 8) * 8
    whole = count.astype(F32)
    table = (tiny + middle + coarse, lanes)
    index = lax.broadcasted_iota(jnp.int32, table, 0)
    order = lax.broadcasted_iota(jnp.int32, table, 1) + tile * lanes
    places = jnp.where(index < tiny, index, (index - tiny) * tiny)
    places = jnp.where(index < tiny + middle, places, (index - tiny - middle) * points)
    phases = (places * order).astype(F32)
    phases = phases - jnp.floor(phases / whole) * whole
    angles = 2.0 * math.pi * phases / whole
    cosine, sine = jnp.cos(angles), jnp.sin(angles)
    weights = jnp.where(order == 0, 1.0, 2.0) * jnp.where(2 * order < count, 1.0, 0.0)
    first = tiny + middle
    base_c, base_s = (cosine * weights)[first:], (sine * weights)[first:]
    for b in range(middle):
        turn_c, turn_s = cosine[tiny + b:tiny + b + 1], sine[tiny + b:tiny + b + 1]
        fcos_ref[pl.ds(b * tiny, tiny), :] = cosine[:tiny] * turn_c - sine[:tiny] * turn_s
        fsin_ref[pl.ds(b * tiny, tiny), :] = sine[:tiny] * turn_c + cosine[:tiny] * turn_s
    fine_c, fine_s = fcos_ref[...], fsin_ref[...]
    for step in range(steps):
        turn_c, turn_s = base_c[step:step + 1], base_s[step:step + 1]
        lookup_c = turn_c * fine_c - turn_s * fine_s
        lookup_s = -(turn_s * fine_c + turn_c * fine_s)
        high, low = split(jnp.concatenate((lookup_c, lookup_s), axis=1))
        high_ref[pl.ds(step * points, points), :] = high
        low_ref[pl.ds(step * points, points), :] = low


def add_tile(tile, spectra_ref, basis_ref, high_ref, low_ref, temps_ref):
    lanes = LANES
    even = spectra_ref[pl.ds(2 * lanes * tile, lanes, stride=2), :]
    odd = spectra_ref[pl.ds(2 * lanes * tile + 1, lanes, stride=2), :]
    half = even.shape[1] // 2
    real = jnp.concatenate((even[:, :half], odd[:, :half]), axis=1)
    imag = jnp.concatenate((even[:, half:], odd[:, half:]), axis=1)
    basis = basis_ref[...]
    top = jnp.concatenate((basis, basis), axis=1)
    wide = jnp.concatenate((top, jnp.concatenate((basis, -basis), axis=1)), axis=0)
    high, low = split(dot3(jnp.concatenate((real, imag), axis=0), wide))
    for step in range(temps_ref.shape[0] // FINE):
        at = pl.ds(step * FINE, FINE)
        lookup_high = high_ref[at, :]
        temps = dot(lookup_high, high) + (dot(low_ref[at, :], high) + dot(lookup_high, low))
        if tile == 0:
            temps_ref[at, :] = temps
        else:
            temps_ref[at, :] += temps


def exchange_kernel(
    n, waves, cut, count_ref, coef_hbm, leg_hbm, basis_hbm, temps_ref, coef_ref, leg_ref, basis_ref, turn_ref, raw_ref, send_ref, seed_ref,
    wide_ref, sums_ref, near_ref, side_ref, far_ref, up_ref, spectra_ref, fcos_ref, fsin_ref, high_ref, low_ref, coef_sem, leg_sem, basis_sem, seed_send, seed_recv,
    near_send, near_recv, side_send, side_recv, last_send, last_recv, far_send, far_recv, up_recv, lone_send, lone_recv,
):
    me, core, side, layer = place_in_ring(n)
    layers = n // 4
    units = n * cut
    chip = me // 2
    rows = n
    columns = coef_hbm.shape[1]
    every = leg_ref.shape[1]
    slots = every // n
    lanes = LANES
    pairs = lanes // rows
    per = pairs // 2
    own = waves // n
    groups = own // (per * cut)
    depth = per * slots * 2
    part = groups * pairs
    room = seed_ref.shape[1] // (2 * cut)
    block = seed_ref.shape[1]
    partner = me + 1 - 2 * core
    across = me + 2 - 4 * side
    both = cut * (n - 2 * (2 * layer + 1))
    mine = cut * (n - 4 * layer)
    lag = 5

    def spot(z, y, c):
        return (z * 2 + y) * 2 + c

    def remote(src, dst, send_sem, recv_sem, target):
        return pltpu.make_async_remote_copy(
            src_ref=src, dst_ref=dst, send_sem=send_sem, recv_sem=recv_sem,
            device_id={"spec": target}, device_id_type=pl.DeviceIdType.MESH,
        )

    def seed_copy(source, target):
        return remote(send_ref.at[target], seed_ref.at[source], seed_send.at[target], seed_recv.at[source], target)

    def near_copy(q, t):
        ring = near_send.shape[0]
        return remote(sums_ref.at[q, 1 - core], near_ref.at[q], near_send.at[t % ring], near_recv.at[t % ring], partner)

    def side_copy(q, z, t):
        at = t % side_recv.shape[0]
        return remote(sums_ref.at[q, core, 1 - side, z], side_ref.at[q, z], side_send.at[0], side_recv.at[at], across)

    def side_come(q, t):
        return remote(rest_of(side_ref.at[q]), rest_of(side_ref.at[q]), side_send.at[0], side_recv.at[t % side_recv.shape[0]], across)

    def last_copy(q):
        return remote(
            sums_ref.at[q, core, 1 - side, layer], side_ref.at[q, layer], last_send.at[0], last_recv.at[q // cut], across
        )

    def last_come(c):
        both_units = side_ref.at[pl.ds(c * cut, cut), layer]
        return remote(both_units, both_units, last_send.at[0], last_recv.at[c], across)

    def lone(q):
        return q - both

    def lone_copy(q, z):
        return remote(
            sums_ref.at[q, core, 1 - side, z], side_ref.at[q, z], lone_send.at[lone(q)], lone_recv.at[lone(q)], across
        )

    def lone_come(q):
        return remote(rest_of(side_ref.at[q]), rest_of(side_ref.at[q]), lone_send.at[lone(q)], lone_recv.at[lone(q)], across)

    def rest_of(ref):
        return ref.at[pl.ds(0, layers - 1)]

    def far_slot(q, target):
        return far_recv.at[(layer - target + layers) % layers - 1, q // cut]

    def far_copy(q, target):
        return remote(
            sums_ref.at[q, core, side, target], far_ref.at[layer, q],
            far_send.at[0], far_slot(q, target), spot(target, side, core),
        )

    def far_come(c, source, dz):
        both_units = far_ref.at[source, pl.ds(c * cut, cut)]
        return remote(both_units, both_units, far_send.at[0], far_recv.at[dz - 1, c], across)

    def up_copy(q, target):
        return remote(
            sums_ref.at[q, core, side, target], up_ref.at[q, target],
            far_send.at[0], up_recv.at[q], spot((layer + 1) % layers, side, core),
        )

    def up_come(q, lower):
        pieces = up_ref.at[q, pl.ds(lower + 1, layers - 1 - lower)]
        return remote(pieces, pieces, far_send.at[0], up_recv.at[q], across)

    def diag_copy(q, target):
        return remote(
            sums_ref.at[q, core, 1 - side, target], far_ref.at[layer, q],
            lone_send.at[lone(q)], far_slot(q, target), spot(target, 1 - side, core),
        )

    def relay_copy(q, target):
        return remote(
            side_ref.at[q, target], far_ref.at[layer, q],
            lone_send.at[lone(q)], far_slot(q, target), spot(target, side, core),
        )

    def signal(target):
        pl.semaphore_signal(barrier, inc=1, device_id={"spec": target}, device_id_type=pl.DeviceIdType.MESH)

    corners = [(dy, dc) for dy in range(2) for dc in range(2)]

    def corner(z, offset):
        dy, dc = offset
        return spot(z, (side + dy) % 2, (core + dc) % 2)

    pieces = coef_sem.shape[0]
    share = n // pieces

    def coef_copy(q):
        size = share * cut * groups * depth
        at = pl.ds(pl.multiple_of(q * size, size), size)
        return pltpu.make_async_copy(coef_hbm.at[at, :], coef_ref.at[at, :], coef_sem.at[q])

    barrier = pltpu.get_barrier_semaphore()
    for offset in corners[1:]:
        signal(corner(layer, offset))

    @pl.when(layer > 0)
    def _():
        for dz in range(1, layers - 1):
            for offset in corners:
                signal(corner(1 + (layer - 1 + dz) % (layers - 1), offset))

    leg_copy = pltpu.make_async_copy(leg_hbm, leg_ref, leg_sem)
    leg_copy.start()

    for q in range(pieces):
        @pl.when(me + q * share < n)
        def _():
            coef_copy(q).start()

    basis_copy = pltpu.make_async_copy(basis_hbm, basis_ref, basis_sem)
    basis_copy.start()

    row = lax.broadcasted_iota(jnp.int32, (lanes, lanes), 0)
    lane = lax.broadcasted_iota(jnp.int32, (lanes, lanes), 1)
    row_at = row % rows
    ordered = ((row_at % 2) * 2 + (row_at // 2) % 2) * layers + row_at // 4
    moves = jnp.where(ordered * pairs + row // rows == lane, 1.0, 0.0).astype(BF16)

    raw_ref[...] = jnp.zeros(raw_ref.shape, F32)
    leg_copy.wait()
    for g in range(cut * groups):
        at = (g // groups) * 2 * room + g % groups
        turn_ref[...] = jnp.transpose(leg_ref[pl.ds(g * lanes, lanes), :])
        raw_ref[pl.ds(at, n, stride=block), :] = turn_ref[pl.ds(0, n, stride=slots), :]
        raw_ref[pl.ds(at + room, n, stride=block), :] = turn_ref[pl.ds(1, n, stride=slots), :]
    start = jnp.broadcast_to(raw_ref[pl.ds(0, 1), :], (8, lanes))
    cosine = pltpu.roll(start, lanes - rows, 1) / start
    sine = pltpu.roll(start, lanes - 2 * rows, 1) / start
    sine = sine * sine * (2.0 / 3.0)
    square = jnp.where(sine < 0.5, 1.0 - sine, cosine * cosine * (1.0 / 3.0))
    square = jnp.where(lax.broadcasted_iota(jnp.int32, (8, lanes), 1) < rows, square, 0.0)
    shift = rows
    while shift < lanes:
        square = square + pltpu.roll(square, shift, 1)
        shift *= 2
    square = jnp.where(me == 0, square, 0.0)
    raw_ref[pl.ds(groups, n, stride=block), :] = jnp.broadcast_to(square[:1], (n, lanes))
    raw = raw_ref[...]
    high = raw.astype(BF16)
    rest = raw - high.astype(F32)
    middle = rest.astype(BF16)
    low = (rest - middle.astype(F32)).astype(BF16)
    send_ref[...] = (dot(high, moves) + (dot(middle, moves) + dot(low, moves))).reshape(send_ref.shape)
    seed_ref[me] = send_ref[me]

    def give_seeds(z, offset):
        target = corner(z, offset)

        @pl.when(me + target < n)
        def _():
            seed_copy(me, target).start()

    @pl.when(layer == 0)
    def _():
        pl.semaphore_wait(barrier, len(corners) - 1)
        for dz in range(1, layers):
            for offset in corners:
                signal(corner(dz, offset))
        for offset in corners[1:]:
            give_seeds(layer, offset)

    @pl.when(layer > 0)
    def _():
        pl.semaphore_wait(barrier, n - 1)
        for offset in corners:
            signal(corner(0, offset))
        for offset in corners[1:]:
            give_seeds(layer, offset)
        for dz in range(1, layers):
            for offset in corners:
                give_seeds((layer + dz) % layers, offset)

    def meet():
        @pl.when(layer == 0)
        def _():
            pl.semaphore_wait(barrier, n - len(corners))
            for dz in range(1, layers):
                for offset in corners:
                    give_seeds(dz, offset)

    expand_row = lax.broadcasted_iota(jnp.int32, (depth, lanes), 0)
    expand_lane = lax.broadcasted_iota(jnp.int32, (depth, lanes), 1) % pairs
    keep = (expand_row // (2 * slots)) * 2 + expand_row % 2 == expand_lane
    pair_at = lax.broadcasted_iota(jnp.int32, (room, lanes), 1) % pairs
    order_part = lax.broadcasted_iota(jnp.int32, (room, lanes), 0) * per + pair_at // 2

    def recur(u):
        owner = u // cut
        at = pl.multiple_of((u % cut) * (2 * room), 2 * room)
        order = order_part + u * (groups * per)
        first = order + pair_at % 2 + me * (2 * slots)
        m = order.astype(F32)
        square = seed_ref[0, pl.ds(groups, 1), :]

        def coupling(d):
            return ((d - m) * (d + m)) / ((2.0 * d - 1.0) * (2.0 * d + 1.0))

        def place(s, value):
            degree = first + 2 * s
            spread = lax.rsqrt((degree + 1).astype(F32) * float(waves))
            value = value * jnp.where(degree < waves, spread, 0.0)
            wide_ref[pl.ds(2 * s, room, stride=2 * slots), :] = value
            wide_ref[pl.ds(2 * s + 1, room, stride=2 * slots), :] = value

        before = seed_ref[owner, pl.ds(at, room), :]
        now = seed_ref[owner, pl.ds(at + room, room), :]
        place(0, before)
        place(1, now)
        degree = first.astype(F32)
        last = coupling(degree + 2.0)
        weight = jnp.sqrt(coupling(degree + 1.0) * last)
        for s in range(1, slots - 1):
            degree = degree + 2.0
            one, two = coupling(degree + 1.0), coupling(degree + 2.0)
            product = one * two
            inverse = lax.rsqrt(product)
            before, now = now, ((square - (one + last)) * now - weight * before) * inverse
            weight = product * inverse
            last = two
            place(s + 1, now)

    def partial(u):
        owner = u // cut

        @pl.when(me + owner < n)
        def _():
            @pl.when(u % cut == 0)
            def _():
                @pl.when(owner % share == 0)
                def _():
                    coef_copy(owner // share).wait()

                @pl.when(owner != me)
                def _():
                    seed_copy(owner, me).wait_recv()

            recur(u)
            for g in range(groups):
                at = u * groups + g
                values = coef_ref[pl.ds(pl.multiple_of(at * depth, depth), depth), :]
                one = wide_ref[pl.ds(g * 2 * slots, 2 * slots), :]
                tiled = jnp.where(keep, jnp.concatenate([one] * per, axis=0), 0.0)
                both = jnp.concatenate(split(tiled), axis=1)
                sums = lax.dot_general(both, values, (((0,), (0,)), ((), ())), preferred_element_type=F32)
                sums = (sums[:lanes] + sums[lanes:]).reshape(2, 2, layers, pairs, columns)
                sums_ref[u, :, :, :, pl.ds(g * pairs, pairs), :] = sums

        @pl.when(me + owner >= n)
        def _():
            sums_ref[u] = jnp.zeros((2, 2, layers, part, columns), F32)

    def held(q, place):
        return q // cut + 2 * place < n

    def compute(q, t):
        @pl.when(held(q, chip))
        def _():
            partial(q)

            @pl.when(t >= near_send.shape[0])
            def _():
                near_copy(q, t).wait_send()

            near_copy(q, t).start()

    def merge_near(q, t):
        shared = held(q, across // 2)

        @pl.when(held(q, chip))
        def _():
            near_copy(q, t).wait_recv()

            for y in (0, 1):
                @pl.loop(0, layers)
                def _(z):
                    sums_ref[q, core, y, z] += near_ref[q, y, z]

            @pl.when(shared)
            def _():
                for dz in reversed(range(1, layers)):
                    side_copy(q, (layer + dz) % layers, t).start()

            @pl.when(jnp.logical_not(shared))
            def _():
                @pl.when(layer > 0)
                def _():
                    for dz in range(1, layers):
                        lone_copy(q, (layer + dz) % layers).start()

                last_copy(q).start()

    def pass_on(q, t):
        shared = held(q, across // 2)

        @pl.when(held(q, chip))
        def _():
            @pl.when(shared)
            def _():
                side_come(q, t).wait_recv()

            for lower in range(1, layers - 1):
                @pl.when(layer == lower)
                def _():
                    up_come(q, lower).wait_recv()

            for dz in reversed(range(1, layers)):
                z = (layer + dz) % layers
                upward = jnp.logical_and(z > layer + 1, held(q, chip + 2))

                @pl.when(shared)
                def _():
                    sums_ref[q, core, side, z] += side_ref[q, z]

                @pl.when(jnp.logical_and(layer > 0, z > layer))
                def _():
                    sums_ref[q, core, side, z] += up_ref[q, z]

                @pl.when(upward)
                def _():
                    up_copy(q, z).start()

                @pl.when(jnp.logical_not(upward))
                def _():
                    far_copy(q, z).start()

            @pl.when(jnp.logical_and(jnp.logical_not(shared), layer == 0))
            def _():
                for dz in reversed(range(1, layers)):
                    diag_copy(q, dz).start()

        @pl.when(jnp.logical_and(jnp.logical_not(held(q, chip)), jnp.logical_and(shared, layer > 0)))
        def _():
            lone_come(q).wait_recv()
            for dz in range(1, layers):
                relay_copy(q, (layer + dz) % layers).start()

    def unit_at(t):
        turn = n // 2
        block_at, place = t // turn, t % turn
        early = jnp.where(place == turn - 1, both + block_at, block_at * (turn - 1) + place)
        return jnp.where(layer == 0, early, t)

    @pl.loop(0, units + lag)
    def _(t):
        @pl.when(t == lag)
        def _():
            meet()

        @pl.when(t < units)
        def _():
            compute(unit_at(t), t)

        @pl.when(jnp.logical_and(t >= 1, t <= units))
        def _():
            merge_near(unit_at(t - 1), t - 1)

        @pl.when(t == mine)
        def _():
            @pl.loop(0, both)
            def _(q):
                last_copy(q).start()

        @pl.when(t >= lag)
        def _():
            pass_on(unit_at(t - lag), t - lag)

    def finish(c):
        near_part = held(c * cut, chip)

        for dz in range(1, layers):
            source = (layer + dz) % layers
            passed = jnp.logical_and(source + 1 < layer, held(c * cut, 2 * (source + 1) + side))

            @pl.when(jnp.logical_and(held(c * cut, 2 * source), jnp.logical_not(passed)))
            def _():
                far_come(c, source, dz).wait_recv()

        @pl.when(held(c * cut, across // 2))
        def _():
            last_come(c).wait_recv()

        for half in range(cut):
            q = c * cut + half
            at = pl.ds(pl.multiple_of(q * part, part), part)

            @pl.when(near_part)
            def _():
                spectra_ref[at, :] = sums_ref[q, core, side, layer]

            @pl.when(jnp.logical_not(near_part))
            def _():
                spectra_ref[at, :] = jnp.zeros((part, columns), F32)

            for dz in range(1, layers):
                source = (layer + dz) % layers
                passed = jnp.logical_and(source + 1 < layer, held(q, 2 * (source + 1) + side))

                @pl.when(jnp.logical_and(held(q, 2 * source), jnp.logical_not(passed)))
                def _():
                    spectra_ref[at, :] += far_ref[source, q]

            @pl.when(held(q, across // 2))
            def _():
                spectra_ref[at, :] += side_ref[q, layer]

    ring = near_send.shape[0]

    @pl.loop(0, n)
    def _(target):
        @pl.when(jnp.logical_and(target != me, me + target < n))
        def _():
            seed_copy(me, target).wait_send()

    @pl.loop(0, ring)
    def _(k):
        @pl.when(held(unit_at(k), chip))
        def _():
            near_copy(k, k).wait_send()

    tiles = waves // lanes
    done = 0
    basis_copy.wait()
    for tile in range(tiles):
        until = -(-(tile + 1) * lanes // own)
        fill_lookup(tile, count_ref[0], fcos_ref, fsin_ref, high_ref, low_ref)

        @pl.loop(done, until)
        def _(c):
            finish(c)

        done = until
        add_tile(tile, spectra_ref, basis_ref, high_ref, low_ref, temps_ref)

    for place in range(n // 2):
        count = cut * (n - 2 * place)
        pair = cut * (n - 2 * (place // 2 * 2 + 1))

        @pl.when(chip == place)
        def _():
            side = side_ref.at[pl.ds(0, pair), pl.ds(0, layers - 1)]
            remote(side, side, side_send.at[0], side_recv.at[0], across).wait_send()
            last = side_ref.at[pl.ds(0, count), 0]
            remote(last, last, last_send.at[0], last_recv.at[0], across).wait_send()
            far = far_ref.at[pl.ds(0, layers - 1), pl.ds(0, count)]
            remote(far, far, far_send.at[0], far_recv.at[0, 0], across).wait_send()

    sends_lone = jnp.logical_or(side == 0, layer > 0)

    @pl.when(sends_lone)
    def _():
        for k in range(lone_send.shape[0]):
            remote(rest_of(side_ref.at[0]), rest_of(side_ref.at[0]), lone_send.at[k], lone_recv.at[k], across).wait_send()


def exchanged_temps(coefficients, legendre, row_counts, basis, n, points):
    waves, _, slots, columns = coefficients.shape
    own, _, every, rows = legendre.shape
    dense = jnp.transpose(coefficients, (0, 2, 1, 3)).reshape(waves * slots * 2, columns)
    legs = jnp.transpose(legendre, (0, 1, 3, 2)).reshape(own * 2 * rows, every)
    layers = n // 4
    pairs = LANES // rows
    groups = own * 2 // pairs
    cut = 2 if groups % 2 == 0 else 1
    units = n * cut
    width = groups // cut * pairs
    room = -(-(groups // cut + 1) // 8) * 8
    block = cut * 2 * room
    dma = pltpu.SemaphoreType.DMA

    def body(*refs):
        exchange_kernel(n, waves, cut, *refs)

    vmem = pl.BlockSpec(memory_space=pltpu.VMEM)
    return pl.pallas_call(
        body,
        out_shape=jax.ShapeDtypeStruct((points, 2 * basis.shape[1]), F32),
        in_specs=[pl.BlockSpec(memory_space=pltpu.SMEM)] + [pl.BlockSpec(memory_space=pl.ANY)] * 3,
        out_specs=vmem,
        scratch_shapes=[
            pltpu.VMEM(dense.shape, BF16),
            pltpu.VMEM(legs.shape, F32),
            pltpu.VMEM(basis.shape, F32),
            pltpu.VMEM((every, LANES), F32),
            pltpu.VMEM((n * block, LANES), F32),
            pltpu.VMEM((n, block, LANES), F32),
            pltpu.VMEM((n, block, LANES), F32),
            pltpu.VMEM((room * 2 * slots, LANES), F32),
            pltpu.VMEM((units, 2, 2, layers, width, columns), F32),
            pltpu.VMEM((units, 2, layers, width, columns), F32),
            pltpu.VMEM((units, layers, width, columns), F32),
            pltpu.VMEM((layers, units, width, columns), F32),
            pltpu.VMEM((units, layers, width, columns), F32),
            pltpu.VMEM((2 * waves, columns), F32),
            pltpu.VMEM((FINE, LANES), F32),
            pltpu.VMEM((FINE, LANES), F32),
            pltpu.VMEM((points, 2 * LANES), BF16),
            pltpu.VMEM((points, 2 * LANES), BF16),
            dma((n // 2,)), dma, dma, dma((n,)), dma((n,)),
            dma((8,)), dma((8,)),
            dma((1,)), dma((16,)),
            dma((1,)), dma((n,)),
            dma((1,)), dma((layers - 1, n)), dma((units - 4 * cut,)), dma((2 * cut,)), dma((2 * cut,)),
        ],
        compiler_params=pltpu.CompilerParams(
            collective_id=0, has_side_effects=True, vmem_limit_bytes=58 * 1024 * 1024
        ),
        name="exchanged_temps",
    )(row_counts, dense, legs, basis)


def plain_temps(spectra, row_counts, basis, points):
    tiles = spectra.shape[0] // (2 * LANES)

    def body(count_ref, spectra_ref, basis_ref, temps_ref, fcos_ref, fsin_ref, high_ref, low_ref):
        for tile in range(tiles):
            fill_lookup(tile, count_ref[0], fcos_ref, fsin_ref, high_ref, low_ref)
            add_tile(tile, spectra_ref, basis_ref, high_ref, low_ref, temps_ref)

    vmem = pl.BlockSpec(memory_space=pltpu.VMEM)
    return pl.pallas_call(
        body,
        out_shape=jax.ShapeDtypeStruct((points, 2 * basis.shape[1]), F32),
        in_specs=[pl.BlockSpec(memory_space=pltpu.SMEM), vmem, vmem],
        out_specs=vmem,
        scratch_shapes=[pltpu.VMEM((FINE, LANES), F32)] * 2 + [pltpu.VMEM((points, 2 * LANES), BF16)] * 2,
        name="plain_temps",
    )(row_counts, spectra, basis)


def row_kernel(count_ref, temps_ref, absorb_ref, peak_ref, width_ref, out_ref, rhigh_ref, rlow_ref):
    step = pl.program_id(0)
    levels = absorb_ref.shape[1]
    points = temps_ref.shape[0]

    @pl.when(step == 0)
    def _():
        height = lax.broadcasted_iota(jnp.int32, rlow_ref.shape, 0)
        offsets = (height - peak_ref[...]).astype(F32) / width_ref[...]
        shape = jnp.exp(-offsets * offsets)
        high, low = split(shape / jnp.sum(shape, axis=0, keepdims=True))
        rhigh_ref[pl.ds(0, levels), :] = high
        rhigh_ref[pl.ds(levels, levels), :] = high
        rlow_ref[...] = low

    temps = temps_ref[...]
    temps = jnp.concatenate((temps[:, :levels], temps[:, levels:]), axis=0)

    source = jnp.exp(0.5 * temps)
    layers = absorb_ref[...] * source
    before = lax.broadcasted_iota(jnp.int32, (2 * levels, levels), 0) % levels
    after = lax.broadcasted_iota(jnp.int32, (2 * levels, levels), 1)
    upper = jnp.where(before < after, 1.0, 0.0).astype(BF16)
    layers_high, layers_low = split(layers)
    above = dot(jnp.concatenate((layers_high, layers_low), axis=1), upper)
    emitted = source * jnp.exp(-above) * (1.0 - jnp.exp(-layers))
    place = step * points + lax.broadcasted_iota(jnp.int32, (2 * points, levels), 0) % points
    emitted = jnp.where(place < count_ref[0], emitted, 0.0)
    emitted_high, emitted_low = split(emitted)
    bright = dot(jnp.concatenate((emitted_high, emitted_low), axis=1), rhigh_ref[...])
    bright = bright + dot(emitted_high, rlow_ref[...])
    out_ref[0, 0] = bright[:points]
    out_ref[0, 1] = bright[points:]


def radiate_row(temps, row_counts, absorb, peak_level, width):
    points = temps.shape[0]
    levels, channels = absorb.shape[0], width.shape[0]

    def whole(*shape):
        return pl.BlockSpec(shape, lambda i, *_: (0,) * len(shape))

    return pl.pallas_call(
        row_kernel,
        out_shape=jax.ShapeDtypeStruct((1, 2, points, channels), F32),
        grid_spec=pltpu.PrefetchScalarGridSpec(
            num_scalar_prefetch=1,
            grid=(points // FINE,),
            in_specs=[
                pl.BlockSpec((FINE, 2 * levels), lambda i, *_: (i, 0)),
                whole(1, levels),
                whole(1, channels),
                whole(1, channels),
            ],
            out_specs=pl.BlockSpec((1, 2, FINE, channels), lambda i, *_: (0, 0, i, 0)),
            scratch_shapes=[
                pltpu.VMEM((2 * levels, channels), BF16),
                pltpu.VMEM((levels, channels), BF16),
            ],
        ),
        name="row_radiance",
    )(row_counts, temps, absorb[None, :], peak_level[None, :], width[None, :])


def moved_coefficients(coefficients, legendre):
    waves, _, slots, _ = coefficients.shape
    first = lax.axis_index("spec") * slots
    spread = prior_spread(jnp.arange(waves, dtype=jnp.int32), first + jnp.arange(slots, dtype=jnp.int32), waves)
    scaled = coefficients.astype(F32) * spread[..., None]
    spectral = lax.all_to_all(scaled, "spec", split_axis=0, concat_axis=2, tiled=True)
    sums = jnp.einsum("mpsj,mpsc->mpjc", legendre, spectral, precision=PRECISE)
    sums = lax.all_to_all(sums, "spec", split_axis=2, concat_axis=0, tiled=True)
    return sums.reshape(2 * waves, sums.shape[-1])


def on_device(coefficients, legendre, row_counts, basis, absorb, peak_level, width):
    own, _, every, rows = legendre.shape
    waves, _, slots, columns = coefficients.shape
    n = waves // own
    fits = n == rows and n % 8 == 0 and LANES % n == 0 and every == n * slots and columns == LANES
    fits = fits and (LANES // n) % 8 == 0 and own % (LANES // n) == 0 and slots % 4 == 0 and waves % LANES == 0
    if fits and (slots * LANES // n) % 16 == 0 and 2 * waves >= 2 * slots * n:
        temps = exchanged_temps(coefficients, legendre, row_counts, basis, n, NLON)
    else:
        spectra = moved_coefficients(coefficients, legendre)
        temps = plain_temps(spectra, row_counts, basis, NLON)
    return radiate_row(temps, row_counts, absorb, peak_level, width)


def solution(mesh):
    placed = (
        P("draws", None, "spec", None),
        P("spec", None, None, None),
        P("spec"),
        P(),
        P(),
        P(),
        P(),
    )
    return jax.shard_map(
        on_device,
        mesh=mesh,
        in_specs=placed,
        out_specs=P(("draws", "spec"), None, None, None),
        check_vma=False,
    )
```

```python
import math

import jax
import jax.numpy as jnp
from jax import lax
from jax.experimental import pallas as pl
from jax.experimental.pallas import tpu as pltpu
from jax.sharding import PartitionSpec as P

NLON = 1280
FINE = 256
SPAN = 640
LANES = 128

PRECISE = lax.Precision.HIGHEST
F32 = jnp.float32
BF16 = jnp.bfloat16


def prior_spread(orders, slots, waves):
    parity = jnp.arange(2, dtype=jnp.int32)[None, :, None]
    degree = orders[:, None, None] + 2 * slots[None, None, :] + parity
    spread = lax.rsqrt((degree + 1).astype(F32) * waves)
    return jnp.where(degree < waves, spread, jnp.zeros_like(spread))


def split(x):
    high = x.astype(BF16)
    return high, (x - high.astype(F32)).astype(BF16)


def dot(a, b):
    return jnp.dot(a, b, preferred_element_type=F32)


def dot3(a, b):
    ah, al = split(a)
    bh, bl = split(b)
    return dot(ah, bh) + dot(al, bh) + dot(ah, bl)


def place_in_ring(n):
    me = lax.axis_index("spec")
    core = me % 2
    side = (me // 2) % 2
    layer = me // 4
    return me, core, side, layer


def fill_lookup(tile, count, fcos_ref, fsin_ref, high_ref, low_ref):
    points, lanes = fcos_ref.shape
    steps = high_ref.shape[1] // points
    tiny = 16
    middle = points // tiny
    coarse = -(-steps // 8) * 8
    whole = count.astype(F32)
    table = (tiny + middle + coarse, lanes)
    index = lax.broadcasted_iota(jnp.int32, table, 0)
    order = lax.broadcasted_iota(jnp.int32, table, 1) + tile * lanes
    places = jnp.where(index < tiny, index, (index - tiny) * tiny)
    places = jnp.where(index < tiny + middle, places, (index - tiny - middle) * points)
    phases = (places * order).astype(F32)
    phases = phases - jnp.floor(phases / whole) * whole
    angles = 2.0 * math.pi * phases / whole
    cosine, sine = jnp.cos(angles), jnp.sin(angles)
    weights = jnp.where(order == 0, 1.0, 2.0) * jnp.where(2 * order < count, 1.0, 0.0)
    first = tiny + middle
    base_c, base_s = (cosine * weights)[first:], (sine * weights)[first:]
    for b in range(middle):
        turn_c, turn_s = cosine[tiny + b:tiny + b + 1], sine[tiny + b:tiny + b + 1]
        fcos_ref[pl.ds(b * tiny, tiny), :] = cosine[:tiny] * turn_c - sine[:tiny] * turn_s
        fsin_ref[pl.ds(b * tiny, tiny), :] = sine[:tiny] * turn_c + cosine[:tiny] * turn_s
    fine_c, fine_s = fcos_ref[...], fsin_ref[...]
    for step in range(steps):
        turn_c, turn_s = base_c[step:step + 1], base_s[step:step + 1]
        lookup_c = turn_c * fine_c - turn_s * fine_s
        lookup_s = -(turn_s * fine_c + turn_c * fine_s)
        high, low = split(jnp.concatenate((lookup_c, lookup_s), axis=1))
        high_ref[tile, pl.ds(step * points, points), :] = high
        low_ref[tile, pl.ds(step * points, points), :] = low


def add_tile(tile, spectra_ref, basis_ref, high_ref, low_ref, temps_ref, after=None):
    lanes = LANES
    first = 2 * lanes * tile
    even = spectra_ref[pl.ds(first, lanes, stride=2), :]
    odd = spectra_ref[pl.ds(first + 1, lanes, stride=2), :]
    half = even.shape[1] // 2
    real = jnp.concatenate((even[:, :half], odd[:, :half]), axis=1)
    imag = jnp.concatenate((even[:, half:], odd[:, half:]), axis=1)
    basis = basis_ref[...]
    top = jnp.concatenate((basis, basis), axis=1)
    wide = jnp.concatenate((top, jnp.concatenate((basis, -basis), axis=1)), axis=0)
    high, low = split(dot3(jnp.concatenate((real, imag), axis=0), wide))
    for step in range(temps_ref.shape[0] // FINE):
        at = pl.ds(step * FINE, FINE)
        lookup_high = high_ref[tile, at, :]
        temps_ref[at, :] += dot(lookup_high, high) + (dot(low_ref[tile, at, :], high) + dot(lookup_high, low))
        if after is not None:
            after(step)


def exchange_kernel(
    n, waves, cut, count_ref, coef_hbm, leg_hbm, basis_hbm, out_hbm, temps_ref, coef_ref, leg_ref, basis_ref, turn_ref, raw_ref, send_ref, seed_ref,
    wide_ref, sums_ref, near_ref, side_ref, far_ref, up_ref, spectra_ref, fcos_ref, fsin_ref, high_ref, low_ref, coef_sem, leg_sem, basis_sem, out_sem, seed_send, seed_recv,
    near_send, near_recv, side_send, side_recv, last_send, last_recv, far_send, far_recv, up_recv, lone_send, lone_recv,
):
    me, core, side, layer = place_in_ring(n)
    layers = n // 4
    units = n * cut
    chip = me // 2
    rows = n
    columns = coef_hbm.shape[1]
    every = leg_ref.shape[1]
    slots = every // n
    lanes = LANES
    pairs = lanes // rows
    per = pairs // 2
    own = waves // n
    groups = own // (per * cut)
    depth = per * slots * 2
    part = groups * pairs
    room = seed_ref.shape[1] // (2 * cut)
    block = seed_ref.shape[1]
    partner = me + 1 - 2 * core
    across = me + 2 - 4 * side
    both = cut * (n - 2 * (2 * layer + 1))
    mine = cut * (n - 4 * layer)
    lag = 5

    def spot(z, y, c):
        return (z * 2 + y) * 2 + c

    def remote(src, dst, send_sem, recv_sem, target):
        return pltpu.make_async_remote_copy(
            src_ref=src, dst_ref=dst, send_sem=send_sem, recv_sem=recv_sem,
            device_id={"spec": target}, device_id_type=pl.DeviceIdType.MESH,
        )

    def seed_copy(source, target):
        return remote(send_ref.at[target], seed_ref.at[source], seed_send.at[target], seed_recv.at[source], target)

    def near_copy(q, t):
        ring = near_send.shape[0]
        return remote(sums_ref.at[q, 1 - core], near_ref.at[q], near_send.at[t % ring], near_recv.at[t % ring], partner)

    def side_copy(q, z, t):
        at = t % side_recv.shape[0]
        return remote(sums_ref.at[q, core, 1 - side, z], side_ref.at[q, z], side_send.at[0], side_recv.at[at], across)

    def side_come(q, t):
        return remote(rest_of(side_ref.at[q]), rest_of(side_ref.at[q]), side_send.at[0], side_recv.at[t % side_recv.shape[0]], across)

    def last_copy(q):
        return remote(
            sums_ref.at[q, core, 1 - side, layer], side_ref.at[q, layer], last_send.at[0], last_recv.at[q // cut], across
        )

    def last_come(c):
        both_units = side_ref.at[pl.ds(c * cut, cut), layer]
        return remote(both_units, both_units, last_send.at[0], last_recv.at[c], across)

    def lone(q):
        return q - both

    def lone_copy(q, z):
        return remote(
            sums_ref.at[q, core, 1 - side, z], side_ref.at[q, z], lone_send.at[lone(q)], lone_recv.at[lone(q)], across
        )

    def lone_come(q):
        return remote(rest_of(side_ref.at[q]), rest_of(side_ref.at[q]), lone_send.at[lone(q)], lone_recv.at[lone(q)], across)

    def rest_of(ref):
        return ref.at[pl.ds(0, layers - 1)]

    def far_slot(q, target):
        return far_recv.at[(layer - target + layers) % layers - 1, q // cut]

    def far_copy(q, target):
        return remote(
            sums_ref.at[q, core, side, target], far_ref.at[layer, q],
            far_send.at[0], far_slot(q, target), spot(target, side, core),
        )

    def far_come(c, source, dz):
        both_units = far_ref.at[source, pl.ds(c * cut, cut)]
        return remote(both_units, both_units, far_send.at[0], far_recv.at[dz - 1, c], across)

    def up_copy(q, target):
        return remote(
            sums_ref.at[q, core, side, target], up_ref.at[q, target],
            far_send.at[0], up_recv.at[q], spot((layer + 1) % layers, side, core),
        )

    def up_come(q, lower):
        pieces = up_ref.at[q, pl.ds(lower + 1, layers - 1 - lower)]
        return remote(pieces, pieces, far_send.at[0], up_recv.at[q], across)

    def diag_copy(q, target):
        return remote(
            sums_ref.at[q, core, 1 - side, target], far_ref.at[layer, q],
            lone_send.at[lone(q)], far_slot(q, target), spot(target, 1 - side, core),
        )

    def relay_copy(q, target):
        return remote(
            side_ref.at[q, target], far_ref.at[layer, q],
            lone_send.at[lone(q)], far_slot(q, target), spot(target, side, core),
        )

    def signal(target):
        pl.semaphore_signal(barrier, inc=1, device_id={"spec": target}, device_id_type=pl.DeviceIdType.MESH)

    corners = [(dy, dc) for dy in range(2) for dc in range(2)]

    def corner(z, offset):
        dy, dc = offset
        return spot(z, (side + dy) % 2, (core + dc) % 2)

    pieces = coef_sem.shape[0]
    share = n // pieces

    def coef_copy(q):
        size = share * cut * groups * depth
        at = pl.ds(pl.multiple_of(q * size, size), size)
        return pltpu.make_async_copy(coef_hbm.at[at, :], coef_ref.at[at, :], coef_sem.at[q])

    barrier = pltpu.get_barrier_semaphore()
    for offset in corners[1:]:
        signal(corner(layer, offset))

    @pl.when(layer > 0)
    def _():
        for dz in range(1, layers - 1):
            for offset in corners:
                signal(corner(1 + (layer - 1 + dz) % (layers - 1), offset))

    leg_copy = pltpu.make_async_copy(leg_hbm, leg_ref, leg_sem)
    leg_copy.start()

    basis_copy = pltpu.make_async_copy(basis_hbm, basis_ref, basis_sem)
    basis_copy.start()

    row = lax.broadcasted_iota(jnp.int32, (lanes, lanes), 0)
    lane = lax.broadcasted_iota(jnp.int32, (lanes, lanes), 1)
    row_at = row % rows
    ordered = ((row_at % 2) * 2 + (row_at // 2) % 2) * layers + row_at // 4
    moves = jnp.where(ordered * pairs + row // rows == lane, 1.0, 0.0).astype(BF16)

    raw_ref[...] = jnp.zeros(raw_ref.shape, F32)
    leg_copy.wait()
    for q in range(pieces):
        @pl.when(me + q * share < n)
        def _():
            coef_copy(q).start()

    for g in range(cut * groups):
        at = (g // groups) * 2 * room + g % groups
        turn_ref[...] = jnp.transpose(leg_ref[pl.ds(g * lanes, lanes), :])
        raw_ref[pl.ds(at, n, stride=block), :] = turn_ref[pl.ds(0, n, stride=slots), :]
        raw_ref[pl.ds(at + room, n, stride=block), :] = turn_ref[pl.ds(1, n, stride=slots), :]
    start = jnp.broadcast_to(raw_ref[pl.ds(0, 1), :], (8, lanes))
    cosine = pltpu.roll(start, lanes - rows, 1) / start
    sine = pltpu.roll(start, lanes - 2 * rows, 1) / start
    sine = sine * sine * (2.0 / 3.0)
    square = jnp.where(sine < 0.5, 1.0 - sine, cosine * cosine * (1.0 / 3.0))
    square = jnp.where(lax.broadcasted_iota(jnp.int32, (8, lanes), 1) < rows, square, 0.0)
    shift = rows
    while shift < lanes:
        square = square + pltpu.roll(square, shift, 1)
        shift *= 2
    square = jnp.where(me == 0, square, 0.0)
    raw_ref[pl.ds(groups, n, stride=block), :] = jnp.broadcast_to(square[:1], (n, lanes))
    raw = raw_ref[...]
    high = raw.astype(BF16)
    rest = raw - high.astype(F32)
    middle = rest.astype(BF16)
    low = (rest - middle.astype(F32)).astype(BF16)
    send_ref[...] = (dot(high, moves) + (dot(middle, moves) + dot(low, moves))).reshape(send_ref.shape)
    seed_ref[me] = send_ref[me]

    def give_seeds(z, offset):
        target = corner(z, offset)

        @pl.when(me + target < n)
        def _():
            seed_copy(me, target).start()

    @pl.when(layer == 0)
    def _():
        pl.semaphore_wait(barrier, len(corners) - 1)
        for dz in range(1, layers):
            for offset in corners:
                signal(corner(dz, offset))
        for offset in corners[1:]:
            give_seeds(layer, offset)

    @pl.when(layer > 0)
    def _():
        pl.semaphore_wait(barrier, n - 1)
        for offset in corners:
            signal(corner(0, offset))
        for offset in corners[1:]:
            give_seeds(layer, offset)
        for dz in range(1, layers):
            for offset in corners:
                give_seeds((layer + dz) % layers, offset)

    tiles = waves // lanes

    def fill(tile):
        fill_lookup(tile, count_ref[0], fcos_ref, fsin_ref, high_ref, low_ref)

    @pl.when(layer > 0)
    def _():
        @pl.loop(0, tiles)
        def _(tile):
            fill(tile)

    def meet():
        @pl.when(layer == 0)
        def _():
            pl.semaphore_wait(barrier, n - len(corners))
            for dz in range(1, layers):
                for offset in corners:
                    give_seeds(dz, offset)

    expand_row = lax.broadcasted_iota(jnp.int32, (depth, lanes), 0)
    expand_lane = lax.broadcasted_iota(jnp.int32, (depth, lanes), 1) % pairs
    keep = (expand_row // (2 * slots)) * 2 + expand_row % 2 == expand_lane
    pair_at = lax.broadcasted_iota(jnp.int32, (room, lanes), 1) % pairs
    order_part = lax.broadcasted_iota(jnp.int32, (room, lanes), 0) * per + pair_at // 2

    def recur(u):
        owner = u // cut
        at = pl.multiple_of((u % cut) * (2 * room), 2 * room)
        order = order_part + u * (groups * per)
        first = order + pair_at % 2 + me * (2 * slots)
        m = order.astype(F32)
        square = seed_ref[0, pl.ds(groups, 1), :]

        def coupling(d):
            return ((d - m) * (d + m)) / ((2.0 * d - 1.0) * (2.0 * d + 1.0))

        def place(s, value):
            degree = first + 2 * s
            spread = lax.rsqrt((degree + 1).astype(F32) * float(waves))
            value = value * jnp.where(degree < waves, spread, 0.0)
            wide_ref[pl.ds(2 * s, room, stride=2 * slots), :] = value
            wide_ref[pl.ds(2 * s + 1, room, stride=2 * slots), :] = value

        before = seed_ref[owner, pl.ds(at, room), :]
        now = seed_ref[owner, pl.ds(at + room, room), :]
        place(0, before)
        place(1, now)
        degree = first.astype(F32)
        last = coupling(degree + 2.0)
        weight = jnp.sqrt(coupling(degree + 1.0) * last)
        for s in range(1, slots - 1):
            degree = degree + 2.0
            one, two = coupling(degree + 1.0), coupling(degree + 2.0)
            product = one * two
            inverse = lax.rsqrt(product)
            before, now = now, ((square - (one + last)) * now - weight * before) * inverse
            weight = product * inverse
            last = two
            place(s + 1, now)

    def partial(u):
        owner = u // cut

        @pl.when(me + owner < n)
        def _():
            @pl.when(u % cut == 0)
            def _():
                @pl.when(owner % share == 0)
                def _():
                    coef_copy(owner // share).wait()

                @pl.when(owner != me)
                def _():
                    seed_copy(owner, me).wait_recv()

            recur(u)
            for g in range(groups):
                at = u * groups + g
                values = coef_ref[pl.ds(pl.multiple_of(at * depth, depth), depth), :]
                one = wide_ref[pl.ds(g * 2 * slots, 2 * slots), :]
                tiled = jnp.where(keep, jnp.concatenate([one] * per, axis=0), 0.0)
                both = jnp.concatenate(split(tiled), axis=1)
                sums = lax.dot_general(both, values, (((0,), (0,)), ((), ())), preferred_element_type=F32)
                sums = (sums[:lanes] + sums[lanes:]).reshape(2, 2, layers, pairs, columns)
                sums_ref[u, :, :, :, pl.ds(g * pairs, pairs), :] = sums

        @pl.when(me + owner >= n)
        def _():
            sums_ref[u] = jnp.zeros((2, 2, layers, part, columns), F32)

    def held(q, place):
        return q // cut + 2 * place < n

    def compute(q, t):
        @pl.when(held(q, chip))
        def _():
            partial(q)

            @pl.when(t >= near_send.shape[0])
            def _():
                near_copy(q, t).wait_send()

            near_copy(q, t).start()

    def merge_near(q, t):
        shared = held(q, across // 2)

        @pl.when(held(q, chip))
        def _():
            near_copy(q, t).wait_recv()

            for y in (0, 1):
                @pl.loop(0, layers)
                def _(z):
                    sums_ref[q, core, y, z] += near_ref[q, y, z]

            @pl.when(shared)
            def _():
                for dz in reversed(range(1, layers)):
                    side_copy(q, (layer + dz) % layers, t).start()

            @pl.when(jnp.logical_not(shared))
            def _():
                @pl.when(layer > 0)
                def _():
                    for dz in range(1, layers):
                        lone_copy(q, (layer + dz) % layers).start()

                last_copy(q).start()

    def pass_on(q, t):
        shared = held(q, across // 2)

        @pl.when(held(q, chip))
        def _():
            @pl.when(shared)
            def _():
                side_come(q, t).wait_recv()

            for lower in range(1, layers - 1):
                @pl.when(layer == lower)
                def _():
                    up_come(q, lower).wait_recv()

            for dz in reversed(range(1, layers)):
                z = (layer + dz) % layers
                upward = jnp.logical_and(z > layer + 1, held(q, chip + 2))

                @pl.when(shared)
                def _():
                    sums_ref[q, core, side, z] += side_ref[q, z]

                @pl.when(jnp.logical_and(layer > 0, z > layer))
                def _():
                    sums_ref[q, core, side, z] += up_ref[q, z]

                @pl.when(upward)
                def _():
                    up_copy(q, z).start()

                @pl.when(jnp.logical_not(upward))
                def _():
                    far_copy(q, z).start()

            @pl.when(jnp.logical_and(jnp.logical_not(shared), layer == 0))
            def _():
                for dz in reversed(range(1, layers)):
                    diag_copy(q, dz).start()

        @pl.when(jnp.logical_and(jnp.logical_not(held(q, chip)), jnp.logical_and(shared, layer > 0)))
        def _():
            lone_come(q).wait_recv()
            for dz in range(1, layers):
                relay_copy(q, (layer + dz) % layers).start()

    def unit_at(t):
        turn = n // 2
        block_at, place = t // turn, t % turn
        early = jnp.where(place == turn - 1, both + block_at, block_at * (turn - 1) + place)
        return jnp.where(layer == 0, early, t)

    def finish(c):
        near_part = held(c * cut, chip)

        for dz in range(1, layers):
            source = (layer + dz) % layers
            passed = jnp.logical_and(source + 1 < layer, held(c * cut, 2 * (source + 1) + side))

            @pl.when(jnp.logical_and(held(c * cut, 2 * source), jnp.logical_not(passed)))
            def _():
                far_come(c, source, dz).wait_recv()

        @pl.when(held(c * cut, across // 2))
        def _():
            last_come(c).wait_recv()

        for half in range(cut):
            q = c * cut + half
            at = pl.ds(pl.multiple_of(q * part, part), part)

            @pl.when(near_part)
            def _():
                spectra_ref[at, :] = sums_ref[q, core, side, layer]

            @pl.when(jnp.logical_not(near_part))
            def _():
                spectra_ref[at, :] = jnp.zeros((part, columns), F32)

            for dz in range(1, layers):
                source = (layer + dz) % layers
                passed = jnp.logical_and(source + 1 < layer, held(q, 2 * (source + 1) + side))

                @pl.when(jnp.logical_and(held(q, 2 * source), jnp.logical_not(passed)))
                def _():
                    spectra_ref[at, :] += far_ref[source, q]

            @pl.when(held(q, across // 2))
            def _():
                spectra_ref[at, :] += side_ref[q, layer]

    temps_ref[...] = jnp.zeros(temps_ref.shape, F32)
    basis_copy.wait()

    def out_copy(step):
        at = pl.ds(step * FINE, FINE)
        return pltpu.make_async_copy(temps_ref.at[at, :], out_hbm.at[at, :], out_sem.at[step])

    def stage(tile, after=None):
        @pl.loop((tile * lanes + own - 1) // own, ((tile + 1) * lanes + own - 1) // own)
        def _(c):
            finish(c)

        add_tile(tile, spectra_ref, basis_ref, high_ref, low_ref, temps_ref, after)

    @pl.loop(0, units + lag)
    def _(t):
        @pl.when(t == lag)
        def _():
            meet()

        @pl.when(jnp.logical_and(layer == 0, jnp.logical_and(t >= 2 * lag, t < 2 * (lag + tiles))))
        def _():
            @pl.when(t % 2 == 0)
            def _():
                fill(t // 2 - lag)

        @pl.when(t < units)
        def _():
            compute(unit_at(t), t)

        @pl.when(jnp.logical_and(t >= 1, t <= units))
        def _():
            merge_near(unit_at(t - 1), t - 1)

        @pl.when(t == mine)
        def _():
            @pl.loop(0, both)
            def _(q):
                last_copy(q).start()

        @pl.when(t >= lag)
        def _():
            pass_on(unit_at(t - lag), t - lag)

    ring = near_send.shape[0]

    @pl.loop(0, n)
    def _(target):
        @pl.when(jnp.logical_and(target != me, me + target < n))
        def _():
            seed_copy(me, target).wait_send()

    @pl.loop(0, ring)
    def _(k):
        @pl.when(held(unit_at(k), chip))
        def _():
            near_copy(k, k).wait_send()

    @pl.loop(0, tiles - 1)
    def _(tile):
        stage(tile)

    stage(tiles - 1, lambda step: out_copy(step).start())

    for place in range(n // 2):
        count = cut * (n - 2 * place)
        pair = cut * (n - 2 * (place // 2 * 2 + 1))

        @pl.when(chip == place)
        def _():
            side = side_ref.at[pl.ds(0, pair), pl.ds(0, layers - 1)]
            remote(side, side, side_send.at[0], side_recv.at[0], across).wait_send()
            last = side_ref.at[pl.ds(0, count), 0]
            remote(last, last, last_send.at[0], last_recv.at[0], across).wait_send()
            far = far_ref.at[pl.ds(0, layers - 1), pl.ds(0, count)]
            remote(far, far, far_send.at[0], far_recv.at[0, 0], across).wait_send()

    sends_lone = jnp.logical_or(side == 0, layer > 0)

    @pl.when(sends_lone)
    def _():
        for k in range(lone_send.shape[0]):
            remote(rest_of(side_ref.at[0]), rest_of(side_ref.at[0]), lone_send.at[k], lone_recv.at[k], across).wait_send()

    for step in range(out_sem.shape[0]):
        out_copy(step).wait()


def exchanged_temps(coefficients, legendre, row_counts, basis, n, points):
    waves, _, slots, columns = coefficients.shape
    own, _, every, rows = legendre.shape
    dense = jnp.transpose(coefficients, (0, 2, 1, 3)).reshape(waves * slots * 2, columns)
    legs = jnp.transpose(legendre, (0, 1, 3, 2)).reshape(own * 2 * rows, every)
    layers = n // 4
    pairs = LANES // rows
    groups = own * 2 // pairs
    cut = 2 if groups % 2 == 0 else 1
    units = n * cut
    width = groups // cut * pairs
    room = -(-(groups // cut + 1) // 8) * 8
    block = cut * 2 * room
    dma = pltpu.SemaphoreType.DMA

    def body(*refs):
        exchange_kernel(n, waves, cut, *refs)

    return pl.pallas_call(
        body,
        out_shape=jax.ShapeDtypeStruct((points, 2 * basis.shape[1]), F32),
        in_specs=[pl.BlockSpec(memory_space=pltpu.SMEM)] + [pl.BlockSpec(memory_space=pl.ANY)] * 3,
        out_specs=pl.BlockSpec(memory_space=pl.ANY),
        scratch_shapes=[
            pltpu.VMEM((points, 2 * basis.shape[1]), F32),
            pltpu.VMEM(dense.shape, BF16),
            pltpu.VMEM(legs.shape, F32),
            pltpu.VMEM(basis.shape, F32),
            pltpu.VMEM((every, LANES), F32),
            pltpu.VMEM((n * block, LANES), F32),
            pltpu.VMEM((n, block, LANES), F32),
            pltpu.VMEM((n, block, LANES), F32),
            pltpu.VMEM((room * 2 * slots, LANES), F32),
            pltpu.VMEM((units, 2, 2, layers, width, columns), F32),
            pltpu.VMEM((units, 2, layers, width, columns), F32),
            pltpu.VMEM((units, layers, width, columns), F32),
            pltpu.VMEM((layers, units, width, columns), F32),
            pltpu.VMEM((units, layers, width, columns), F32),
            pltpu.VMEM((2 * waves, columns), F32),
            pltpu.VMEM((FINE, LANES), F32),
            pltpu.VMEM((FINE, LANES), F32),
            pltpu.VMEM((waves // LANES, points, 2 * LANES), BF16),
            pltpu.VMEM((waves // LANES, points, 2 * LANES), BF16),
            dma((n // 2,)), dma, dma, dma((points // FINE,)), dma((n,)), dma((n,)),
            dma((8,)), dma((8,)),
            dma((1,)), dma((16,)),
            dma((1,)), dma((n,)),
            dma((1,)), dma((layers - 1, n)), dma((units - 4 * cut,)), dma((2 * cut,)), dma((2 * cut,)),
        ],
        compiler_params=pltpu.CompilerParams(
            collective_id=0, has_side_effects=True, vmem_limit_bytes=58 * 1024 * 1024
        ),
        name="exchanged_temps",
    )(row_counts, dense, legs, basis)


def plain_temps(spectra, row_counts, basis, points):
    tiles = spectra.shape[0] // (2 * LANES)

    def body(count_ref, spectra_ref, basis_ref, temps_ref, fcos_ref, fsin_ref, high_ref, low_ref):
        temps_ref[...] = jnp.zeros(temps_ref.shape, F32)
        for tile in range(tiles):
            fill_lookup(tile, count_ref[0], fcos_ref, fsin_ref, high_ref, low_ref)
            add_tile(tile, spectra_ref, basis_ref, high_ref, low_ref, temps_ref)

    vmem = pl.BlockSpec(memory_space=pltpu.VMEM)
    return pl.pallas_call(
        body,
        out_shape=jax.ShapeDtypeStruct((points, 2 * basis.shape[1]), F32),
        in_specs=[pl.BlockSpec(memory_space=pltpu.SMEM), vmem, vmem],
        out_specs=vmem,
        scratch_shapes=[pltpu.VMEM((FINE, LANES), F32)] * 2 + [pltpu.VMEM((tiles, points, 2 * LANES), BF16)] * 2,
        name="plain_temps",
    )(row_counts, spectra, basis)


def row_kernel(count_ref, temps_ref, absorb_ref, peak_ref, width_ref, out_ref, rhigh_ref, rlow_ref):
    step = pl.program_id(0)
    levels = absorb_ref.shape[1]
    points = temps_ref.shape[0]

    @pl.when(step == 0)
    def _():
        height = lax.broadcasted_iota(jnp.int32, rlow_ref.shape, 0)
        offsets = (height - peak_ref[...]).astype(F32) / width_ref[...]
        shape = jnp.exp(-offsets * offsets)
        high, low = split(shape / jnp.sum(shape, axis=0, keepdims=True))
        rhigh_ref[pl.ds(0, levels), :] = high
        rhigh_ref[pl.ds(levels, levels), :] = high
        rlow_ref[...] = low

    temps = temps_ref[...]
    temps = jnp.concatenate((temps[:, :levels], temps[:, levels:]), axis=0)

    source = jnp.exp(0.5 * temps)
    layers = absorb_ref[...] * source
    before = lax.broadcasted_iota(jnp.int32, (2 * levels, levels), 0) % levels
    after = lax.broadcasted_iota(jnp.int32, (2 * levels, levels), 1)
    upper = jnp.where(before < after, 1.0, 0.0).astype(BF16)
    layers_high, layers_low = split(layers)
    above = dot(jnp.concatenate((layers_high, layers_low), axis=1), upper)
    emitted = source * jnp.exp(-above) * (1.0 - jnp.exp(-layers))
    place = step * points + lax.broadcasted_iota(jnp.int32, (2 * points, levels), 0) % points
    emitted = jnp.where(place < count_ref[0], emitted, 0.0)
    emitted_high, emitted_low = split(emitted)
    bright = dot(jnp.concatenate((emitted_high, emitted_low), axis=1), rhigh_ref[...])
    bright = bright + dot(emitted_high, rlow_ref[...])
    out_ref[0, 0] = bright[:points]
    out_ref[0, 1] = bright[points:]


def radiate_row(temps, row_counts, absorb, peak_level, width):
    points = temps.shape[0]
    span = SPAN if points % SPAN == 0 else FINE
    levels, channels = absorb.shape[0], width.shape[0]

    def whole(*shape):
        return pl.BlockSpec(shape, lambda i, *_: (0,) * len(shape))

    return pl.pallas_call(
        row_kernel,
        out_shape=jax.ShapeDtypeStruct((1, 2, points, channels), F32),
        grid_spec=pltpu.PrefetchScalarGridSpec(
            num_scalar_prefetch=1,
            grid=(points // span,),
            in_specs=[
                pl.BlockSpec((span, 2 * levels), lambda i, *_: (i, 0)),
                whole(1, levels),
                whole(1, channels),
                whole(1, channels),
            ],
            out_specs=pl.BlockSpec((1, 2, span, channels), lambda i, *_: (0, 0, i, 0)),
            scratch_shapes=[
                pltpu.VMEM((2 * levels, channels), BF16),
                pltpu.VMEM((levels, channels), BF16),
            ],
        ),
        name="row_radiance",
    )(row_counts, temps, absorb[None, :], peak_level[None, :], width[None, :])


def moved_coefficients(coefficients, legendre):
    waves, _, slots, _ = coefficients.shape
    first = lax.axis_index("spec") * slots
    spread = prior_spread(jnp.arange(waves, dtype=jnp.int32), first + jnp.arange(slots, dtype=jnp.int32), waves)
    scaled = coefficients.astype(F32) * spread[..., None]
    spectral = lax.all_to_all(scaled, "spec", split_axis=0, concat_axis=2, tiled=True)
    sums = jnp.einsum("mpsj,mpsc->mpjc", legendre, spectral, precision=PRECISE)
    sums = lax.all_to_all(sums, "spec", split_axis=2, concat_axis=0, tiled=True)
    return sums.reshape(2 * waves, sums.shape[-1])


def on_device(coefficients, legendre, row_counts, basis, absorb, peak_level, width):
    own, _, every, rows = legendre.shape
    waves, _, slots, columns = coefficients.shape
    n = waves // own
    fits = n == rows and n % 8 == 0 and LANES % n == 0 and every == n * slots and columns == LANES
    fits = fits and (LANES // n) % 8 == 0 and own % (LANES // n) == 0 and slots % 4 == 0 and waves % LANES == 0
    if fits and (slots * LANES // n) % 16 == 0 and 2 * waves >= 2 * slots * n:
        temps = exchanged_temps(coefficients, legendre, row_counts, basis, n, NLON)
    else:
        spectra = moved_coefficients(coefficients, legendre)
        temps = plain_temps(spectra, row_counts, basis, NLON)
    return radiate_row(temps, row_counts, absorb, peak_level, width)


def solution(mesh):
    placed = (
        P("draws", None, "spec", None),
        P("spec", None, None, None),
        P("spec"),
        P(),
        P(),
        P(),
        P(),
    )
    return jax.shard_map(
        on_device,
        mesh=mesh,
        in_specs=placed,
        out_specs=P(("draws", "spec"), None, None, None),
        check_vma=False,
    )
```

```python
import math

import jax
import jax.numpy as jnp
from jax import lax
from jax.experimental import pallas as pl
from jax.experimental.pallas import tpu as pltpu
from jax.sharding import PartitionSpec as P

NLON = 1280
FINE = 256
SPAN = 640
LANES = 128

PRECISE = lax.Precision.HIGHEST
F32 = jnp.float32
BF16 = jnp.bfloat16


def prior_spread(orders, slots, waves):
    parity = jnp.arange(2, dtype=jnp.int32)[None, :, None]
    degree = orders[:, None, None] + 2 * slots[None, None, :] + parity
    spread = lax.rsqrt((degree + 1).astype(F32) * waves)
    return jnp.where(degree < waves, spread, jnp.zeros_like(spread))


def split(x):
    high = x.astype(BF16)
    return high, (x - high.astype(F32)).astype(BF16)


def dot(a, b):
    return jnp.dot(a, b, preferred_element_type=F32)


def dot3(a, b):
    ah, al = split(a)
    bh, bl = split(b)
    return dot(ah, bh) + dot(al, bh) + dot(ah, bl)


def place_in_ring(n):
    me = lax.axis_index("spec")
    core = me % 2
    side = (me // 2) % 2
    layer = me // 4
    return me, core, side, layer


def fill_lookup(tile, count, fcos_ref, fsin_ref, high_ref, low_ref):
    points, lanes = fcos_ref.shape
    steps = high_ref.shape[1] // points
    tiny = 16
    middle = points // tiny
    coarse = -(-steps // 8) * 8
    whole = count.astype(F32)
    table = (tiny + middle + coarse, lanes)
    index = lax.broadcasted_iota(jnp.int32, table, 0)
    order = lax.broadcasted_iota(jnp.int32, table, 1) + tile * lanes
    places = jnp.where(index < tiny, index, (index - tiny) * tiny)
    places = jnp.where(index < tiny + middle, places, (index - tiny - middle) * points)
    phases = (places * order).astype(F32)
    phases = phases - jnp.floor(phases / whole) * whole
    angles = 2.0 * math.pi * phases / whole
    cosine, sine = jnp.cos(angles), jnp.sin(angles)
    weights = jnp.where(order == 0, 1.0, 2.0) * jnp.where(2 * order < count, 1.0, 0.0)
    first = tiny + middle
    base_c, base_s = (cosine * weights)[first:], (sine * weights)[first:]
    for b in range(middle):
        turn_c, turn_s = cosine[tiny + b:tiny + b + 1], sine[tiny + b:tiny + b + 1]
        fcos_ref[pl.ds(b * tiny, tiny), :] = cosine[:tiny] * turn_c - sine[:tiny] * turn_s
        fsin_ref[pl.ds(b * tiny, tiny), :] = sine[:tiny] * turn_c + cosine[:tiny] * turn_s
    fine_c, fine_s = fcos_ref[...], fsin_ref[...]
    for step in range(steps):
        turn_c, turn_s = base_c[step:step + 1], base_s[step:step + 1]
        lookup_c = turn_c * fine_c - turn_s * fine_s
        lookup_s = -(turn_s * fine_c + turn_c * fine_s)
        high, low = split(jnp.concatenate((lookup_c, lookup_s), axis=1))
        high_ref[tile, pl.ds(step * points, points), :] = high
        low_ref[tile, pl.ds(step * points, points), :] = low


def add_tile(tile, spectra_ref, basis_ref, high_ref, low_ref, temps_ref, after=None):
    lanes = LANES
    first = 2 * lanes * tile
    even = spectra_ref[pl.ds(first, lanes, stride=2), :]
    odd = spectra_ref[pl.ds(first + 1, lanes, stride=2), :]
    half = even.shape[1] // 2
    real = jnp.concatenate((even[:, :half], odd[:, :half]), axis=1)
    imag = jnp.concatenate((even[:, half:], odd[:, half:]), axis=1)
    basis = basis_ref[...]
    top = jnp.concatenate((basis, basis), axis=1)
    wide = jnp.concatenate((top, jnp.concatenate((basis, -basis), axis=1)), axis=0)
    high, low = split(dot3(jnp.concatenate((real, imag), axis=0), wide))
    for step in range(temps_ref.shape[0] // FINE):
        at = pl.ds(step * FINE, FINE)
        lookup_high = high_ref[tile, at, :]
        temps_ref[at, :] += dot(lookup_high, high) + (dot(low_ref[tile, at, :], high) + dot(lookup_high, low))
        if after is not None:
            after(step)


def exchange_kernel(
    n, waves, cut, count_ref, coef_hbm, leg_hbm, basis_hbm, out_hbm, temps_ref, coef_ref, leg_ref, basis_ref, turn_ref, raw_ref, send_ref, seed_ref, hold_ref,
    wide_ref, sums_ref, near_ref, side_ref, far_ref, up_ref, spectra_ref, fcos_ref, fsin_ref, high_ref, low_ref, coef_sem, leg_sem, basis_sem, out_sem, seed_send, seed_recv, hold_send, hold_recv,
    near_send, near_recv, side_send, side_recv, last_send, come_recv, far_send, up_recv, lone_send, lone_recv,
):
    me, core, side, layer = place_in_ring(n)
    layers = n // 4
    units = n * cut
    chip = me // 2
    rows = n
    columns = coef_hbm.shape[1]
    every = leg_ref.shape[1]
    slots = every // n
    lanes = LANES
    pairs = lanes // rows
    per = pairs // 2
    own = waves // n
    groups = own // (per * cut)
    depth = per * slots * 2
    part = groups * pairs
    room = seed_ref.shape[1] // (2 * cut)
    block = seed_ref.shape[1]
    partner = me + 1 - 2 * core
    across = me + 2 - 4 * side
    both = cut * (n - 2 * (2 * layer + 1))
    mine = cut * (n - 4 * layer)
    lag = 5

    def spot(z, y, c):
        return (z * 2 + y) * 2 + c

    def remote(src, dst, send_sem, recv_sem, target):
        return pltpu.make_async_remote_copy(
            src_ref=src, dst_ref=dst, send_sem=send_sem, recv_sem=recv_sem,
            device_id={"spec": target}, device_id_type=pl.DeviceIdType.MESH,
        )

    def seed_copy(source, target):
        return remote(send_ref.at[target], seed_ref.at[source], seed_send.at[target], seed_recv.at[source], target)

    def hold_copy(place, target):
        at = spot(layer, 1 - side, place)
        return remote(send_ref.at[target], hold_ref.at[core], seed_send.at[target], hold_recv.at[core], at)

    def hold_come(k):
        return remote(hold_ref.at[k], hold_ref.at[k], hold_send.at[k], hold_recv.at[k], across)

    def hold_pass(k):
        owner = spot(layer, 1 - side, k)
        return remote(hold_ref.at[k], seed_ref.at[owner], hold_send.at[k], seed_recv.at[owner], spot(0, side, core))

    def near_copy(q, t):
        ring = near_recv.shape[0]
        return remote(sums_ref.at[q, 1 - core], near_ref.at[q], near_send, near_recv.at[t % ring], partner)

    def side_copy(q, z, t):
        at = t % side_recv.shape[0]
        return remote(sums_ref.at[q, core, 1 - side, z], side_ref.at[q, z], side_send.at[0], side_recv.at[at], across)

    def side_come(q, t):
        return remote(rest_of(side_ref.at[q]), rest_of(side_ref.at[q]), side_send.at[0], side_recv.at[t % side_recv.shape[0]], across)

    def last_copy(q):
        return remote(
            sums_ref.at[q, core, 1 - side, layer], side_ref.at[q, layer], last_send.at[0], come_recv.at[q // cut], across
        )

    def lone(q):
        return q - both

    def lone_copy(q, z):
        return remote(
            sums_ref.at[q, core, 1 - side, z], side_ref.at[q, z], lone_send.at[lone(q)], lone_recv.at[lone(q)], across
        )

    def lone_part(q, pieces):
        part_ref = side_ref.at[q, pl.ds(0, pieces)]
        return remote(part_ref, part_ref, lone_send.at[lone(q)], lone_recv.at[lone(q)], across)

    def relayed(z, at):
        return z != at and at > 0

    def relays(at):
        return [z for z in range(layers) if relayed(z, at)]

    def rest_of(ref):
        return ref.at[pl.ds(0, layers - 1)]

    def far_copy(q, target):
        return remote(
            sums_ref.at[q, core, side, target], far_ref.at[layer, q],
            far_send.at[0], come_recv.at[q // cut], spot(target, side, core),
        )

    def come(c, pieces):
        arrived = far_ref.at[pl.ds(0, pieces), pl.ds(c * cut, cut)]
        return remote(arrived, arrived, far_send.at[0], come_recv.at[c], across)

    def up_copy(q, target):
        return remote(
            sums_ref.at[q, core, side, target], up_ref.at[q, target],
            far_send.at[0], up_recv.at[q], spot((layer + 1) % layers, side, core),
        )

    def up_come(q, lower):
        pieces = up_ref.at[q, pl.ds(lower + 1, layers - 1 - lower)]
        return remote(pieces, pieces, far_send.at[0], up_recv.at[q], across)

    def diag_copy(q, target):
        return remote(
            sums_ref.at[q, core, 1 - side, target], far_ref.at[layer, q],
            lone_send.at[lone(q)], come_recv.at[q // cut], spot(target, 1 - side, core),
        )

    def relay_copy(q, target):
        return remote(
            side_ref.at[q, target], far_ref.at[layer, q],
            lone_send.at[lone(q)], come_recv.at[q // cut], spot(target, side, core),
        )

    def signal(target):
        pl.semaphore_signal(barrier, inc=1, device_id={"spec": target}, device_id_type=pl.DeviceIdType.MESH)

    corners = [(dy, dc) for dy in range(2) for dc in range(2)]

    def corner(z, offset):
        dy, dc = offset
        return spot(z, (side + dy) % 2, (core + dc) % 2)

    pieces = coef_sem.shape[0]
    share = n // pieces

    def coef_copy(q):
        size = share * cut * groups * depth
        at = pl.ds(pl.multiple_of(q * size, size), size)
        return pltpu.make_async_copy(coef_hbm.at[at, :], coef_ref.at[at, :], coef_sem.at[q])

    barrier = pltpu.get_barrier_semaphore()
    for offset in corners[1:]:
        signal(corner(layer, offset))

    @pl.when(layer > 0)
    def _():
        for dz in range(1, layers - 1):
            for offset in corners:
                signal(corner(1 + (layer - 1 + dz) % (layers - 1), offset))

    leg_copy = pltpu.make_async_copy(leg_hbm, leg_ref, leg_sem)
    leg_copy.start()

    basis_copy = pltpu.make_async_copy(basis_hbm, basis_ref, basis_sem)
    basis_copy.start()

    row = lax.broadcasted_iota(jnp.int32, (lanes, lanes), 0)
    lane = lax.broadcasted_iota(jnp.int32, (lanes, lanes), 1)
    row_at = row % rows
    ordered = ((row_at % 2) * 2 + (row_at // 2) % 2) * layers + row_at // 4
    moves = jnp.where(ordered * pairs + row // rows == lane, 1.0, 0.0).astype(BF16)

    raw_ref[...] = jnp.zeros(raw_ref.shape, F32)
    leg_copy.wait()
    for q in range(pieces):
        @pl.when(me + q * share < n)
        def _():
            coef_copy(q).start()

    for g in range(cut * groups):
        at = (g // groups) * 2 * room + g % groups
        turn_ref[...] = jnp.transpose(leg_ref[pl.ds(g * lanes, lanes), :])
        raw_ref[pl.ds(at, n, stride=block), :] = turn_ref[pl.ds(0, n, stride=slots), :]
        raw_ref[pl.ds(at + room, n, stride=block), :] = turn_ref[pl.ds(1, n, stride=slots), :]
    start = jnp.broadcast_to(raw_ref[pl.ds(0, 1), :], (8, lanes))
    cosine = pltpu.roll(start, lanes - rows, 1) / start
    sine = pltpu.roll(start, lanes - 2 * rows, 1) / start
    sine = sine * sine * (2.0 / 3.0)
    square = jnp.where(sine < 0.5, 1.0 - sine, cosine * cosine * (1.0 / 3.0))
    square = jnp.where(lax.broadcasted_iota(jnp.int32, (8, lanes), 1) < rows, square, 0.0)
    shift = rows
    while shift < lanes:
        square = square + pltpu.roll(square, shift, 1)
        shift *= 2
    square = jnp.where(me == 0, square, 0.0)
    raw_ref[pl.ds(groups, n, stride=block), :] = jnp.broadcast_to(square[:1], (n, lanes))
    raw = raw_ref[...]
    high = raw.astype(BF16)
    rest = raw - high.astype(F32)
    middle = rest.astype(BF16)
    low = (rest - middle.astype(F32)).astype(BF16)
    send_ref[...] = (dot(high, moves) + (dot(middle, moves) + dot(low, moves))).reshape(send_ref.shape)
    seed_ref[me] = send_ref[me]

    def give_seeds(z, offset):
        target = corner(z, offset)

        @pl.when(me + target < n)
        def _():
            seed_copy(me, target).start()

    @pl.when(layer == 0)
    def _():
        pl.semaphore_wait(barrier, len(corners) - 1)
        for dz in range(1, layers):
            for offset in corners:
                signal(corner(dz, offset))
        for offset in corners[1:]:
            give_seeds(layer, offset)

    @pl.when(layer > 0)
    def _():
        pl.semaphore_wait(barrier, n - 1)
        for offset in corners:
            signal(corner(0, offset))
        for dy, dc in corners:
            target = spot(0, (side + dy) % 2, (core + dc) % 2)

            @pl.when(me + target < n)
            def _():
                if dy:
                    hold_copy((core + dc) % 2, target).start()
                else:
                    seed_copy(me, target).start()

        for offset in corners[1:]:
            give_seeds(layer, offset)
        for dz in range(1, layers - 1):
            for offset in corners:
                give_seeds(1 + (layer - 1 + dz) % (layers - 1), offset)
        for k in range(2):
            @pl.when(spot(layer, 1 - side, k) + spot(0, side, core) < n)
            def _():
                hold_come(k).wait_recv()
                hold_pass(k).start()

    tiles = waves // lanes

    def fill(tile):
        fill_lookup(tile, count_ref[0], fcos_ref, fsin_ref, high_ref, low_ref)

    @pl.when(layer > 0)
    def _():
        @pl.loop(0, tiles)
        def _(tile):
            fill(tile)

    def meet():
        @pl.when(layer == 0)
        def _():
            pl.semaphore_wait(barrier, n - len(corners))
            for dz in range(1, layers):
                for offset in corners:
                    give_seeds(dz, offset)

    expand_row = lax.broadcasted_iota(jnp.int32, (depth, lanes), 0)
    expand_lane = lax.broadcasted_iota(jnp.int32, (depth, lanes), 1) % pairs
    keep = (expand_row // (2 * slots)) * 2 + expand_row % 2 == expand_lane
    pair_at = lax.broadcasted_iota(jnp.int32, (room, lanes), 1) % pairs
    order_part = lax.broadcasted_iota(jnp.int32, (room, lanes), 0) * per + pair_at // 2

    def recur(u):
        owner = u // cut
        at = pl.multiple_of((u % cut) * (2 * room), 2 * room)
        order = order_part + u * (groups * per)
        first = order + pair_at % 2 + me * (2 * slots)
        m = order.astype(F32)
        square = seed_ref[0, pl.ds(groups, 1), :]

        def coupling(d):
            return ((d - m) * (d + m)) / ((2.0 * d - 1.0) * (2.0 * d + 1.0))

        def place(s, value):
            degree = first + 2 * s
            spread = lax.rsqrt((degree + 1).astype(F32) * float(waves))
            value = value * jnp.where(degree < waves, spread, 0.0)
            wide_ref[pl.ds(2 * s, room, stride=2 * slots), :] = value
            wide_ref[pl.ds(2 * s + 1, room, stride=2 * slots), :] = value

        before = seed_ref[owner, pl.ds(at, room), :]
        now = seed_ref[owner, pl.ds(at + room, room), :]
        place(0, before)
        place(1, now)
        degree = first.astype(F32)
        last = coupling(degree + 2.0)
        weight = jnp.sqrt(coupling(degree + 1.0) * last)
        for s in range(1, slots - 1):
            degree = degree + 2.0
            one, two = coupling(degree + 1.0), coupling(degree + 2.0)
            product = one * two
            inverse = lax.rsqrt(product)
            before, now = now, ((square - (one + last)) * now - weight * before) * inverse
            weight = product * inverse
            last = two
            place(s + 1, now)

    def partial(u):
        owner = u // cut

        @pl.when(me + owner < n)
        def _():
            @pl.when(u % cut == 0)
            def _():
                @pl.when(owner % share == 0)
                def _():
                    coef_copy(owner // share).wait()

                @pl.when(owner != me)
                def _():
                    seed_copy(owner, me).wait_recv()

            recur(u)
            for g in range(groups):
                at = u * groups + g
                values = coef_ref[pl.ds(pl.multiple_of(at * depth, depth), depth), :]
                one = wide_ref[pl.ds(g * 2 * slots, 2 * slots), :]
                tiled = jnp.where(keep, jnp.concatenate([one] * per, axis=0), 0.0)
                both = jnp.concatenate(split(tiled), axis=1)
                sums = lax.dot_general(both, values, (((0,), (0,)), ((), ())), preferred_element_type=F32)
                sums = (sums[:lanes] + sums[lanes:]).reshape(2, 2, layers, pairs, columns)
                sums_ref[u, :, :, :, pl.ds(g * pairs, pairs), :] = sums

        @pl.when(me + owner >= n)
        def _():
            sums_ref[u] = jnp.zeros((2, 2, layers, part, columns), F32)

    def held(q, place):
        return q // cut + 2 * place < n

    def compute(q, t):
        @pl.when(held(q, chip))
        def _():
            partial(q)

            near_copy(q, t).start()

    def merge_near(q, t):
        shared = held(q, across // 2)

        @pl.when(held(q, chip))
        def _():
            near_copy(q, t).wait_recv()

            for y in (0, 1):
                @pl.loop(0, layers)
                def _(z):
                    sums_ref[q, core, y, z] += near_ref[q, y, z]

            @pl.when(shared)
            def _():
                for dz in reversed(range(1, layers)):
                    side_copy(q, (layer + dz) % layers, t).start()

            @pl.when(jnp.logical_not(shared))
            def _():
                for at in range(1, layers):
                    @pl.when(layer == at)
                    def _():
                        for z in relays(at):
                            lone_copy(q, z).start()

                last_copy(q).start()

    def pass_on(q, t):
        shared = held(q, across // 2)

        @pl.when(held(q, chip))
        def _():
            @pl.when(shared)
            def _():
                side_come(q, t).wait_recv()

            for lower in range(1, layers - 1):
                @pl.when(layer == lower)
                def _():
                    up_come(q, lower).wait_recv()

            for dz in reversed(range(1, layers)):
                z = (layer + dz) % layers
                upward = jnp.logical_and(z > layer + 1, held(q, chip + 2))

                @pl.when(shared)
                def _():
                    sums_ref[q, core, side, z] += side_ref[q, z]

                @pl.when(jnp.logical_and(layer > 0, z > layer))
                def _():
                    sums_ref[q, core, side, z] += up_ref[q, z]

                @pl.when(upward)
                def _():
                    up_copy(q, z).start()

                @pl.when(jnp.logical_not(upward))
                def _():
                    far_copy(q, z).start()

            for at in range(layers - 1):
                straight = [z for z in reversed(range(at + 1, layers)) if not relayed(z, at)]
                if straight:
                    @pl.when(jnp.logical_and(jnp.logical_not(shared), layer == at))
                    def _():
                        for z in straight:
                            diag_copy(q, z).start()

        @pl.when(jnp.logical_and(jnp.logical_not(held(q, chip)), jnp.logical_and(shared, layer > 0)))
        def _():
            for lower in range(1, layers):
                @pl.when(layer == lower)
                def _():
                    lone_part(q, len(relays(lower))).wait_recv()
                    for z in relays(lower):
                        relay_copy(q, z).start()

    def unit_at(t):
        turn = n // 2
        block_at, place = t // turn, t % turn
        early = jnp.where(place == turn - 1, both + block_at, block_at * (turn - 1) + place)
        late = jnp.where(t < both + 2, t - 2, t)
        return jnp.where(layer == 0, jnp.where(t < 2 * turn, early, late), t)

    def finish(c):
        near_part = held(c * cut, chip)

        pieces = jnp.where(held(c * cut, across // 2), 1, 0)
        for dz in range(1, layers):
            source = (layer + dz) % layers
            passed = jnp.logical_and(source + 1 < layer, held(c * cut, 2 * (source + 1) + side))
            sends = jnp.logical_and(held(c * cut, 2 * source), jnp.logical_not(passed))
            pieces = pieces + jnp.where(sends, 1, 0)
        for number in range(1, layers + 1):
            @pl.when(pieces == number)
            def _():
                come(c, number).wait_recv()

        for half in range(cut):
            q = c * cut + half
            at = pl.ds(pl.multiple_of(q * part, part), part)

            @pl.when(near_part)
            def _():
                spectra_ref[at, :] = sums_ref[q, core, side, layer]

            @pl.when(jnp.logical_not(near_part))
            def _():
                spectra_ref[at, :] = jnp.zeros((part, columns), F32)

            for dz in range(1, layers):
                source = (layer + dz) % layers
                passed = jnp.logical_and(source + 1 < layer, held(q, 2 * (source + 1) + side))

                @pl.when(jnp.logical_and(held(q, 2 * source), jnp.logical_not(passed)))
                def _():
                    spectra_ref[at, :] += far_ref[source, q]

            @pl.when(held(q, across // 2))
            def _():
                spectra_ref[at, :] += side_ref[q, layer]

    temps_ref[...] = jnp.zeros(temps_ref.shape, F32)
    basis_copy.wait()
    early = jnp.logical_and(layer == 1, side == 0)

    def out_copy(step):
        at = pl.ds(step * FINE, FINE)
        return pltpu.make_async_copy(temps_ref.at[at, :], out_hbm.at[at, :], out_sem)

    def stage(tile, after=None):
        @pl.loop((tile * lanes + own - 1) // own, ((tile + 1) * lanes + own - 1) // own)
        def _(c):
            finish(c)

        add_tile(tile, spectra_ref, basis_ref, high_ref, low_ref, temps_ref, after)

    @pl.loop(0, units + lag)
    def _(t):
        @pl.when(t == lag)
        def _():
            meet()

        @pl.when(jnp.logical_and(layer == 0, jnp.logical_and(t >= 2 * lag, t < 2 * (lag + tiles))))
        def _():
            @pl.when(t % 2 == 0)
            def _():
                fill(t // 2 - lag)

        @pl.when(t < units)
        def _():
            compute(unit_at(t), t)

        @pl.when(jnp.logical_and(t >= 1, t <= units))
        def _():
            merge_near(unit_at(t - 1), t - 1)

        @pl.when(t == mine)
        def _():
            @pl.loop(0, both)
            def _(q):
                last_copy(q).start()

        @pl.when(jnp.logical_and(early, t == mine + 1))
        def _():
            stage(0)

        @pl.when(t >= lag)
        def _():
            pass_on(unit_at(t - lag), t - lag)

    @pl.loop(0, n)
    def _(target):
        @pl.when(jnp.logical_and(target != me, me + target < n))
        def _():
            seed_copy(me, target).wait_send()

    for k in range(2):
        @pl.when(jnp.logical_and(layer > 0, spot(layer, 1 - side, k) + spot(0, side, core) < n))
        def _():
            hold_pass(k).wait_send()

    @pl.loop(jnp.where(early, 1, 0), tiles - 1)
    def _(tile):
        stage(tile)

    stage(tiles - 1, lambda step: out_copy(step).start())

    for place in range(n // 2):
        count = cut * (n - 2 * place)
        pair = cut * (n - 2 * (place // 2 * 2 + 1))

        @pl.when(chip == place)
        def _():
            near = near_ref.at[pl.ds(0, count)]
            remote(near, near, near_send, near_recv.at[0], across).wait_send()
            side = side_ref.at[pl.ds(0, pair), pl.ds(0, layers - 1)]
            remote(side, side, side_send.at[0], side_recv.at[0], across).wait_send()
            last = side_ref.at[pl.ds(0, count), 0]
            remote(last, last, last_send.at[0], come_recv.at[0], across).wait_send()
            far = far_ref.at[pl.ds(0, layers - 1), pl.ds(0, count)]
            remote(far, far, far_send.at[0], come_recv.at[0], across).wait_send()

    for lower in range(layers):
        @pl.when(jnp.logical_and(layer == lower, side == 0))
        def _():
            for k in range(lone_send.shape[0]):
                lone_part(both + k, layers - 1).wait_send()

        if lower:
            @pl.when(jnp.logical_and(layer == lower, side == 1))
            def _():
                for k in range(lone_send.shape[0]):
                    lone_part(both + k, len(relays(lower))).wait_send()

    pltpu.make_async_copy(temps_ref, out_hbm, out_sem).wait()


def exchanged_temps(coefficients, legendre, row_counts, basis, n, points):
    waves, _, slots, columns = coefficients.shape
    own, _, every, rows = legendre.shape
    dense = jnp.transpose(coefficients, (0, 2, 1, 3)).reshape(waves * slots * 2, columns)
    legs = jnp.transpose(legendre, (0, 1, 3, 2)).reshape(own * 2 * rows, every)
    layers = n // 4
    pairs = LANES // rows
    groups = own * 2 // pairs
    cut = 2 if groups % 2 == 0 else 1
    units = n * cut
    width = groups // cut * pairs
    room = -(-(groups // cut + 1) // 8) * 8
    block = cut * 2 * room
    dma = pltpu.SemaphoreType.DMA

    def body(*refs):
        exchange_kernel(n, waves, cut, *refs)

    return pl.pallas_call(
        body,
        out_shape=jax.ShapeDtypeStruct((points, 2 * basis.shape[1]), F32),
        in_specs=[pl.BlockSpec(memory_space=pltpu.SMEM)] + [pl.BlockSpec(memory_space=pl.ANY)] * 3,
        out_specs=pl.BlockSpec(memory_space=pl.ANY),
        scratch_shapes=[
            pltpu.VMEM((points, 2 * basis.shape[1]), F32),
            pltpu.VMEM(dense.shape, BF16),
            pltpu.VMEM(legs.shape, F32),
            pltpu.VMEM(basis.shape, F32),
            pltpu.VMEM((every, LANES), F32),
            pltpu.VMEM((n * block, LANES), F32),
            pltpu.VMEM((n, block, LANES), F32),
            pltpu.VMEM((n, block, LANES), F32),
            pltpu.VMEM((2, block, LANES), F32),
            pltpu.VMEM((room * 2 * slots, LANES), F32),
            pltpu.VMEM((units, 2, 2, layers, width, columns), F32),
            pltpu.VMEM((units, 2, layers, width, columns), F32),
            pltpu.VMEM((units, layers, width, columns), F32),
            pltpu.VMEM((layers, units, width, columns), F32),
            pltpu.VMEM((units, layers, width, columns), F32),
            pltpu.VMEM((2 * waves, columns), F32),
            pltpu.VMEM((FINE, LANES), F32),
            pltpu.VMEM((FINE, LANES), F32),
            pltpu.VMEM((waves // LANES, points, 2 * LANES), BF16),
            pltpu.VMEM((waves // LANES, points, 2 * LANES), BF16),
            dma((n // 2,)), dma, dma, dma, dma((n,)), dma((n,)), dma((2,)), dma((2,)),
            dma, dma((8,)),
            dma((1,)), dma((16,)),
            dma((1,)), dma((n,)),
            dma((1,)), dma((units - 4 * cut,)), dma((2 * cut,)), dma((2 * cut,)),
        ],
        compiler_params=pltpu.CompilerParams(
            collective_id=0, has_side_effects=True, vmem_limit_bytes=58 * 1024 * 1024
        ),
        name="exchanged_temps",
    )(row_counts, dense, legs, basis)


def plain_temps(spectra, row_counts, basis, points):
    tiles = spectra.shape[0] // (2 * LANES)

    def body(count_ref, spectra_ref, basis_ref, temps_ref, fcos_ref, fsin_ref, high_ref, low_ref):
        temps_ref[...] = jnp.zeros(temps_ref.shape, F32)
        for tile in range(tiles):
            fill_lookup(tile, count_ref[0], fcos_ref, fsin_ref, high_ref, low_ref)
            add_tile(tile, spectra_ref, basis_ref, high_ref, low_ref, temps_ref)

    vmem = pl.BlockSpec(memory_space=pltpu.VMEM)
    return pl.pallas_call(
        body,
        out_shape=jax.ShapeDtypeStruct((points, 2 * basis.shape[1]), F32),
        in_specs=[pl.BlockSpec(memory_space=pltpu.SMEM), vmem, vmem],
        out_specs=vmem,
        scratch_shapes=[pltpu.VMEM((FINE, LANES), F32)] * 2 + [pltpu.VMEM((tiles, points, 2 * LANES), BF16)] * 2,
        name="plain_temps",
    )(row_counts, spectra, basis)


def row_kernel(count_ref, temps_ref, absorb_ref, peak_ref, width_ref, out_ref, rhigh_ref, rlow_ref):
    step = pl.program_id(0)
    levels = absorb_ref.shape[1]
    points = temps_ref.shape[0]

    @pl.when(step == 0)
    def _():
        height = lax.broadcasted_iota(jnp.int32, rlow_ref.shape, 0)
        offsets = (height - peak_ref[...]).astype(F32) / width_ref[...]
        shape = jnp.exp(-offsets * offsets)
        high, low = split(shape / jnp.sum(shape, axis=0, keepdims=True))
        rhigh_ref[pl.ds(0, levels), :] = high
        rhigh_ref[pl.ds(levels, levels), :] = high
        rlow_ref[...] = low

    temps = temps_ref[...]
    temps = jnp.concatenate((temps[:, :levels], temps[:, levels:]), axis=0)

    source = jnp.exp(0.5 * temps)
    layers = absorb_ref[...] * source
    before = lax.broadcasted_iota(jnp.int32, (2 * levels, levels), 0) % levels
    after = lax.broadcasted_iota(jnp.int32, (2 * levels, levels), 1)
    upper = jnp.where(before < after, 1.0, 0.0).astype(BF16)
    layers_high, layers_low = split(layers)
    above = dot(jnp.concatenate((layers_high, layers_low), axis=1), upper)
    emitted = source * jnp.exp(-above) * (1.0 - jnp.exp(-layers))
    place = step * points + lax.broadcasted_iota(jnp.int32, (2 * points, levels), 0) % points
    emitted = jnp.where(place < count_ref[0], emitted, 0.0)
    emitted_high, emitted_low = split(emitted)
    bright = dot(jnp.concatenate((emitted_high, emitted_low), axis=1), rhigh_ref[...])
    bright = bright + dot(emitted_high, rlow_ref[...])
    out_ref[0, 0] = bright[:points]
    out_ref[0, 1] = bright[points:]


def radiate_row(temps, row_counts, absorb, peak_level, width):
    points = temps.shape[0]
    span = SPAN if points % SPAN == 0 else FINE
    levels, channels = absorb.shape[0], width.shape[0]

    def whole(*shape):
        return pl.BlockSpec(shape, lambda i, *_: (0,) * len(shape))

    return pl.pallas_call(
        row_kernel,
        out_shape=jax.ShapeDtypeStruct((1, 2, points, channels), F32),
        grid_spec=pltpu.PrefetchScalarGridSpec(
            num_scalar_prefetch=1,
            grid=(points // span,),
            in_specs=[
                pl.BlockSpec((span, 2 * levels), lambda i, *_: (i, 0)),
                whole(1, levels),
                whole(1, channels),
                whole(1, channels),
            ],
            out_specs=pl.BlockSpec((1, 2, span, channels), lambda i, *_: (0, 0, i, 0)),
            scratch_shapes=[
                pltpu.VMEM((2 * levels, channels), BF16),
                pltpu.VMEM((levels, channels), BF16),
            ],
        ),
        name="row_radiance",
    )(row_counts, temps, absorb[None, :], peak_level[None, :], width[None, :])


def moved_coefficients(coefficients, legendre):
    waves, _, slots, _ = coefficients.shape
    first = lax.axis_index("spec") * slots
    spread = prior_spread(jnp.arange(waves, dtype=jnp.int32), first + jnp.arange(slots, dtype=jnp.int32), waves)
    scaled = coefficients.astype(F32) * spread[..., None]
    spectral = lax.all_to_all(scaled, "spec", split_axis=0, concat_axis=2, tiled=True)
    sums = jnp.einsum("mpsj,mpsc->mpjc", legendre, spectral, precision=PRECISE)
    sums = lax.all_to_all(sums, "spec", split_axis=2, concat_axis=0, tiled=True)
    return sums.reshape(2 * waves, sums.shape[-1])


def on_device(coefficients, legendre, row_counts, basis, absorb, peak_level, width):
    own, _, every, rows = legendre.shape
    waves, _, slots, columns = coefficients.shape
    n = waves // own
    fits = n == rows and n % 8 == 0 and LANES % n == 0 and every == n * slots and columns == LANES
    fits = fits and (LANES // n) % 8 == 0 and own % (LANES // n) == 0 and slots % 4 == 0 and waves % LANES == 0
    if fits and (slots * LANES // n) % 16 == 0 and 2 * waves >= 2 * slots * n:
        temps = exchanged_temps(coefficients, legendre, row_counts, basis, n, NLON)
    else:
        spectra = moved_coefficients(coefficients, legendre)
        temps = plain_temps(spectra, row_counts, basis, NLON)
    return radiate_row(temps, row_counts, absorb, peak_level, width)


def solution(mesh):
    placed = (
        P("draws", None, "spec", None),
        P("spec", None, None, None),
        P("spec"),
        P(),
        P(),
        P(),
        P(),
    )
    return jax.shard_map(
        on_device,
        mesh=mesh,
        in_specs=placed,
        out_specs=P(("draws", "spec"), None, None, None),
        check_vma=False,
    )
```

```python
import math

import jax
import jax.numpy as jnp
from jax import lax
from jax.experimental import pallas as pl
from jax.experimental.pallas import tpu as pltpu
from jax.sharding import PartitionSpec as P

NLON = 1280
FINE = 256
SPAN = 640
LANES = 128

PRECISE = lax.Precision.HIGHEST
F32 = jnp.float32
BF16 = jnp.bfloat16


def prior_spread(orders, slots, waves):
    parity = jnp.arange(2, dtype=jnp.int32)[None, :, None]
    degree = orders[:, None, None] + 2 * slots[None, None, :] + parity
    spread = lax.rsqrt((degree + 1).astype(F32) * waves)
    return jnp.where(degree < waves, spread, jnp.zeros_like(spread))


def split(x):
    high = x.astype(BF16)
    return high, (x - high.astype(F32)).astype(BF16)


def dot(a, b):
    return jnp.dot(a, b, preferred_element_type=F32)


def dot3(a, b):
    ah, al = split(a)
    bh, bl = split(b)
    return dot(ah, bh) + dot(al, bh) + dot(ah, bl)


def place_in_ring(n):
    me = lax.axis_index("spec")
    core = me % 2
    side = (me // 2) % 2
    layer = me // 4
    return me, core, side, layer


def fill_lookup(tile, count, fcos_ref, fsin_ref, high_ref, low_ref):
    points, lanes = fcos_ref.shape
    steps = high_ref.shape[1] // points
    tiny = 16
    middle = points // tiny
    coarse = -(-steps // 8) * 8
    whole = count.astype(F32)
    table = (tiny + middle + coarse, lanes)
    index = lax.broadcasted_iota(jnp.int32, table, 0)
    order = lax.broadcasted_iota(jnp.int32, table, 1) + tile * lanes
    places = jnp.where(index < tiny, index, (index - tiny) * tiny)
    places = jnp.where(index < tiny + middle, places, (index - tiny - middle) * points)
    phases = (places * order).astype(F32)
    phases = phases - jnp.floor(phases / whole) * whole
    angles = 2.0 * math.pi * phases / whole
    cosine, sine = jnp.cos(angles), jnp.sin(angles)
    weights = jnp.where(order == 0, 1.0, 2.0) * jnp.where(2 * order < count, 1.0, 0.0)
    first = tiny + middle
    base_c, base_s = (cosine * weights)[first:], (sine * weights)[first:]
    for b in range(middle):
        turn_c, turn_s = cosine[tiny + b:tiny + b + 1], sine[tiny + b:tiny + b + 1]
        fcos_ref[pl.ds(b * tiny, tiny), :] = cosine[:tiny] * turn_c - sine[:tiny] * turn_s
        fsin_ref[pl.ds(b * tiny, tiny), :] = sine[:tiny] * turn_c + cosine[:tiny] * turn_s
    fine_c, fine_s = fcos_ref[...], fsin_ref[...]
    for step in range(steps):
        turn_c, turn_s = base_c[step:step + 1], base_s[step:step + 1]
        lookup_c = turn_c * fine_c - turn_s * fine_s
        lookup_s = -(turn_s * fine_c + turn_c * fine_s)
        high, low = split(jnp.concatenate((lookup_c, lookup_s), axis=1))
        high_ref[tile, pl.ds(step * points, points), :] = high
        low_ref[tile, pl.ds(step * points, points), :] = low


def add_tile(tile, spectra_ref, basis_ref, high_ref, low_ref, temps_ref, after=None):
    lanes = LANES
    first = 2 * lanes * tile
    even = spectra_ref[pl.ds(first, lanes, stride=2), :]
    odd = spectra_ref[pl.ds(first + 1, lanes, stride=2), :]
    half = even.shape[1] // 2
    real = jnp.concatenate((even[:, :half], odd[:, :half]), axis=1)
    imag = jnp.concatenate((even[:, half:], odd[:, half:]), axis=1)
    basis = basis_ref[...]
    top = jnp.concatenate((basis, basis), axis=1)
    wide = jnp.concatenate((top, jnp.concatenate((basis, -basis), axis=1)), axis=0)
    high, low = split(dot3(jnp.concatenate((real, imag), axis=0), wide))
    for step in range(temps_ref.shape[0] // FINE):
        at = pl.ds(step * FINE, FINE)
        lookup_high = high_ref[tile, at, :]
        temps_ref[at, :] += dot(lookup_high, high) + (dot(low_ref[tile, at, :], high) + dot(lookup_high, low))
        if after is not None:
            after(step)


def exchange_kernel(
    n, waves, cut, count_ref, coef_hbm, leg_hbm, basis_hbm, out_hbm, temps_ref, coef_ref, leg_ref, basis_ref, turn_ref, raw_ref, send_ref, seed_ref, hold_ref,
    wide_ref, sums_ref, near_ref, side_ref, far_ref, up_ref, spectra_ref, fcos_ref, fsin_ref, high_ref, low_ref, coef_sem, leg_sem, basis_sem, out_sem, seed_send, seed_recv, hold_send, hold_recv,
    near_send, near_recv, side_send, side_recv, last_send, come_recv, far_send, up_recv, lone_send, lone_recv,
):
    me, core, side, layer = place_in_ring(n)
    layers = n // 4
    units = n * cut
    chip = me // 2
    rows = n
    columns = coef_hbm.shape[1]
    every = leg_ref.shape[1]
    slots = every // n
    lanes = LANES
    pairs = lanes // rows
    per = pairs // 2
    own = waves // n
    groups = own // (per * cut)
    depth = per * slots * 2
    part = groups * pairs
    room = seed_ref.shape[1] // (2 * cut)
    block = seed_ref.shape[1]
    partner = me + 1 - 2 * core
    across = me + 2 - 4 * side
    both = cut * (n - 2 * (2 * layer + 1))
    mine = cut * (n - 4 * layer)
    lag = 5

    def spot(z, y, c):
        return (z * 2 + y) * 2 + c

    def remote(src, dst, send_sem, recv_sem, target):
        return pltpu.make_async_remote_copy(
            src_ref=src, dst_ref=dst, send_sem=send_sem, recv_sem=recv_sem,
            device_id={"spec": target}, device_id_type=pl.DeviceIdType.MESH,
        )

    def seed_copy(source, target):
        return remote(send_ref.at[target], seed_ref.at[source], seed_send, seed_recv.at[source], target)

    def hold_copy(place, target):
        at = spot(layer, 1 - side, place)
        return remote(send_ref.at[target], hold_ref.at[core], seed_send, hold_recv.at[core], at)

    def hold_come(k):
        return remote(hold_ref.at[k], hold_ref.at[k], hold_send.at[k], hold_recv.at[k], across)

    def hold_pass(k):
        owner = spot(layer, 1 - side, k)
        return remote(hold_ref.at[k], seed_ref.at[owner], hold_send.at[k], seed_recv.at[owner], spot(0, side, core))

    def near_copy(q, t):
        ring = near_recv.shape[0]
        return remote(sums_ref.at[q, 1 - core], near_ref.at[q], near_send, near_recv.at[t % ring], partner)

    def side_copy(q, z, t):
        at = t % side_recv.shape[0]
        return remote(sums_ref.at[q, core, 1 - side, z], side_ref.at[q, z], side_send.at[0], side_recv.at[at], across)

    def side_come(q, t):
        return remote(rest_of(side_ref.at[q]), rest_of(side_ref.at[q]), side_send.at[0], side_recv.at[t % side_recv.shape[0]], across)

    def last_copy(q):
        return remote(
            sums_ref.at[q, core, 1 - side, layer], side_ref.at[q, layer], last_send.at[0], come_recv.at[q // cut], across
        )

    def lone(q):
        return q - both

    def lone_copy(q, z):
        return remote(
            sums_ref.at[q, core, 1 - side, z], side_ref.at[q, z], lone_send.at[lone(q)], lone_recv.at[lone(q)], across
        )

    def lone_part(q, pieces):
        part_ref = side_ref.at[q, pl.ds(0, pieces)]
        return remote(part_ref, part_ref, lone_send.at[lone(q)], lone_recv.at[lone(q)], across)

    def relayed(z, at):
        return z != at and at > 0

    def relays(at):
        return [z for z in range(layers) if relayed(z, at)]

    def rest_of(ref):
        return ref.at[pl.ds(0, layers - 1)]

    def far_copy(q, target):
        return remote(
            sums_ref.at[q, core, side, target], far_ref.at[layer, q],
            far_send.at[0], come_recv.at[q // cut], spot(target, side, core),
        )

    def come(c, pieces):
        arrived = far_ref.at[pl.ds(0, pieces), pl.ds(c * cut, cut)]
        return remote(arrived, arrived, far_send.at[0], come_recv.at[c], across)

    def up_copy(q, target):
        return remote(
            sums_ref.at[q, core, side, target], up_ref.at[q, target],
            far_send.at[0], up_recv.at[q], spot((layer + 1) % layers, side, core),
        )

    def up_come(q, lower):
        pieces = up_ref.at[q, pl.ds(lower + 1, layers - 1 - lower)]
        return remote(pieces, pieces, far_send.at[0], up_recv.at[q], across)

    def diag_copy(q, target):
        return remote(
            sums_ref.at[q, core, 1 - side, target], far_ref.at[layer, q],
            lone_send.at[lone(q)], come_recv.at[q // cut], spot(target, 1 - side, core),
        )

    def relay_copy(q, target):
        return remote(
            side_ref.at[q, target], far_ref.at[layer, q],
            lone_send.at[lone(q)], come_recv.at[q // cut], spot(target, side, core),
        )

    def signal(target):
        pl.semaphore_signal(barrier, inc=1, device_id={"spec": target}, device_id_type=pl.DeviceIdType.MESH)

    corners = [(dy, dc) for dy in range(2) for dc in range(2)]

    def corner(z, offset):
        dy, dc = offset
        return spot(z, (side + dy) % 2, (core + dc) % 2)

    pieces = coef_sem.shape[0]
    share = n // pieces

    def coef_copy(q):
        size = share * cut * groups * depth
        at = pl.ds(pl.multiple_of(q * size, size), size)
        return pltpu.make_async_copy(coef_hbm.at[at, :], coef_ref.at[at, :], coef_sem.at[q])

    barrier = pltpu.get_barrier_semaphore()
    for offset in corners[1:]:
        signal(corner(layer, offset))

    @pl.when(layer > 0)
    def _():
        for dz in range(1, layers - 1):
            for offset in corners:
                signal(corner(1 + (layer - 1 + dz) % (layers - 1), offset))

    leg_copy = pltpu.make_async_copy(leg_hbm, leg_ref, leg_sem)
    leg_copy.start()

    basis_copy = pltpu.make_async_copy(basis_hbm, basis_ref, basis_sem)
    basis_copy.start()

    def greet():
        pl.semaphore_wait(barrier, len(corners) - 1)
        for dz in range(1, layers):
            for offset in corners:
                signal(corner(dz, offset))

    @pl.when(jnp.logical_and(layer == 0, side == 1))
    def _():
        greet()

    row = lax.broadcasted_iota(jnp.int32, (lanes, lanes), 0)
    lane = lax.broadcasted_iota(jnp.int32, (lanes, lanes), 1)
    row_at = row % rows
    ordered = ((row_at % 2) * 2 + (row_at // 2) % 2) * layers + row_at // 4
    moves = jnp.where(ordered * pairs + row // rows == lane, 1.0, 0.0).astype(BF16)

    raw_ref[...] = jnp.zeros(raw_ref.shape, F32)
    leg_copy.wait()
    coef_copy(0).start()

    for g in range(cut * groups):
        at = (g // groups) * 2 * room + g % groups
        turn_ref[...] = jnp.transpose(leg_ref[pl.ds(g * lanes, lanes), :])
        raw_ref[pl.ds(at, n, stride=block), :] = turn_ref[pl.ds(0, n, stride=slots), :]
        raw_ref[pl.ds(at + room, n, stride=block), :] = turn_ref[pl.ds(1, n, stride=slots), :]
    start = jnp.broadcast_to(raw_ref[pl.ds(0, 1), :], (8, lanes))
    cosine = pltpu.roll(start, lanes - rows, 1) / start
    sine = pltpu.roll(start, lanes - 2 * rows, 1) / start
    sine = sine * sine * (2.0 / 3.0)
    square = jnp.where(sine < 0.5, 1.0 - sine, cosine * cosine * (1.0 / 3.0))
    square = jnp.where(lax.broadcasted_iota(jnp.int32, (8, lanes), 1) < rows, square, 0.0)
    shift = rows
    while shift < lanes:
        square = square + pltpu.roll(square, shift, 1)
        shift *= 2
    square = jnp.where(me == 0, square, 0.0)
    raw_ref[pl.ds(groups, n, stride=block), :] = jnp.broadcast_to(square[:1], (n, lanes))
    raw = raw_ref[...]
    high = raw.astype(BF16)
    rest = raw - high.astype(F32)
    middle = rest.astype(BF16)
    low = (rest - middle.astype(F32)).astype(BF16)
    send_ref[...] = (dot(high, moves) + (dot(middle, moves) + dot(low, moves))).reshape(send_ref.shape)
    seed_ref[me] = send_ref[me]

    def give_seeds(z, offset):
        target = corner(z, offset)

        @pl.when(me + target < n)
        def _():
            seed_copy(me, target).start()

    @pl.when(jnp.logical_and(layer == 0, side == 0))
    def _():
        greet()

    @pl.when(layer == 0)
    def _():
        for offset in corners[1:]:
            give_seeds(layer, offset)

    @pl.when(layer > 0)
    def _():
        pl.semaphore_wait(barrier, n - 1)
        for offset in corners:
            signal(corner(0, offset))
        for dy, dc in corners:
            target = spot(0, (side + dy) % 2, (core + dc) % 2)

            @pl.when(me + target < n)
            def _():
                if dy:
                    hold_copy((core + dc) % 2, target).start()
                else:
                    seed_copy(me, target).start()

        for offset in corners[1:]:
            give_seeds(layer, offset)
        for dz in range(1, layers - 1):
            for offset in corners:
                give_seeds(1 + (layer - 1 + dz) % (layers - 1), offset)
        for k in range(2):
            @pl.when(spot(layer, 1 - side, k) + spot(0, side, core) < n)
            def _():
                hold_come(k).wait_recv()
                hold_pass(k).start()

    for q in range(1, pieces):
        @pl.when(me + q * share < n)
        def _():
            coef_copy(q).start()

    tiles = waves // lanes

    def fill(tile):
        fill_lookup(tile, count_ref[0], fcos_ref, fsin_ref, high_ref, low_ref)

    @pl.when(layer > 0)
    def _():
        @pl.loop(0, tiles)
        def _(tile):
            fill(tile)

    def meet():
        @pl.when(layer == 0)
        def _():
            pl.semaphore_wait(barrier, n - len(corners))
            for dz in range(1, layers):
                for offset in corners:
                    give_seeds(dz, offset)

    expand_row = lax.broadcasted_iota(jnp.int32, (depth, lanes), 0)
    expand_lane = lax.broadcasted_iota(jnp.int32, (depth, lanes), 1) % pairs
    keep = (expand_row // (2 * slots)) * 2 + expand_row % 2 == expand_lane
    pair_at = lax.broadcasted_iota(jnp.int32, (room, lanes), 1) % pairs
    order_part = lax.broadcasted_iota(jnp.int32, (room, lanes), 0) * per + pair_at // 2

    def recur(u):
        owner = u // cut
        at = pl.multiple_of((u % cut) * (2 * room), 2 * room)
        order = order_part + u * (groups * per)
        first = order + pair_at % 2 + me * (2 * slots)
        m = order.astype(F32)
        square = seed_ref[0, pl.ds(groups, 1), :]

        def coupling(d):
            return ((d - m) * (d + m)) / ((2.0 * d - 1.0) * (2.0 * d + 1.0))

        def place(s, value):
            degree = first + 2 * s
            spread = lax.rsqrt((degree + 1).astype(F32) * float(waves))
            value = value * jnp.where(degree < waves, spread, 0.0)
            wide_ref[pl.ds(2 * s, room, stride=2 * slots), :] = value
            wide_ref[pl.ds(2 * s + 1, room, stride=2 * slots), :] = value

        before = seed_ref[owner, pl.ds(at, room), :]
        now = seed_ref[owner, pl.ds(at + room, room), :]
        place(0, before)
        place(1, now)
        degree = first.astype(F32)
        last = coupling(degree + 2.0)
        weight = jnp.sqrt(coupling(degree + 1.0) * last)
        for s in range(1, slots - 1):
            degree = degree + 2.0
            one, two = coupling(degree + 1.0), coupling(degree + 2.0)
            product = one * two
            inverse = lax.rsqrt(product)
            before, now = now, ((square - (one + last)) * now - weight * before) * inverse
            weight = product * inverse
            last = two
            place(s + 1, now)

    def partial(u):
        owner = u // cut

        @pl.when(me + owner < n)
        def _():
            @pl.when(u % cut == 0)
            def _():
                @pl.when(owner % share == 0)
                def _():
                    coef_copy(owner // share).wait()

                @pl.when(owner != me)
                def _():
                    seed_copy(owner, me).wait_recv()

            recur(u)
            for g in range(groups):
                at = u * groups + g
                values = coef_ref[pl.ds(pl.multiple_of(at * depth, depth), depth), :]
                one = wide_ref[pl.ds(g * 2 * slots, 2 * slots), :]
                tiled = jnp.where(keep, jnp.concatenate([one] * per, axis=0), 0.0)
                both = jnp.concatenate(split(tiled), axis=1)
                sums = lax.dot_general(both, values, (((0,), (0,)), ((), ())), preferred_element_type=F32)
                sums = (sums[:lanes] + sums[lanes:]).reshape(2, 2, layers, pairs, columns)
                sums_ref[u, :, :, :, pl.ds(g * pairs, pairs), :] = sums

        @pl.when(me + owner >= n)
        def _():
            sums_ref[u] = jnp.zeros((2, 2, layers, part, columns), F32)

    def held(q, place):
        return q // cut + 2 * place < n

    def compute(q, t):
        @pl.when(held(q, chip))
        def _():
            partial(q)

            near_copy(q, t).start()

    def merge_near(q, t):
        shared = held(q, across // 2)

        @pl.when(held(q, chip))
        def _():
            near_copy(q, t).wait_recv()

            for y in (0, 1):
                @pl.loop(0, layers)
                def _(z):
                    sums_ref[q, core, y, z] += near_ref[q, y, z]

            @pl.when(shared)
            def _():
                for dz in reversed(range(1, layers)):
                    side_copy(q, (layer + dz) % layers, t).start()

            @pl.when(jnp.logical_not(shared))
            def _():
                for at in range(1, layers):
                    @pl.when(layer == at)
                    def _():
                        for z in relays(at):
                            lone_copy(q, z).start()

                last_copy(q).start()

    def pass_on(q, t):
        shared = held(q, across // 2)

        @pl.when(held(q, chip))
        def _():
            @pl.when(shared)
            def _():
                side_come(q, t).wait_recv()

            for lower in range(1, layers - 1):
                @pl.when(layer == lower)
                def _():
                    up_come(q, lower).wait_recv()

            for dz in reversed(range(1, layers)):
                z = (layer + dz) % layers
                upward = jnp.logical_and(z > layer + 1, held(q, chip + 2))

                @pl.when(shared)
                def _():
                    sums_ref[q, core, side, z] += side_ref[q, z]

                @pl.when(jnp.logical_and(layer > 0, z > layer))
                def _():
                    sums_ref[q, core, side, z] += up_ref[q, z]

                @pl.when(upward)
                def _():
                    up_copy(q, z).start()

                @pl.when(jnp.logical_not(upward))
                def _():
                    far_copy(q, z).start()

            for at in range(layers - 1):
                straight = [z for z in reversed(range(at + 1, layers)) if not relayed(z, at)]
                if straight:
                    @pl.when(jnp.logical_and(jnp.logical_not(shared), layer == at))
                    def _():
                        for z in straight:
                            diag_copy(q, z).start()

        @pl.when(jnp.logical_and(jnp.logical_not(held(q, chip)), jnp.logical_and(shared, layer > 0)))
        def _():
            for lower in range(1, layers):
                @pl.when(layer == lower)
                def _():
                    lone_part(q, len(relays(lower))).wait_recv()
                    for z in relays(lower):
                        relay_copy(q, z).start()

    def unit_at(t):
        turn = n // 2
        block_at, place = t // turn, t % turn
        early = jnp.where(place == turn - 1, both + block_at, block_at * (turn - 1) + place)
        late = jnp.where(t < both + 2, t - 2, t)
        return jnp.where(layer == 0, jnp.where(t < 2 * turn, early, late), t)

    def finish(c):
        near_part = held(c * cut, chip)

        pieces = jnp.where(held(c * cut, across // 2), 1, 0)
        for dz in range(1, layers):
            source = (layer + dz) % layers
            passed = jnp.logical_and(source + 1 < layer, held(c * cut, 2 * (source + 1) + side))
            sends = jnp.logical_and(held(c * cut, 2 * source), jnp.logical_not(passed))
            pieces = pieces + jnp.where(sends, 1, 0)
        for number in range(1, layers + 1):
            @pl.when(pieces == number)
            def _():
                come(c, number).wait_recv()

        for half in range(cut):
            q = c * cut + half
            at = pl.ds(pl.multiple_of(q * part, part), part)

            @pl.when(near_part)
            def _():
                spectra_ref[at, :] = sums_ref[q, core, side, layer]

            @pl.when(jnp.logical_not(near_part))
            def _():
                spectra_ref[at, :] = jnp.zeros((part, columns), F32)

            for dz in range(1, layers):
                source = (layer + dz) % layers
                passed = jnp.logical_and(source + 1 < layer, held(q, 2 * (source + 1) + side))

                @pl.when(jnp.logical_and(held(q, 2 * source), jnp.logical_not(passed)))
                def _():
                    spectra_ref[at, :] += far_ref[source, q]

            @pl.when(held(q, across // 2))
            def _():
                spectra_ref[at, :] += side_ref[q, layer]

    temps_ref[...] = jnp.zeros(temps_ref.shape, F32)
    basis_copy.wait()
    early = jnp.logical_and(layer == 1, side == 0)

    def out_copy(step):
        at = pl.ds(step * FINE, FINE)
        return pltpu.make_async_copy(temps_ref.at[at, :], out_hbm.at[at, :], out_sem)

    def drain():
        for place in range(n // 2):
            count = cut * (n - 2 * place)
            pair = cut * (n - 2 * (place // 2 * 2 + 1))

            @pl.when(chip == place)
            def _():
                near = near_ref.at[pl.ds(0, count)]
                remote(near, near, near_send, near_recv.at[0], across).wait_send()
                side = side_ref.at[pl.ds(0, pair), pl.ds(0, layers - 1)]
                remote(side, side, side_send.at[0], side_recv.at[0], across).wait_send()
                last = side_ref.at[pl.ds(0, count), 0]
                remote(last, last, last_send.at[0], come_recv.at[0], across).wait_send()
                far = far_ref.at[pl.ds(0, layers - 1), pl.ds(0, count)]
                remote(far, far, far_send.at[0], come_recv.at[0], across).wait_send()

        for lower in range(layers):
            @pl.when(jnp.logical_and(layer == lower, side == 0))
            def _():
                for k in range(lone_send.shape[0]):
                    lone_part(both + k, layers - 1).wait_send()

            if lower:
                @pl.when(jnp.logical_and(layer == lower, side == 1))
                def _():
                    for k in range(lone_send.shape[0]):
                        lone_part(both + k, len(relays(lower))).wait_send()

    def stage(tile, after=None):
        @pl.loop((tile * lanes + own - 1) // own, ((tile + 1) * lanes + own - 1) // own)
        def _(c):
            finish(c)

        if after is not None:
            @pl.when(layer > 0)
            def _():
                drain()

        add_tile(tile, spectra_ref, basis_ref, high_ref, low_ref, temps_ref, after)

    @pl.loop(0, units + lag)
    def _(t):
        @pl.when(t == lag - 1)
        def _():
            meet()

        @pl.when(jnp.logical_and(layer == 0, jnp.logical_and(t >= 2 * lag, t < 2 * (lag + tiles))))
        def _():
            @pl.when(t % 2 == 0)
            def _():
                fill(t // 2 - lag)

        @pl.when(t < units)
        def _():
            compute(unit_at(t), t)

        @pl.when(jnp.logical_and(t >= 1, t <= units))
        def _():
            merge_near(unit_at(t - 1), t - 1)

        @pl.when(t == mine)
        def _():
            @pl.loop(0, both)
            def _(q):
                last_copy(q).start()

        @pl.when(jnp.logical_and(early, t == mine + 1))
        def _():
            stage(0)

        @pl.when(t >= lag)
        def _():
            pass_on(unit_at(t - lag), t - lag)

    for number in range(1, n):
        @pl.when(jnp.where(2 * me < n, n - me - 1, n - me) == number)
        def _():
            gone = send_ref.at[pl.ds(0, number)]
            remote(gone, gone, seed_send, seed_recv.at[0], across).wait_send()

    for k in range(2):
        @pl.when(jnp.logical_and(layer > 0, spot(layer, 1 - side, k) + spot(0, side, core) < n))
        def _():
            hold_pass(k).wait_send()

    @pl.loop(jnp.where(early, 1, 0), tiles - 1)
    def _(tile):
        stage(tile)

    stage(tiles - 1, lambda step: out_copy(step).start())

    @pl.when(layer == 0)
    def _():
        drain()

    pltpu.make_async_copy(temps_ref, out_hbm, out_sem).wait()


def exchanged_temps(coefficients, legendre, row_counts, basis, n, points):
    waves, _, slots, columns = coefficients.shape
    own, _, every, rows = legendre.shape
    dense = jnp.transpose(coefficients, (0, 2, 1, 3)).reshape(waves * slots * 2, columns)
    legs = jnp.transpose(legendre, (0, 1, 3, 2)).reshape(own * 2 * rows, every)
    layers = n // 4
    pairs = LANES // rows
    groups = own * 2 // pairs
    cut = 2 if groups % 2 == 0 else 1
    units = n * cut
    width = groups // cut * pairs
    room = -(-(groups // cut + 1) // 8) * 8
    block = cut * 2 * room
    dma = pltpu.SemaphoreType.DMA

    def body(*refs):
        exchange_kernel(n, waves, cut, *refs)

    return pl.pallas_call(
        body,
        out_shape=jax.ShapeDtypeStruct((points, 2 * basis.shape[1]), F32),
        in_specs=[pl.BlockSpec(memory_space=pltpu.SMEM)] + [pl.BlockSpec(memory_space=pl.ANY)] * 3,
        out_specs=pl.BlockSpec(memory_space=pl.ANY),
        scratch_shapes=[
            pltpu.VMEM((points, 2 * basis.shape[1]), F32),
            pltpu.VMEM(dense.shape, BF16),
            pltpu.VMEM(legs.shape, F32),
            pltpu.VMEM(basis.shape, F32),
            pltpu.VMEM((every, LANES), F32),
            pltpu.VMEM((n * block, LANES), F32),
            pltpu.VMEM((n, block, LANES), F32),
            pltpu.VMEM((n, block, LANES), F32),
            pltpu.VMEM((2, block, LANES), F32),
            pltpu.VMEM((room * 2 * slots, LANES), F32),
            pltpu.VMEM((units, 2, 2, layers, width, columns), F32),
            pltpu.VMEM((units, 2, layers, width, columns), F32),
            pltpu.VMEM((units, layers, width, columns), F32),
            pltpu.VMEM((layers, units, width, columns), F32),
            pltpu.VMEM((units, layers, width, columns), F32),
            pltpu.VMEM((2 * waves, columns), F32),
            pltpu.VMEM((FINE, LANES), F32),
            pltpu.VMEM((FINE, LANES), F32),
            pltpu.VMEM((waves // LANES, points, 2 * LANES), BF16),
            pltpu.VMEM((waves // LANES, points, 2 * LANES), BF16),
            dma((n // 2,)), dma, dma, dma, dma, dma((n,)), dma((2,)), dma((2,)),
            dma, dma((8,)),
            dma((1,)), dma((12,)),
            dma((1,)), dma((n,)),
            dma((1,)), dma((units - 4 * cut,)), dma((2 * cut,)), dma((2 * cut,)),
        ],
        compiler_params=pltpu.CompilerParams(
            collective_id=0, has_side_effects=True, vmem_limit_bytes=58 * 1024 * 1024
        ),
        name="exchanged_temps",
    )(row_counts, dense, legs, basis)


def plain_temps(spectra, row_counts, basis, points):
    tiles = spectra.shape[0] // (2 * LANES)

    def body(count_ref, spectra_ref, basis_ref, temps_ref, fcos_ref, fsin_ref, high_ref, low_ref):
        temps_ref[...] = jnp.zeros(temps_ref.shape, F32)
        for tile in range(tiles):
            fill_lookup(tile, count_ref[0], fcos_ref, fsin_ref, high_ref, low_ref)
            add_tile(tile, spectra_ref, basis_ref, high_ref, low_ref, temps_ref)

    vmem = pl.BlockSpec(memory_space=pltpu.VMEM)
    return pl.pallas_call(
        body,
        out_shape=jax.ShapeDtypeStruct((points, 2 * basis.shape[1]), F32),
        in_specs=[pl.BlockSpec(memory_space=pltpu.SMEM), vmem, vmem],
        out_specs=vmem,
        scratch_shapes=[pltpu.VMEM((FINE, LANES), F32)] * 2 + [pltpu.VMEM((tiles, points, 2 * LANES), BF16)] * 2,
        name="plain_temps",
    )(row_counts, spectra, basis)


def row_kernel(count_ref, temps_ref, absorb_ref, peak_ref, width_ref, out_ref, rhigh_ref, rlow_ref):
    step = pl.program_id(0)
    levels = absorb_ref.shape[1]
    points = temps_ref.shape[0]

    @pl.when(step == 0)
    def _():
        height = lax.broadcasted_iota(jnp.int32, rlow_ref.shape, 0)
        offsets = (height - peak_ref[...]).astype(F32) / width_ref[...]
        shape = jnp.exp(-offsets * offsets)
        high, low = split(shape / jnp.sum(shape, axis=0, keepdims=True))
        rhigh_ref[pl.ds(0, levels), :] = high
        rhigh_ref[pl.ds(levels, levels), :] = high
        rlow_ref[...] = low

    temps = temps_ref[...]
    temps = jnp.concatenate((temps[:, :levels], temps[:, levels:]), axis=0)

    source = jnp.exp(0.5 * temps)
    layers = absorb_ref[...] * source
    before = lax.broadcasted_iota(jnp.int32, (2 * levels, levels), 0) % levels
    after = lax.broadcasted_iota(jnp.int32, (2 * levels, levels), 1)
    upper = jnp.where(before < after, 1.0, 0.0).astype(BF16)
    layers_high, layers_low = split(layers)
    above = dot(jnp.concatenate((layers_high, layers_low), axis=1), upper)
    emitted = source * jnp.exp(-above) * (1.0 - jnp.exp(-layers))
    place = step * points + lax.broadcasted_iota(jnp.int32, (2 * points, levels), 0) % points
    emitted = jnp.where(place < count_ref[0], emitted, 0.0)
    emitted_high, emitted_low = split(emitted)
    bright = dot(jnp.concatenate((emitted_high, emitted_low), axis=1), rhigh_ref[...])
    bright = bright + dot(emitted_high, rlow_ref[...])
    out_ref[0, 0] = bright[:points]
    out_ref[0, 1] = bright[points:]


def radiate_row(temps, row_counts, absorb, peak_level, width):
    points = temps.shape[0]
    span = SPAN if points % SPAN == 0 else FINE
    levels, channels = absorb.shape[0], width.shape[0]

    def whole(*shape):
        return pl.BlockSpec(shape, lambda i, *_: (0,) * len(shape))

    return pl.pallas_call(
        row_kernel,
        out_shape=jax.ShapeDtypeStruct((1, 2, points, channels), F32),
        grid_spec=pltpu.PrefetchScalarGridSpec(
            num_scalar_prefetch=1,
            grid=(points // span,),
            in_specs=[
                pl.BlockSpec((span, 2 * levels), lambda i, *_: (i, 0)),
                whole(1, levels),
                whole(1, channels),
                whole(1, channels),
            ],
            out_specs=pl.BlockSpec((1, 2, span, channels), lambda i, *_: (0, 0, i, 0)),
            scratch_shapes=[
                pltpu.VMEM((2 * levels, channels), BF16),
                pltpu.VMEM((levels, channels), BF16),
            ],
        ),
        name="row_radiance",
    )(row_counts, temps, absorb[None, :], peak_level[None, :], width[None, :])


def moved_coefficients(coefficients, legendre):
    waves, _, slots, _ = coefficients.shape
    first = lax.axis_index("spec") * slots
    spread = prior_spread(jnp.arange(waves, dtype=jnp.int32), first + jnp.arange(slots, dtype=jnp.int32), waves)
    scaled = coefficients.astype(F32) * spread[..., None]
    spectral = lax.all_to_all(scaled, "spec", split_axis=0, concat_axis=2, tiled=True)
    sums = jnp.einsum("mpsj,mpsc->mpjc", legendre, spectral, precision=PRECISE)
    sums = lax.all_to_all(sums, "spec", split_axis=2, concat_axis=0, tiled=True)
    return sums.reshape(2 * waves, sums.shape[-1])


def on_device(coefficients, legendre, row_counts, basis, absorb, peak_level, width):
    own, _, every, rows = legendre.shape
    waves, _, slots, columns = coefficients.shape
    n = waves // own
    fits = n == rows and n % 8 == 0 and LANES % n == 0 and every == n * slots and columns == LANES
    fits = fits and (LANES // n) % 8 == 0 and own % (LANES // n) == 0 and slots % 4 == 0 and waves % LANES == 0
    if fits and (slots * LANES // n) % 16 == 0 and 2 * waves >= 2 * slots * n:
        temps = exchanged_temps(coefficients, legendre, row_counts, basis, n, NLON)
    else:
        spectra = moved_coefficients(coefficients, legendre)
        temps = plain_temps(spectra, row_counts, basis, NLON)
    return radiate_row(temps, row_counts, absorb, peak_level, width)


def solution(mesh):
    placed = (
        P("draws", None, "spec", None),
        P("spec", None, None, None),
        P("spec"),
        P(),
        P(),
        P(),
        P(),
    )
    return jax.shard_map(
        on_device,
        mesh=mesh,
        in_specs=placed,
        out_specs=P(("draws", "spec"), None, None, None),
        check_vma=False,
    )
```

```python
import math

import jax
import jax.numpy as jnp
from jax import lax
from jax.experimental import pallas as pl
from jax.experimental.pallas import tpu as pltpu
from jax.sharding import PartitionSpec as P

NLON = 1280
FINE = 256
SPAN = 640
PARTS = 4
LANES = 128

PRECISE = lax.Precision.HIGHEST
F32 = jnp.float32
BF16 = jnp.bfloat16


def prior_spread(orders, slots, waves):
    parity = jnp.arange(2, dtype=jnp.int32)[None, :, None]
    degree = orders[:, None, None] + 2 * slots[None, None, :] + parity
    spread = lax.rsqrt((degree + 1).astype(F32) * waves)
    return jnp.where(degree < waves, spread, jnp.zeros_like(spread))


def split(x):
    high = x.astype(BF16)
    return high, (x - high.astype(F32)).astype(BF16)


def dot(a, b):
    return jnp.dot(a, b, preferred_element_type=F32)


def dot3(a, b):
    ah, al = split(a)
    bh, bl = split(b)
    return dot(ah, bh) + dot(al, bh) + dot(ah, bl)


def place_in_ring(n):
    me = lax.axis_index("spec")
    core = me % 2
    side = (me // 2) % 2
    layer = me // 4
    return me, core, side, layer


def fill_lookup(tile, count, fcos_ref, fsin_ref, high_ref, low_ref):
    points, lanes = fcos_ref.shape
    steps = high_ref.shape[1] // points
    tiny = 16
    middle = points // tiny
    coarse = -(-steps // 8) * 8
    whole = count.astype(F32)
    table = (tiny + middle + coarse, lanes)
    index = lax.broadcasted_iota(jnp.int32, table, 0)
    order = lax.broadcasted_iota(jnp.int32, table, 1) + tile * lanes
    places = jnp.where(index < tiny, index, (index - tiny) * tiny)
    places = jnp.where(index < tiny + middle, places, (index - tiny - middle) * points)
    phases = (places * order).astype(F32)
    phases = phases - jnp.floor(phases / whole) * whole
    angles = 2.0 * math.pi * phases / whole
    cosine, sine = jnp.cos(angles), jnp.sin(angles)
    weights = jnp.where(order == 0, 1.0, 2.0) * jnp.where(2 * order < count, 1.0, 0.0)
    first = tiny + middle
    base_c, base_s = (cosine * weights)[first:], (sine * weights)[first:]
    for b in range(middle):
        turn_c, turn_s = cosine[tiny + b:tiny + b + 1], sine[tiny + b:tiny + b + 1]
        fcos_ref[pl.ds(b * tiny, tiny), :] = cosine[:tiny] * turn_c - sine[:tiny] * turn_s
        fsin_ref[pl.ds(b * tiny, tiny), :] = sine[:tiny] * turn_c + cosine[:tiny] * turn_s
    fine_c, fine_s = fcos_ref[...], fsin_ref[...]
    for step in range(steps):
        turn_c, turn_s = base_c[step:step + 1], base_s[step:step + 1]
        lookup_c = turn_c * fine_c - turn_s * fine_s
        lookup_s = -(turn_s * fine_c + turn_c * fine_s)
        high, low = split(jnp.concatenate((lookup_c, lookup_s), axis=1))
        high_ref[tile, pl.ds(step * points, points), :] = high
        low_ref[tile, pl.ds(step * points, points), :] = low


def add_tile(tile, spectra_ref, basis_ref, high_ref, low_ref, temps_ref, after=None):
    lanes = LANES
    first = 2 * lanes * tile
    even = spectra_ref[pl.ds(first, lanes, stride=2), :]
    odd = spectra_ref[pl.ds(first + 1, lanes, stride=2), :]
    half = even.shape[1] // 2
    real = jnp.concatenate((even[:, :half], odd[:, :half]), axis=1)
    imag = jnp.concatenate((even[:, half:], odd[:, half:]), axis=1)
    basis = basis_ref[...]
    top = jnp.concatenate((basis, basis), axis=1)
    wide = jnp.concatenate((top, jnp.concatenate((basis, -basis), axis=1)), axis=0)
    high, low = split(dot3(jnp.concatenate((real, imag), axis=0), wide))
    for step in range(temps_ref.shape[0] // FINE):
        at = pl.ds(step * FINE, FINE)
        lookup_high = high_ref[tile, at, :]
        temps_ref[at, :] += dot(lookup_high, high) + (dot(low_ref[tile, at, :], high) + dot(lookup_high, low))
        if after is not None:
            after(step)


def exchange_kernel(
    n, waves, cut, count_ref, coef_hbm, leg_hbm, basis_hbm, out_hbm, temps_ref, coef_ref, leg_ref, basis_ref, turn_ref, raw_ref, send_ref, seed_ref, hold_ref,
    wide_ref, sums_ref, near_ref, side_ref, far_ref, up_ref, spectra_ref, fcos_ref, fsin_ref, high_ref, low_ref, coef_sem, leg_sem, basis_sem, out_sem, seed_send, seed_recv, hold_send, hold_recv,
    near_send, near_recv, side_send, side_recv, last_send, come_recv, far_send, up_recv, lone_send, lone_recv,
):
    me, core, side, layer = place_in_ring(n)
    layers = n // 4
    units = n * cut
    chip = me // 2
    rows = n
    columns = coef_hbm.shape[1]
    every = leg_ref.shape[1]
    slots = every // n
    lanes = LANES
    pairs = lanes // rows
    per = pairs // 2
    own = waves // n
    groups = own // (per * cut)
    depth = per * slots * 2
    part = groups * pairs
    room = seed_ref.shape[1] // (2 * cut)
    block = seed_ref.shape[1]
    partner = me + 1 - 2 * core
    across = me + 2 - 4 * side
    both = cut * (n - 2 * (2 * layer + 1))
    mine = cut * (n - 4 * layer)
    lag = 5

    def spot(z, y, c):
        return (z * 2 + y) * 2 + c

    def remote(src, dst, send_sem, recv_sem, target):
        return pltpu.make_async_remote_copy(
            src_ref=src, dst_ref=dst, send_sem=send_sem, recv_sem=recv_sem,
            device_id={"spec": target}, device_id_type=pl.DeviceIdType.MESH,
        )

    def seed_copy(source, target):
        return remote(send_ref.at[target], seed_ref.at[source], seed_send, seed_recv.at[source], target)

    def hold_copy(place, target):
        at = spot(layer, 1 - side, place)
        return remote(send_ref.at[target], hold_ref.at[core], seed_send, hold_recv.at[core], at)

    def hold_come(k):
        return remote(hold_ref.at[k], hold_ref.at[k], hold_send.at[k], hold_recv.at[k], across)

    def hold_pass(k):
        owner = spot(layer, 1 - side, k)
        return remote(hold_ref.at[k], seed_ref.at[owner], hold_send.at[k], seed_recv.at[owner], spot(0, side, core))

    def near_copy(q, t):
        ring = near_recv.shape[0]
        return remote(sums_ref.at[q, 1 - core], near_ref.at[q], near_send, near_recv.at[t % ring], partner)

    def side_copy(q, z, t):
        at = t % side_recv.shape[0]
        return remote(sums_ref.at[q, core, 1 - side, z], side_ref.at[q, z], side_send.at[0], side_recv.at[at], across)

    def side_come(q, t):
        return remote(rest_of(side_ref.at[q]), rest_of(side_ref.at[q]), side_send.at[0], side_recv.at[t % side_recv.shape[0]], across)

    def last_copy(q):
        return remote(
            sums_ref.at[q, core, 1 - side, layer], side_ref.at[q, layer], last_send.at[0], come_recv.at[q // cut], across
        )

    def lone(q):
        return q - both

    def lone_copy(q, z):
        return remote(
            sums_ref.at[q, core, 1 - side, z], side_ref.at[q, z], lone_send.at[lone(q)], lone_recv.at[lone(q)], across
        )

    def lone_part(q, pieces):
        part_ref = side_ref.at[q, pl.ds(0, pieces)]
        return remote(part_ref, part_ref, lone_send.at[lone(q)], lone_recv.at[lone(q)], across)

    def relayed(z, at):
        return z != at and at > 0

    def relays(at):
        return [z for z in range(layers) if relayed(z, at)]

    def rest_of(ref):
        return ref.at[pl.ds(0, layers - 1)]

    def far_copy(q, target):
        return remote(
            sums_ref.at[q, core, side, target], far_ref.at[layer, q],
            far_send.at[0], come_recv.at[q // cut], spot(target, side, core),
        )

    def come(c, pieces):
        arrived = far_ref.at[pl.ds(0, pieces), pl.ds(c * cut, cut)]
        return remote(arrived, arrived, far_send.at[0], come_recv.at[c], across)

    def up_copy(q, target):
        return remote(
            sums_ref.at[q, core, side, target], up_ref.at[q, target],
            far_send.at[0], up_recv.at[q], spot((layer + 1) % layers, side, core),
        )

    def up_come(q, lower):
        pieces = up_ref.at[q, pl.ds(lower + 1, layers - 1 - lower)]
        return remote(pieces, pieces, far_send.at[0], up_recv.at[q], across)

    def diag_copy(q, target):
        return remote(
            sums_ref.at[q, core, 1 - side, target], far_ref.at[layer, q],
            lone_send.at[lone(q)], come_recv.at[q // cut], spot(target, 1 - side, core),
        )

    def relay_copy(q, target):
        return remote(
            side_ref.at[q, target], far_ref.at[layer, q],
            lone_send.at[lone(q)], come_recv.at[q // cut], spot(target, side, core),
        )

    def signal(target):
        pl.semaphore_signal(barrier, inc=1, device_id={"spec": target}, device_id_type=pl.DeviceIdType.MESH)

    corners = [(dy, dc) for dy in range(2) for dc in range(2)]

    def corner(z, offset):
        dy, dc = offset
        return spot(z, (side + dy) % 2, (core + dc) % 2)

    pieces = coef_sem.shape[0]
    share = n // pieces

    def coef_copy(q):
        size = share * cut * groups * depth
        at = pl.ds(pl.multiple_of(q * size, size), size)
        return pltpu.make_async_copy(coef_hbm.at[at, :], coef_ref.at[at, :], coef_sem.at[q])

    barrier = pltpu.get_barrier_semaphore()
    for offset in corners[1:]:
        signal(corner(layer, offset))

    @pl.when(layer > 0)
    def _():
        for dz in range(1, layers - 1):
            for offset in corners:
                signal(corner(1 + (layer - 1 + dz) % (layers - 1), offset))

    leg_copy = pltpu.make_async_copy(leg_hbm, leg_ref, leg_sem)
    leg_copy.start()

    basis_copy = pltpu.make_async_copy(basis_hbm, basis_ref, basis_sem)
    basis_copy.start()

    def greet():
        pl.semaphore_wait(barrier, len(corners) - 1)
        for dz in range(1, layers):
            for offset in corners:
                signal(corner(dz, offset))

    @pl.when(jnp.logical_and(layer == 0, side == 1))
    def _():
        greet()

    row = lax.broadcasted_iota(jnp.int32, (lanes, lanes), 0)
    lane = lax.broadcasted_iota(jnp.int32, (lanes, lanes), 1)
    row_at = row % rows
    ordered = ((row_at % 2) * 2 + (row_at // 2) % 2) * layers + row_at // 4
    moves = jnp.where(ordered * pairs + row // rows == lane, 1.0, 0.0).astype(BF16)

    raw_ref[...] = jnp.zeros(raw_ref.shape, F32)
    leg_copy.wait()
    coef_copy(0).start()

    for g in range(cut * groups):
        at = (g // groups) * 2 * room + g % groups
        turn_ref[...] = jnp.transpose(leg_ref[pl.ds(g * lanes, lanes), :])
        raw_ref[pl.ds(at, n, stride=block), :] = turn_ref[pl.ds(0, n, stride=slots), :]
        raw_ref[pl.ds(at + room, n, stride=block), :] = turn_ref[pl.ds(1, n, stride=slots), :]
    start = jnp.broadcast_to(raw_ref[pl.ds(0, 1), :], (8, lanes))
    cosine = pltpu.roll(start, lanes - rows, 1) / start
    sine = pltpu.roll(start, lanes - 2 * rows, 1) / start
    sine = sine * sine * (2.0 / 3.0)
    square = jnp.where(sine < 0.5, 1.0 - sine, cosine * cosine * (1.0 / 3.0))
    square = jnp.where(lax.broadcasted_iota(jnp.int32, (8, lanes), 1) < rows, square, 0.0)
    shift = rows
    while shift < lanes:
        square = square + pltpu.roll(square, shift, 1)
        shift *= 2
    square = jnp.where(me == 0, square, 0.0)
    raw_ref[pl.ds(groups, n, stride=block), :] = jnp.broadcast_to(square[:1], (n, lanes))
    raw = raw_ref[...]
    high = raw.astype(BF16)
    rest = raw - high.astype(F32)
    middle = rest.astype(BF16)
    low = (rest - middle.astype(F32)).astype(BF16)
    send_ref[...] = (dot(high, moves) + (dot(middle, moves) + dot(low, moves))).reshape(send_ref.shape)
    seed_ref[me] = send_ref[me]

    def give_seeds(z, offset):
        target = corner(z, offset)

        @pl.when(me + target < n)
        def _():
            seed_copy(me, target).start()

    @pl.when(jnp.logical_and(layer == 0, side == 0))
    def _():
        greet()

    @pl.when(layer == 0)
    def _():
        for offset in corners[1:]:
            give_seeds(layer, offset)

    @pl.when(layer > 0)
    def _():
        pl.semaphore_wait(barrier, n - 1)
        for offset in corners:
            signal(corner(0, offset))
        for dy, dc in corners:
            target = spot(0, (side + dy) % 2, (core + dc) % 2)

            @pl.when(me + target < n)
            def _():
                if dy:
                    hold_copy((core + dc) % 2, target).start()
                else:
                    seed_copy(me, target).start()

        for offset in corners[1:]:
            give_seeds(layer, offset)
        for dz in range(1, layers - 1):
            for offset in corners:
                give_seeds(1 + (layer - 1 + dz) % (layers - 1), offset)
        for k in range(2):
            @pl.when(spot(layer, 1 - side, k) + spot(0, side, core) < n)
            def _():
                hold_come(k).wait_recv()
                hold_pass(k).start()

    for q in range(1, pieces):
        @pl.when(me + q * share < n)
        def _():
            coef_copy(q).start()

    tiles = waves // lanes

    def fill(tile):
        fill_lookup(tile, count_ref[0], fcos_ref, fsin_ref, high_ref, low_ref)

    @pl.when(layer > 0)
    def _():
        @pl.loop(0, tiles)
        def _(tile):
            fill(tile)

    def meet():
        @pl.when(layer == 0)
        def _():
            pl.semaphore_wait(barrier, n - len(corners))
            for dz in range(1, layers):
                for offset in corners:
                    give_seeds(dz, offset)

    expand_row = lax.broadcasted_iota(jnp.int32, (depth, lanes), 0)
    expand_lane = lax.broadcasted_iota(jnp.int32, (depth, lanes), 1) % pairs
    keep = (expand_row // (2 * slots)) * 2 + expand_row % 2 == expand_lane
    pair_at = lax.broadcasted_iota(jnp.int32, (room, lanes), 1) % pairs
    order_part = lax.broadcasted_iota(jnp.int32, (room, lanes), 0) * per + pair_at // 2

    def recur(u):
        owner = u // cut
        at = pl.multiple_of((u % cut) * (2 * room), 2 * room)
        order = order_part + u * (groups * per)
        first = order + pair_at % 2 + me * (2 * slots)
        m = order.astype(F32)
        square = seed_ref[0, pl.ds(groups, 1), :]

        def coupling(d):
            return ((d - m) * (d + m)) / ((2.0 * d - 1.0) * (2.0 * d + 1.0))

        def place(s, value):
            degree = first + 2 * s
            spread = lax.rsqrt((degree + 1).astype(F32) * float(waves))
            value = value * jnp.where(degree < waves, spread, 0.0)
            wide_ref[pl.ds(2 * s, room, stride=2 * slots), :] = value
            wide_ref[pl.ds(2 * s + 1, room, stride=2 * slots), :] = value

        before = seed_ref[owner, pl.ds(at, room), :]
        now = seed_ref[owner, pl.ds(at + room, room), :]
        place(0, before)
        place(1, now)
        degree = first.astype(F32)
        last = coupling(degree + 2.0)
        weight = jnp.sqrt(coupling(degree + 1.0) * last)
        for s in range(1, slots - 1):
            degree = degree + 2.0
            one, two = coupling(degree + 1.0), coupling(degree + 2.0)
            product = one * two
            inverse = lax.rsqrt(product)
            before, now = now, ((square - (one + last)) * now - weight * before) * inverse
            weight = product * inverse
            last = two
            place(s + 1, now)

    def partial(u):
        owner = u // cut

        @pl.when(me + owner < n)
        def _():
            @pl.when(u % cut == 0)
            def _():
                @pl.when(owner % share == 0)
                def _():
                    coef_copy(owner // share).wait()

                @pl.when(owner != me)
                def _():
                    seed_copy(owner, me).wait_recv()

            recur(u)
            for g in range(groups):
                at = u * groups + g
                values = coef_ref[pl.ds(pl.multiple_of(at * depth, depth), depth), :]
                one = wide_ref[pl.ds(g * 2 * slots, 2 * slots), :]
                tiled = jnp.where(keep, jnp.concatenate([one] * per, axis=0), 0.0)
                both = jnp.concatenate(split(tiled), axis=1)
                sums = lax.dot_general(both, values, (((0,), (0,)), ((), ())), preferred_element_type=F32)
                sums = (sums[:lanes] + sums[lanes:]).reshape(2, 2, layers, pairs, columns)
                sums_ref[u, :, :, :, pl.ds(g * pairs, pairs), :] = sums

        @pl.when(me + owner >= n)
        def _():
            sums_ref[u] = jnp.zeros((2, 2, layers, part, columns), F32)

    def held(q, place):
        return q // cut + 2 * place < n

    def compute(q, t):
        @pl.when(held(q, chip))
        def _():
            partial(q)

            near_copy(q, t).start()

    def merge_near(q, t):
        shared = held(q, across // 2)

        @pl.when(held(q, chip))
        def _():
            near_copy(q, t).wait_recv()

            for y in (0, 1):
                @pl.loop(0, layers)
                def _(z):
                    sums_ref[q, core, y, z] += near_ref[q, y, z]

            @pl.when(shared)
            def _():
                for dz in reversed(range(1, layers)):
                    side_copy(q, (layer + dz) % layers, t).start()

            @pl.when(jnp.logical_not(shared))
            def _():
                for at in range(1, layers):
                    @pl.when(layer == at)
                    def _():
                        for z in relays(at):
                            lone_copy(q, z).start()

                last_copy(q).start()

    def pass_on(q, t):
        shared = held(q, across // 2)

        @pl.when(held(q, chip))
        def _():
            @pl.when(shared)
            def _():
                side_come(q, t).wait_recv()

            for lower in range(1, layers - 1):
                @pl.when(layer == lower)
                def _():
                    up_come(q, lower).wait_recv()

            for dz in reversed(range(1, layers)):
                z = (layer + dz) % layers
                upward = jnp.logical_and(z > layer + 1, held(q, chip + 2))

                @pl.when(shared)
                def _():
                    sums_ref[q, core, side, z] += side_ref[q, z]

                @pl.when(jnp.logical_and(layer > 0, z > layer))
                def _():
                    sums_ref[q, core, side, z] += up_ref[q, z]

                @pl.when(upward)
                def _():
                    up_copy(q, z).start()

                @pl.when(jnp.logical_not(upward))
                def _():
                    far_copy(q, z).start()

            for at in range(layers - 1):
                straight = [z for z in reversed(range(at + 1, layers)) if not relayed(z, at)]
                if straight:
                    @pl.when(jnp.logical_and(jnp.logical_not(shared), layer == at))
                    def _():
                        for z in straight:
                            diag_copy(q, z).start()

        @pl.when(jnp.logical_and(jnp.logical_not(held(q, chip)), jnp.logical_and(shared, layer > 0)))
        def _():
            for lower in range(1, layers):
                @pl.when(layer == lower)
                def _():
                    lone_part(q, len(relays(lower))).wait_recv()
                    for z in relays(lower):
                        relay_copy(q, z).start()

    def unit_at(t):
        turn = n // 2
        block_at, place = t // turn, t % turn
        early = jnp.where(place == turn - 1, both + block_at, block_at * (turn - 1) + place)
        late = jnp.where(t < both + 2, t - 2, t)
        return jnp.where(layer == 0, jnp.where(t < 2 * turn, early, late), t)

    def finish(c):
        near_part = held(c * cut, chip)

        pieces = jnp.where(held(c * cut, across // 2), 1, 0)
        for dz in range(1, layers):
            source = (layer + dz) % layers
            passed = jnp.logical_and(source + 1 < layer, held(c * cut, 2 * (source + 1) + side))
            sends = jnp.logical_and(held(c * cut, 2 * source), jnp.logical_not(passed))
            pieces = pieces + jnp.where(sends, 1, 0)
        for number in range(1, layers + 1):
            @pl.when(pieces == number)
            def _():
                come(c, number).wait_recv()

        for half in range(cut):
            q = c * cut + half
            at = pl.ds(pl.multiple_of(q * part, part), part)

            @pl.when(near_part)
            def _():
                spectra_ref[at, :] = sums_ref[q, core, side, layer]

            @pl.when(jnp.logical_not(near_part))
            def _():
                spectra_ref[at, :] = jnp.zeros((part, columns), F32)

            for dz in range(1, layers):
                source = (layer + dz) % layers
                passed = jnp.logical_and(source + 1 < layer, held(q, 2 * (source + 1) + side))

                @pl.when(jnp.logical_and(held(q, 2 * source), jnp.logical_not(passed)))
                def _():
                    spectra_ref[at, :] += far_ref[source, q]

            @pl.when(held(q, across // 2))
            def _():
                spectra_ref[at, :] += side_ref[q, layer]

    temps_ref[...] = jnp.zeros(temps_ref.shape, F32)
    basis_copy.wait()
    early = jnp.logical_and(layer == 1, side == 0)

    def out_copy(step):
        at = pl.ds(step * FINE, FINE)
        return pltpu.make_async_copy(temps_ref.at[at, :], out_hbm.at[at, :], out_sem)

    def drain():
        for place in range(n // 2):
            count = cut * (n - 2 * place)
            pair = cut * (n - 2 * (place // 2 * 2 + 1))

            @pl.when(chip == place)
            def _():
                near = near_ref.at[pl.ds(0, count)]
                remote(near, near, near_send, near_recv.at[0], across).wait_send()
                side = side_ref.at[pl.ds(0, pair), pl.ds(0, layers - 1)]
                remote(side, side, side_send.at[0], side_recv.at[0], across).wait_send()
                last = side_ref.at[pl.ds(0, count), 0]
                remote(last, last, last_send.at[0], come_recv.at[0], across).wait_send()
                far = far_ref.at[pl.ds(0, layers - 1), pl.ds(0, count)]
                remote(far, far, far_send.at[0], come_recv.at[0], across).wait_send()

        for lower in range(layers):
            @pl.when(jnp.logical_and(layer == lower, side == 0))
            def _():
                for k in range(lone_send.shape[0]):
                    lone_part(both + k, layers - 1).wait_send()

            if lower:
                @pl.when(jnp.logical_and(layer == lower, side == 1))
                def _():
                    for k in range(lone_send.shape[0]):
                        lone_part(both + k, len(relays(lower))).wait_send()

    def stage(tile, after=None):
        @pl.loop((tile * lanes + own - 1) // own, ((tile + 1) * lanes + own - 1) // own)
        def _(c):
            finish(c)

        if after is not None:
            @pl.when(layer > 0)
            def _():
                drain()

        add_tile(tile, spectra_ref, basis_ref, high_ref, low_ref, temps_ref, after)

    @pl.loop(0, units + lag)
    def _(t):
        @pl.when(t == lag - 1)
        def _():
            meet()

        @pl.when(jnp.logical_and(layer == 0, jnp.logical_and(t >= 2 * lag, t < 2 * (lag + tiles))))
        def _():
            @pl.when(t % 2 == 0)
            def _():
                fill(t // 2 - lag)

        @pl.when(t < units)
        def _():
            compute(unit_at(t), t)

        @pl.when(jnp.logical_and(t >= 1, t <= units))
        def _():
            merge_near(unit_at(t - 1), t - 1)

        @pl.when(t == mine)
        def _():
            @pl.loop(0, both)
            def _(q):
                last_copy(q).start()

        @pl.when(jnp.logical_and(early, t == mine + 1))
        def _():
            stage(0)

        @pl.when(t >= lag)
        def _():
            pass_on(unit_at(t - lag), t - lag)

    for number in range(1, n):
        @pl.when(jnp.where(2 * me < n, n - me - 1, n - me) == number)
        def _():
            gone = send_ref.at[pl.ds(0, number)]
            remote(gone, gone, seed_send, seed_recv.at[0], across).wait_send()

    for k in range(2):
        @pl.when(jnp.logical_and(layer > 0, spot(layer, 1 - side, k) + spot(0, side, core) < n))
        def _():
            hold_pass(k).wait_send()

    @pl.loop(jnp.where(early, 1, 0), tiles - 1)
    def _(tile):
        stage(tile)

    stage(tiles - 1, lambda step: out_copy(step).start())

    @pl.when(layer == 0)
    def _():
        drain()

    pltpu.make_async_copy(temps_ref, out_hbm, out_sem).wait()


def exchanged_temps(coefficients, legendre, row_counts, basis, n, points):
    waves, _, slots, columns = coefficients.shape
    own, _, every, rows = legendre.shape
    dense = jnp.transpose(coefficients, (0, 2, 1, 3)).reshape(waves * slots * 2, columns)
    legs = jnp.transpose(legendre, (0, 1, 3, 2)).reshape(own * 2 * rows, every)
    layers = n // 4
    pairs = LANES // rows
    groups = own * 2 // pairs
    cut = 2 if groups % 2 == 0 else 1
    units = n * cut
    width = groups // cut * pairs
    room = -(-(groups // cut + 1) // 8) * 8
    block = cut * 2 * room
    dma = pltpu.SemaphoreType.DMA

    def body(*refs):
        exchange_kernel(n, waves, cut, *refs)

    return pl.pallas_call(
        body,
        out_shape=jax.ShapeDtypeStruct((points, 2 * basis.shape[1]), F32),
        in_specs=[pl.BlockSpec(memory_space=pltpu.SMEM)] + [pl.BlockSpec(memory_space=pl.ANY)] * 3,
        out_specs=pl.BlockSpec(memory_space=pl.ANY),
        scratch_shapes=[
            pltpu.VMEM((points, 2 * basis.shape[1]), F32),
            pltpu.VMEM(dense.shape, BF16),
            pltpu.VMEM(legs.shape, F32),
            pltpu.VMEM(basis.shape, F32),
            pltpu.VMEM((every, LANES), F32),
            pltpu.VMEM((n * block, LANES), F32),
            pltpu.VMEM((n, block, LANES), F32),
            pltpu.VMEM((n, block, LANES), F32),
            pltpu.VMEM((2, block, LANES), F32),
            pltpu.VMEM((room * 2 * slots, LANES), F32),
            pltpu.VMEM((units, 2, 2, layers, width, columns), F32),
            pltpu.VMEM((units, 2, layers, width, columns), F32),
            pltpu.VMEM((units, layers, width, columns), F32),
            pltpu.VMEM((layers, units, width, columns), F32),
            pltpu.VMEM((units, layers, width, columns), F32),
            pltpu.VMEM((2 * waves, columns), F32),
            pltpu.VMEM((FINE, LANES), F32),
            pltpu.VMEM((FINE, LANES), F32),
            pltpu.VMEM((waves // LANES, points, 2 * LANES), BF16),
            pltpu.VMEM((waves // LANES, points, 2 * LANES), BF16),
            dma((n // 2,)), dma, dma, dma, dma, dma((n,)), dma((2,)), dma((2,)),
            dma, dma((8,)),
            dma((1,)), dma((12,)),
            dma((1,)), dma((n,)),
            dma((1,)), dma((units - 4 * cut,)), dma((2 * cut,)), dma((2 * cut,)),
        ],
        compiler_params=pltpu.CompilerParams(
            collective_id=0, has_side_effects=True, vmem_limit_bytes=58 * 1024 * 1024
        ),
        name="exchanged_temps",
    )(row_counts, dense, legs, basis)


def plain_temps(spectra, row_counts, basis, points):
    tiles = spectra.shape[0] // (2 * LANES)

    def body(count_ref, spectra_ref, basis_ref, temps_ref, fcos_ref, fsin_ref, high_ref, low_ref):
        temps_ref[...] = jnp.zeros(temps_ref.shape, F32)
        for tile in range(tiles):
            fill_lookup(tile, count_ref[0], fcos_ref, fsin_ref, high_ref, low_ref)
            add_tile(tile, spectra_ref, basis_ref, high_ref, low_ref, temps_ref)

    vmem = pl.BlockSpec(memory_space=pltpu.VMEM)
    return pl.pallas_call(
        body,
        out_shape=jax.ShapeDtypeStruct((points, 2 * basis.shape[1]), F32),
        in_specs=[pl.BlockSpec(memory_space=pltpu.SMEM), vmem, vmem],
        out_specs=vmem,
        scratch_shapes=[pltpu.VMEM((FINE, LANES), F32)] * 2 + [pltpu.VMEM((tiles, points, 2 * LANES), BF16)] * 2,
        name="plain_temps",
    )(row_counts, spectra, basis)


def row_kernel(
    count_ref, temps_hbm, absorb_ref, peak_ref, width_ref, out_hbm, temps_ref, out_ref, pair_ref, rhigh_ref, rlow_ref,
    temps_sem, out_sem,
):
    levels = absorb_ref.shape[1]
    points = temps_ref.shape[0]
    chunk = pair_ref.shape[0] // 2
    steps = points // chunk
    piece = chunk // PARTS

    def come(step):
        at = pl.ds(pl.multiple_of(step * chunk, chunk), chunk)
        return pltpu.make_async_copy(temps_hbm.at[at, :], temps_ref.at[at, :], temps_sem.at[step])

    for step in range(steps):
        come(step).start()
    height = lax.broadcasted_iota(jnp.int32, rlow_ref.shape, 0)
    offsets = (height - peak_ref[...]).astype(F32) / width_ref[...]
    shape = jnp.exp(-offsets * offsets)
    high, low = split(shape / jnp.sum(shape, axis=0, keepdims=True))
    rhigh_ref[pl.ds(0, levels), :] = high
    rhigh_ref[pl.ds(levels, levels), :] = high
    rlow_ref[...] = low

    @pl.loop(0, steps)
    def _(step):
        come(step).wait()
        first = pl.multiple_of(step * chunk, chunk)
        temps = temps_ref[pl.ds(first, chunk), :]
        temps = jnp.concatenate((temps[:, :levels], temps[:, levels:]), axis=0)
        source = jnp.exp(0.5 * temps)
        layers = absorb_ref[...] * source
        before = lax.broadcasted_iota(jnp.int32, (2 * levels, levels), 0) % levels
        after = lax.broadcasted_iota(jnp.int32, (2 * levels, levels), 1)
        upper = jnp.where(before < after, 1.0, 0.0).astype(BF16)
        layers_high, layers_low = split(layers)
        above = dot(jnp.concatenate((layers_high, layers_low), axis=1), upper)
        emitted = source * jnp.exp(-above) * (1.0 - jnp.exp(-layers))
        place = first + lax.broadcasted_iota(jnp.int32, (2 * chunk, levels), 0) % chunk
        emitted = jnp.where(place < count_ref[0], emitted, 0.0)
        pair_ref[...] = jnp.concatenate(split(emitted), axis=1)
        for half in range(2):
            for part in range(PARTS):
                pair = pair_ref[pl.ds(half * chunk + part * piece, piece), :]
                bright = dot(pair, rhigh_ref[...]) + dot(pair[:, :levels], rlow_ref[...])
                at = pl.ds(pl.multiple_of(first + part * piece, piece), piece)
                out_ref[0, half, at, :] = bright
                pltpu.make_async_copy(out_ref.at[0, half, at, :], out_hbm.at[0, half, at, :], out_sem).start()

    pltpu.make_async_copy(out_ref, out_hbm, out_sem).wait()


def radiate_row(temps, row_counts, absorb, peak_level, width):
    points = temps.shape[0]
    levels, channels = absorb.shape[0], width.shape[0]
    span = SPAN if points % SPAN == 0 else FINE
    vmem = pl.BlockSpec(memory_space=pltpu.VMEM)
    return pl.pallas_call(
        row_kernel,
        out_shape=jax.ShapeDtypeStruct((1, 2, points, channels), F32),
        in_specs=[pl.BlockSpec(memory_space=pltpu.SMEM), pl.BlockSpec(memory_space=pl.ANY), vmem, vmem, vmem],
        out_specs=pl.BlockSpec(memory_space=pl.ANY),
        scratch_shapes=[
            pltpu.VMEM(temps.shape, F32),
            pltpu.VMEM((1, 2, points, channels), F32),
            pltpu.VMEM((2 * span, 2 * levels), BF16),
            pltpu.VMEM((2 * levels, channels), BF16),
            pltpu.VMEM((levels, channels), BF16),
            pltpu.SemaphoreType.DMA((points // span,)),
            pltpu.SemaphoreType.DMA,
        ],
        name="row_radiance",
    )(row_counts, temps, absorb[None, :], peak_level[None, :], width[None, :])


def moved_coefficients(coefficients, legendre):
    waves, _, slots, _ = coefficients.shape
    first = lax.axis_index("spec") * slots
    spread = prior_spread(jnp.arange(waves, dtype=jnp.int32), first + jnp.arange(slots, dtype=jnp.int32), waves)
    scaled = coefficients.astype(F32) * spread[..., None]
    spectral = lax.all_to_all(scaled, "spec", split_axis=0, concat_axis=2, tiled=True)
    sums = jnp.einsum("mpsj,mpsc->mpjc", legendre, spectral, precision=PRECISE)
    sums = lax.all_to_all(sums, "spec", split_axis=2, concat_axis=0, tiled=True)
    return sums.reshape(2 * waves, sums.shape[-1])


def on_device(coefficients, legendre, row_counts, basis, absorb, peak_level, width):
    own, _, every, rows = legendre.shape
    waves, _, slots, columns = coefficients.shape
    n = waves // own
    fits = n == rows and n % 8 == 0 and LANES % n == 0 and every == n * slots and columns == LANES
    fits = fits and (LANES // n) % 8 == 0 and own % (LANES // n) == 0 and slots % 4 == 0 and waves % LANES == 0
    if fits and (slots * LANES // n) % 16 == 0 and 2 * waves >= 2 * slots * n:
        temps = exchanged_temps(coefficients, legendre, row_counts, basis, n, NLON)
    else:
        spectra = moved_coefficients(coefficients, legendre)
        temps = plain_temps(spectra, row_counts, basis, NLON)
    return radiate_row(temps, row_counts, absorb, peak_level, width)


def solution(mesh):
    placed = (
        P("draws", None, "spec", None),
        P("spec", None, None, None),
        P("spec"),
        P(),
        P(),
        P(),
        P(),
    )
    return jax.shard_map(
        on_device,
        mesh=mesh,
        in_specs=placed,
        out_specs=P(("draws", "spec"), None, None, None),
        check_vma=False,
    )
```

```python
import math

import jax
import jax.numpy as jnp
from jax import lax
from jax.experimental import pallas as pl
from jax.experimental.pallas import tpu as pltpu
from jax.sharding import PartitionSpec as P

NLON = 1280
FINE = 256
SPAN = 640
PARTS = 4
LANES = 128

PRECISE = lax.Precision.HIGHEST
F32 = jnp.float32
BF16 = jnp.bfloat16


def prior_spread(orders, slots, waves):
    parity = jnp.arange(2, dtype=jnp.int32)[None, :, None]
    degree = orders[:, None, None] + 2 * slots[None, None, :] + parity
    spread = lax.rsqrt((degree + 1).astype(F32) * waves)
    return jnp.where(degree < waves, spread, jnp.zeros_like(spread))


def split(x):
    high = x.astype(BF16)
    return high, (x - high.astype(F32)).astype(BF16)


def dot(a, b):
    return jnp.dot(a, b, preferred_element_type=F32)


def dot3(a, b):
    ah, al = split(a)
    bh, bl = split(b)
    return dot(ah, bh) + dot(al, bh) + dot(ah, bl)


def place_in_ring(n):
    me = lax.axis_index("spec")
    core = me % 2
    side = (me // 2) % 2
    layer = me // 4
    return me, core, side, layer


def fill_lookup(tile, count, fcos_ref, fsin_ref, high_ref, low_ref):
    points, lanes = fcos_ref.shape
    steps = high_ref.shape[1] // points
    tiny = 16
    middle = points // tiny
    coarse = -(-steps // 8) * 8
    whole = count.astype(F32)
    table = (tiny + middle + coarse, lanes)
    index = lax.broadcasted_iota(jnp.int32, table, 0)
    order = lax.broadcasted_iota(jnp.int32, table, 1) + tile * lanes
    places = jnp.where(index < tiny, index, (index - tiny) * tiny)
    places = jnp.where(index < tiny + middle, places, (index - tiny - middle) * points)
    phases = (places * order).astype(F32)
    phases = phases - jnp.floor(phases / whole) * whole
    angles = 2.0 * math.pi * phases / whole
    cosine, sine = jnp.cos(angles), jnp.sin(angles)
    weights = jnp.where(order == 0, 1.0, 2.0) * jnp.where(2 * order < count, 1.0, 0.0)
    first = tiny + middle
    base_c, base_s = (cosine * weights)[first:], (sine * weights)[first:]
    for b in range(middle):
        turn_c, turn_s = cosine[tiny + b:tiny + b + 1], sine[tiny + b:tiny + b + 1]
        fcos_ref[pl.ds(b * tiny, tiny), :] = cosine[:tiny] * turn_c - sine[:tiny] * turn_s
        fsin_ref[pl.ds(b * tiny, tiny), :] = sine[:tiny] * turn_c + cosine[:tiny] * turn_s
    fine_c, fine_s = fcos_ref[...], fsin_ref[...]
    for step in range(steps):
        turn_c, turn_s = base_c[step:step + 1], base_s[step:step + 1]
        lookup_c = turn_c * fine_c - turn_s * fine_s
        lookup_s = -(turn_s * fine_c + turn_c * fine_s)
        high, low = split(jnp.concatenate((lookup_c, lookup_s), axis=1))
        high_ref[tile, pl.ds(step * points, points), :] = high
        low_ref[tile, pl.ds(step * points, points), :] = low


def add_tile(tile, spectra_ref, basis_ref, high_ref, low_ref, temps_ref, after=None):
    lanes = LANES
    first = 2 * lanes * tile
    even = spectra_ref[pl.ds(first, lanes, stride=2), :]
    odd = spectra_ref[pl.ds(first + 1, lanes, stride=2), :]
    half = even.shape[1] // 2
    real = jnp.concatenate((even[:, :half], odd[:, :half]), axis=1)
    imag = jnp.concatenate((even[:, half:], odd[:, half:]), axis=1)
    basis = basis_ref[...]
    top = jnp.concatenate((basis, basis), axis=1)
    wide = jnp.concatenate((top, jnp.concatenate((basis, -basis), axis=1)), axis=0)
    high, low = split(dot3(jnp.concatenate((real, imag), axis=0), wide))
    for step in range(temps_ref.shape[0] // FINE):
        at = pl.ds(step * FINE, FINE)
        lookup_high = high_ref[tile, at, :]
        temps_ref[at, :] += dot(lookup_high, high) + (dot(low_ref[tile, at, :], high) + dot(lookup_high, low))
        if after is not None:
            after(step)


def exchange_kernel(
    n, waves, cut, count_ref, coef_hbm, leg_hbm, basis_hbm, out_hbm, temps_ref, coef_ref, leg_ref, basis_ref, turn_ref, raw_ref, send_ref, seed_ref, hold_ref,
    wide_ref, sums_ref, near_ref, side_ref, far_ref, up_ref, spectra_ref, fcos_ref, fsin_ref, high_ref, low_ref, coef_sem, leg_sem, basis_sem, out_sem, seed_send, seed_recv, hold_send, hold_recv,
    near_send, near_recv, side_send, side_recv, last_send, come_recv, far_send, up_recv, lone_send, lone_recv,
):
    me, core, side, layer = place_in_ring(n)
    layers = n // 4
    units = n * cut
    chip = me // 2
    rows = n
    columns = coef_hbm.shape[1]
    every = leg_ref.shape[1]
    slots = every // n
    lanes = LANES
    pairs = lanes // rows
    per = pairs // 2
    own = waves // n
    groups = own // (per * cut)
    depth = per * slots * 2
    part = groups * pairs
    room = seed_ref.shape[1] // (2 * cut)
    block = seed_ref.shape[1]
    partner = me + 1 - 2 * core
    across = me + 2 - 4 * side
    both = cut * (n - 2 * (2 * layer + 1))
    mine = cut * (n - 4 * layer)
    lag = 6

    def spot(z, y, c):
        return (z * 2 + y) * 2 + c

    def remote(src, dst, send_sem, recv_sem, target):
        return pltpu.make_async_remote_copy(
            src_ref=src, dst_ref=dst, send_sem=send_sem, recv_sem=recv_sem,
            device_id={"spec": target}, device_id_type=pl.DeviceIdType.MESH,
        )

    def seed_copy(source, target):
        return remote(send_ref.at[target], seed_ref.at[source], seed_send, seed_recv.at[source], target)

    def hold_copy(place, target):
        at = spot(layer, 1 - side, place)
        return remote(send_ref.at[target], hold_ref.at[core], seed_send, hold_recv.at[core], at)

    def hold_come(k):
        return remote(hold_ref.at[k], hold_ref.at[k], hold_send.at[k], hold_recv.at[k], across)

    def hold_pass(k):
        owner = spot(layer, 1 - side, k)
        return remote(hold_ref.at[k], seed_ref.at[owner], hold_send.at[k], seed_recv.at[owner], spot(0, side, core))

    def near_copy(q, t):
        ring = near_recv.shape[0]
        return remote(sums_ref.at[q, 1 - core], near_ref.at[q], near_send, near_recv.at[t % ring], partner)

    def side_copy(q, z, t):
        at = t % side_recv.shape[0]
        return remote(sums_ref.at[q, core, 1 - side, z], side_ref.at[q, z], side_send.at[0], side_recv.at[at], across)

    def side_come(q, t):
        return remote(rest_of(side_ref.at[q]), rest_of(side_ref.at[q]), side_send.at[0], side_recv.at[t % side_recv.shape[0]], across)

    def last_copy(q):
        return remote(
            sums_ref.at[q, core, 1 - side, layer], side_ref.at[q, layer], last_send.at[0], come_recv.at[q // cut], across
        )

    def lone(q):
        return q - both

    def lone_copy(q, z):
        return remote(
            sums_ref.at[q, core, 1 - side, z], side_ref.at[q, z], lone_send.at[lone(q)], lone_recv.at[lone(q)], across
        )

    def lone_part(q, pieces):
        part_ref = side_ref.at[q, pl.ds(0, pieces)]
        return remote(part_ref, part_ref, lone_send.at[lone(q)], lone_recv.at[lone(q)], across)

    def relayed(z, at):
        return z != at and at > 0

    def relays(at):
        return [z for z in range(layers) if relayed(z, at)]

    def rest_of(ref):
        return ref.at[pl.ds(0, layers - 1)]

    def far_copy(q, target):
        return remote(
            sums_ref.at[q, core, side, target], far_ref.at[layer, q],
            far_send.at[0], come_recv.at[q // cut], spot(target, side, core),
        )

    def come(c, pieces):
        arrived = far_ref.at[pl.ds(0, pieces), pl.ds(c * cut, cut)]
        return remote(arrived, arrived, far_send.at[0], come_recv.at[c], across)

    def up_copy(q, target):
        return remote(
            sums_ref.at[q, core, side, target], up_ref.at[q, target],
            far_send.at[0], up_recv.at[q], spot((layer + 1) % layers, side, core),
        )

    def up_come(q, lower):
        pieces = up_ref.at[q, pl.ds(lower + 1, layers - 1 - lower)]
        return remote(pieces, pieces, far_send.at[0], up_recv.at[q], across)

    def diag_copy(q, target):
        return remote(
            sums_ref.at[q, core, 1 - side, target], far_ref.at[layer, q],
            lone_send.at[lone(q)], come_recv.at[q // cut], spot(target, 1 - side, core),
        )

    def relay_copy(q, target):
        return remote(
            side_ref.at[q, target], far_ref.at[layer, q],
            lone_send.at[lone(q)], come_recv.at[q // cut], spot(target, side, core),
        )

    def signal(target):
        pl.semaphore_signal(barrier, inc=1, device_id={"spec": target}, device_id_type=pl.DeviceIdType.MESH)

    corners = [(dy, dc) for dy in range(2) for dc in range(2)]

    def corner(z, offset):
        dy, dc = offset
        return spot(z, (side + dy) % 2, (core + dc) % 2)

    pieces = coef_sem.shape[0]
    share = n // pieces

    def coef_copy(q):
        size = share * cut * groups * depth
        at = pl.ds(pl.multiple_of(q * size, size), size)
        return pltpu.make_async_copy(coef_hbm.at[at, :], coef_ref.at[at, :], coef_sem.at[q])

    barrier = pltpu.get_barrier_semaphore()
    for offset in corners[1:]:
        signal(corner(layer, offset))

    @pl.when(layer > 0)
    def _():
        for dz in range(1, layers - 1):
            for offset in corners:
                signal(corner(1 + (layer - 1 + dz) % (layers - 1), offset))

    leg_copy = pltpu.make_async_copy(leg_hbm, leg_ref, leg_sem)
    leg_copy.start()

    basis_copy = pltpu.make_async_copy(basis_hbm, basis_ref, basis_sem)
    basis_copy.start()

    def greet():
        pl.semaphore_wait(barrier, len(corners) - 1)
        for dz in range(1, layers):
            for offset in corners:
                signal(corner(dz, offset))

    @pl.when(jnp.logical_and(layer == 0, side == 1))
    def _():
        greet()

    row = lax.broadcasted_iota(jnp.int32, (lanes, lanes), 0)
    lane = lax.broadcasted_iota(jnp.int32, (lanes, lanes), 1)
    row_at = row % rows
    ordered = ((row_at % 2) * 2 + (row_at // 2) % 2) * layers + row_at // 4
    moves = jnp.where(ordered * pairs + row // rows == lane, 1.0, 0.0).astype(BF16)

    raw_ref[...] = jnp.zeros(raw_ref.shape, F32)
    leg_copy.wait()
    coef_copy(0).start()

    for g in range(cut * groups):
        at = (g // groups) * 2 * room + g % groups
        turn_ref[...] = jnp.transpose(leg_ref[pl.ds(g * lanes, lanes), :])
        raw_ref[pl.ds(at, n, stride=block), :] = turn_ref[pl.ds(0, n, stride=slots), :]
        raw_ref[pl.ds(at + room, n, stride=block), :] = turn_ref[pl.ds(1, n, stride=slots), :]
    start = jnp.broadcast_to(raw_ref[pl.ds(0, 1), :], (8, lanes))
    cosine = pltpu.roll(start, lanes - rows, 1) / start
    sine = pltpu.roll(start, lanes - 2 * rows, 1) / start
    sine = sine * sine * (2.0 / 3.0)
    square = jnp.where(sine < 0.5, 1.0 - sine, cosine * cosine * (1.0 / 3.0))
    square = jnp.where(lax.broadcasted_iota(jnp.int32, (8, lanes), 1) < rows, square, 0.0)
    shift = rows
    while shift < lanes:
        square = square + pltpu.roll(square, shift, 1)
        shift *= 2
    square = jnp.where(me == 0, square, 0.0)
    raw_ref[pl.ds(groups, n, stride=block), :] = jnp.broadcast_to(square[:1], (n, lanes))
    raw = raw_ref[...]
    high = raw.astype(BF16)
    rest = raw - high.astype(F32)
    middle = rest.astype(BF16)
    low = (rest - middle.astype(F32)).astype(BF16)
    send_ref[...] = (dot(high, moves) + (dot(middle, moves) + dot(low, moves))).reshape(send_ref.shape)
    seed_ref[me] = send_ref[me]

    def give_seeds(z, offset):
        target = corner(z, offset)

        @pl.when(me + target < n)
        def _():
            seed_copy(me, target).start()

    @pl.when(jnp.logical_and(layer == 0, side == 0))
    def _():
        greet()

    @pl.when(layer == 0)
    def _():
        for offset in corners[1:]:
            give_seeds(layer, offset)

    @pl.when(layer > 0)
    def _():
        pl.semaphore_wait(barrier, n - 1)
        for offset in corners:
            signal(corner(0, offset))
        for dy, dc in corners:
            target = spot(0, (side + dy) % 2, (core + dc) % 2)

            @pl.when(me + target < n)
            def _():
                if dy:
                    hold_copy((core + dc) % 2, target).start()
                else:
                    seed_copy(me, target).start()

        for offset in corners[1:]:
            give_seeds(layer, offset)
        for dz in range(1, layers - 1):
            for offset in corners:
                give_seeds(1 + (layer - 1 + dz) % (layers - 1), offset)
        for k in range(2):
            @pl.when(spot(layer, 1 - side, k) + spot(0, side, core) < n)
            def _():
                hold_come(k).wait_recv()
                hold_pass(k).start()

    for q in range(1, pieces):
        @pl.when(me + q * share < n)
        def _():
            coef_copy(q).start()

    tiles = waves // lanes

    def fill(tile):
        fill_lookup(tile, count_ref[0], fcos_ref, fsin_ref, high_ref, low_ref)

    @pl.when(layer > 0)
    def _():
        @pl.loop(0, tiles)
        def _(tile):
            fill(tile)

    def meet():
        @pl.when(layer == 0)
        def _():
            pl.semaphore_wait(barrier, n - len(corners))
            for dz in range(1, layers):
                for offset in corners:
                    give_seeds(dz, offset)

    expand_row = lax.broadcasted_iota(jnp.int32, (depth, lanes), 0)
    expand_lane = lax.broadcasted_iota(jnp.int32, (depth, lanes), 1) % pairs
    keep = (expand_row // (2 * slots)) * 2 + expand_row % 2 == expand_lane
    pair_at = lax.broadcasted_iota(jnp.int32, (room, lanes), 1) % pairs
    order_part = lax.broadcasted_iota(jnp.int32, (room, lanes), 0) * per + pair_at // 2

    def recur(u):
        owner = u // cut
        at = pl.multiple_of((u % cut) * (2 * room), 2 * room)
        order = order_part + u * (groups * per)
        first = order + pair_at % 2 + me * (2 * slots)
        m = order.astype(F32)
        square = seed_ref[0, pl.ds(groups, 1), :]

        def coupling(d):
            return ((d - m) * (d + m)) / ((2.0 * d - 1.0) * (2.0 * d + 1.0))

        def place(s, value):
            degree = first + 2 * s
            spread = lax.rsqrt((degree + 1).astype(F32) * float(waves))
            value = value * jnp.where(degree < waves, spread, 0.0)
            wide_ref[pl.ds(2 * s, room, stride=2 * slots), :] = value
            wide_ref[pl.ds(2 * s + 1, room, stride=2 * slots), :] = value

        before = seed_ref[owner, pl.ds(at, room), :]
        now = seed_ref[owner, pl.ds(at + room, room), :]
        place(0, before)
        place(1, now)
        degree = first.astype(F32)
        last = coupling(degree + 2.0)
        weight = jnp.sqrt(coupling(degree + 1.0) * last)
        for s in range(1, slots - 1):
            degree = degree + 2.0
            one, two = coupling(degree + 1.0), coupling(degree + 2.0)
            product = one * two
            inverse = lax.rsqrt(product)
            before, now = now, ((square - (one + last)) * now - weight * before) * inverse
            weight = product * inverse
            last = two
            place(s + 1, now)

    def partial(u):
        owner = u // cut

        @pl.when(me + owner < n)
        def _():
            @pl.when(u % cut == 0)
            def _():
                @pl.when(owner % share == 0)
                def _():
                    coef_copy(owner // share).wait()

                @pl.when(owner != me)
                def _():
                    seed_copy(owner, me).wait_recv()

            recur(u)
            for g in range(groups):
                at = u * groups + g
                values = coef_ref[pl.ds(pl.multiple_of(at * depth, depth), depth), :]
                one = wide_ref[pl.ds(g * 2 * slots, 2 * slots), :]
                tiled = jnp.where(keep, jnp.concatenate([one] * per, axis=0), 0.0)
                both = jnp.concatenate(split(tiled), axis=1)
                sums = lax.dot_general(both, values, (((0,), (0,)), ((), ())), preferred_element_type=F32)
                sums = (sums[:lanes] + sums[lanes:]).reshape(2, 2, layers, pairs, columns)
                sums_ref[u, :, :, :, pl.ds(g * pairs, pairs), :] = sums

        @pl.when(me + owner >= n)
        def _():
            sums_ref[u] = jnp.zeros((2, 2, layers, part, columns), F32)

    def held(q, place):
        return q // cut + 2 * place < n

    def compute(q, t):
        @pl.when(held(q, chip))
        def _():
            partial(q)

            near_copy(q, t).start()

    def merge_near(q, t):
        shared = held(q, across // 2)

        @pl.when(held(q, chip))
        def _():
            near_copy(q, t).wait_recv()

            for y in (0, 1):
                @pl.loop(0, layers)
                def _(z):
                    sums_ref[q, core, y, z] += near_ref[q, y, z]

            @pl.when(shared)
            def _():
                for dz in reversed(range(1, layers)):
                    side_copy(q, (layer + dz) % layers, t).start()

            @pl.when(jnp.logical_not(shared))
            def _():
                for at in range(1, layers):
                    @pl.when(layer == at)
                    def _():
                        for z in relays(at):
                            lone_copy(q, z).start()

                last_copy(q).start()

    def pass_on(q, t):
        shared = held(q, across // 2)

        @pl.when(held(q, chip))
        def _():
            @pl.when(shared)
            def _():
                side_come(q, t).wait_recv()

            for lower in range(1, layers - 1):
                @pl.when(layer == lower)
                def _():
                    up_come(q, lower).wait_recv()

            for dz in reversed(range(1, layers)):
                z = (layer + dz) % layers
                upward = jnp.logical_and(z > layer + 1, held(q, chip + 2))

                @pl.when(shared)
                def _():
                    sums_ref[q, core, side, z] += side_ref[q, z]

                @pl.when(jnp.logical_and(layer > 0, z > layer))
                def _():
                    sums_ref[q, core, side, z] += up_ref[q, z]

                @pl.when(upward)
                def _():
                    up_copy(q, z).start()

                @pl.when(jnp.logical_not(upward))
                def _():
                    far_copy(q, z).start()

            for at in range(layers - 1):
                straight = [z for z in reversed(range(at + 1, layers)) if not relayed(z, at)]
                if straight:
                    @pl.when(jnp.logical_and(jnp.logical_not(shared), layer == at))
                    def _():
                        for z in straight:
                            diag_copy(q, z).start()

        @pl.when(jnp.logical_and(jnp.logical_not(held(q, chip)), jnp.logical_and(shared, layer > 0)))
        def _():
            for lower in range(1, layers):
                @pl.when(layer == lower)
                def _():
                    lone_part(q, len(relays(lower))).wait_recv()
                    for z in relays(lower):
                        relay_copy(q, z).start()

    def unit_at(t):
        turn = n // 2
        block_at, place = t // turn, t % turn
        early = jnp.where(place == turn - 1, both + block_at, block_at * (turn - 1) + place)
        late = jnp.where(t < both + 2, t - 2, t)
        return jnp.where(layer == 0, jnp.where(t < 2 * turn, early, late), t)

    def finish(c):
        near_part = held(c * cut, chip)

        pieces = jnp.where(held(c * cut, across // 2), 1, 0)
        for dz in range(1, layers):
            source = (layer + dz) % layers
            passed = jnp.logical_and(source + 1 < layer, held(c * cut, 2 * (source + 1) + side))
            sends = jnp.logical_and(held(c * cut, 2 * source), jnp.logical_not(passed))
            pieces = pieces + jnp.where(sends, 1, 0)
        for number in range(1, layers + 1):
            @pl.when(pieces == number)
            def _():
                come(c, number).wait_recv()

        for half in range(cut):
            q = c * cut + half
            at = pl.ds(pl.multiple_of(q * part, part), part)

            @pl.when(near_part)
            def _():
                spectra_ref[at, :] = sums_ref[q, core, side, layer]

            @pl.when(jnp.logical_not(near_part))
            def _():
                spectra_ref[at, :] = jnp.zeros((part, columns), F32)

            for dz in range(1, layers):
                source = (layer + dz) % layers
                passed = jnp.logical_and(source + 1 < layer, held(q, 2 * (source + 1) + side))

                @pl.when(jnp.logical_and(held(q, 2 * source), jnp.logical_not(passed)))
                def _():
                    spectra_ref[at, :] += far_ref[source, q]

            @pl.when(held(q, across // 2))
            def _():
                spectra_ref[at, :] += side_ref[q, layer]

    temps_ref[...] = jnp.zeros(temps_ref.shape, F32)
    basis_copy.wait()
    early = jnp.logical_and(layer == 1, side == 0)

    def out_copy(step):
        at = pl.ds(step * FINE, FINE)
        return pltpu.make_async_copy(temps_ref.at[at, :], out_hbm.at[at, :], out_sem)

    def drain():
        for place in range(n // 2):
            count = cut * (n - 2 * place)
            pair = cut * (n - 2 * (place // 2 * 2 + 1))

            @pl.when(chip == place)
            def _():
                near = near_ref.at[pl.ds(0, count)]
                remote(near, near, near_send, near_recv.at[0], across).wait_send()
                side = side_ref.at[pl.ds(0, pair), pl.ds(0, layers - 1)]
                remote(side, side, side_send.at[0], side_recv.at[0], across).wait_send()
                last = side_ref.at[pl.ds(0, count), 0]
                remote(last, last, last_send.at[0], come_recv.at[0], across).wait_send()
                far = far_ref.at[pl.ds(0, layers - 1), pl.ds(0, count)]
                remote(far, far, far_send.at[0], come_recv.at[0], across).wait_send()

        for lower in range(layers):
            @pl.when(jnp.logical_and(layer == lower, side == 0))
            def _():
                for k in range(lone_send.shape[0]):
                    lone_part(both + k, layers - 1).wait_send()

            if lower:
                @pl.when(jnp.logical_and(layer == lower, side == 1))
                def _():
                    for k in range(lone_send.shape[0]):
                        lone_part(both + k, len(relays(lower))).wait_send()

    def stage(tile, after=None):
        @pl.loop((tile * lanes + own - 1) // own, ((tile + 1) * lanes + own - 1) // own)
        def _(c):
            finish(c)

        if after is not None:
            @pl.when(layer > 0)
            def _():
                drain()

        add_tile(tile, spectra_ref, basis_ref, high_ref, low_ref, temps_ref, after)

    @pl.loop(0, units + lag)
    def _(t):
        @pl.when(t == lag - 2)
        def _():
            meet()

        @pl.when(jnp.logical_and(layer == 0, jnp.logical_and(t >= 2 * lag, t < 2 * (lag + tiles))))
        def _():
            @pl.when(t % 2 == 0)
            def _():
                fill(t // 2 - lag)

        @pl.when(t < units)
        def _():
            compute(unit_at(t), t)

        @pl.when(jnp.logical_and(t >= 1, t <= units))
        def _():
            merge_near(unit_at(t - 1), t - 1)

        @pl.when(t == mine)
        def _():
            @pl.loop(0, both)
            def _(q):
                last_copy(q).start()

        @pl.when(jnp.logical_and(early, t == mine + 1))
        def _():
            stage(0)

        @pl.when(t >= lag)
        def _():
            pass_on(unit_at(t - lag), t - lag)

    for number in range(1, n):
        @pl.when(jnp.where(2 * me < n, n - me - 1, n - me) == number)
        def _():
            gone = send_ref.at[pl.ds(0, number)]
            remote(gone, gone, seed_send, seed_recv.at[0], across).wait_send()

    for k in range(2):
        @pl.when(jnp.logical_and(layer > 0, spot(layer, 1 - side, k) + spot(0, side, core) < n))
        def _():
            hold_pass(k).wait_send()

    @pl.loop(jnp.where(early, 1, 0), tiles - 1)
    def _(tile):
        stage(tile)

    stage(tiles - 1, lambda step: out_copy(step).start())

    @pl.when(layer == 0)
    def _():
        drain()

    pltpu.make_async_copy(temps_ref, out_hbm, out_sem).wait()


def exchanged_temps(coefficients, legendre, row_counts, basis, n, points):
    waves, _, slots, columns = coefficients.shape
    own, _, every, rows = legendre.shape
    dense = jnp.transpose(coefficients, (0, 2, 1, 3)).reshape(waves * slots * 2, columns)
    legs = jnp.transpose(legendre, (0, 1, 3, 2)).reshape(own * 2 * rows, every)
    layers = n // 4
    pairs = LANES // rows
    groups = own * 2 // pairs
    cut = 2 if groups % 2 == 0 else 1
    units = n * cut
    width = groups // cut * pairs
    room = -(-(groups // cut + 1) // 8) * 8
    block = cut * 2 * room
    dma = pltpu.SemaphoreType.DMA

    def body(*refs):
        exchange_kernel(n, waves, cut, *refs)

    return pl.pallas_call(
        body,
        out_shape=jax.ShapeDtypeStruct((points, 2 * basis.shape[1]), F32),
        in_specs=[pl.BlockSpec(memory_space=pltpu.SMEM)] + [pl.BlockSpec(memory_space=pl.ANY)] * 3,
        out_specs=pl.BlockSpec(memory_space=pl.ANY),
        scratch_shapes=[
            pltpu.VMEM((points, 2 * basis.shape[1]), F32),
            pltpu.VMEM(dense.shape, BF16),
            pltpu.VMEM(legs.shape, F32),
            pltpu.VMEM(basis.shape, F32),
            pltpu.VMEM((every, LANES), F32),
            pltpu.VMEM((n * block, LANES), F32),
            pltpu.VMEM((n, block, LANES), F32),
            pltpu.VMEM((n, block, LANES), F32),
            pltpu.VMEM((2, block, LANES), F32),
            pltpu.VMEM((room * 2 * slots, LANES), F32),
            pltpu.VMEM((units, 2, 2, layers, width, columns), F32),
            pltpu.VMEM((units, 2, layers, width, columns), F32),
            pltpu.VMEM((units, layers, width, columns), F32),
            pltpu.VMEM((layers, units, width, columns), F32),
            pltpu.VMEM((units, layers, width, columns), F32),
            pltpu.VMEM((2 * waves, columns), F32),
            pltpu.VMEM((FINE, LANES), F32),
            pltpu.VMEM((FINE, LANES), F32),
            pltpu.VMEM((waves // LANES, points, 2 * LANES), BF16),
            pltpu.VMEM((waves // LANES, points, 2 * LANES), BF16),
            dma((n // 2,)), dma, dma, dma, dma, dma((n,)), dma((2,)), dma((2,)),
            dma, dma((8,)),
            dma((1,)), dma((16,)),
            dma((1,)), dma((n,)),
            dma((1,)), dma((units - 4 * cut,)), dma((2 * cut,)), dma((2 * cut,)),
        ],
        compiler_params=pltpu.CompilerParams(
            collective_id=0, has_side_effects=True, vmem_limit_bytes=58 * 1024 * 1024
        ),
        name="exchanged_temps",
    )(row_counts, dense, legs, basis)


def plain_temps(spectra, row_counts, basis, points):
    tiles = spectra.shape[0] // (2 * LANES)

    def body(count_ref, spectra_ref, basis_ref, temps_ref, fcos_ref, fsin_ref, high_ref, low_ref):
        temps_ref[...] = jnp.zeros(temps_ref.shape, F32)
        for tile in range(tiles):
            fill_lookup(tile, count_ref[0], fcos_ref, fsin_ref, high_ref, low_ref)
            add_tile(tile, spectra_ref, basis_ref, high_ref, low_ref, temps_ref)

    vmem = pl.BlockSpec(memory_space=pltpu.VMEM)
    return pl.pallas_call(
        body,
        out_shape=jax.ShapeDtypeStruct((points, 2 * basis.shape[1]), F32),
        in_specs=[pl.BlockSpec(memory_space=pltpu.SMEM), vmem, vmem],
        out_specs=vmem,
        scratch_shapes=[pltpu.VMEM((FINE, LANES), F32)] * 2 + [pltpu.VMEM((tiles, points, 2 * LANES), BF16)] * 2,
        name="plain_temps",
    )(row_counts, spectra, basis)


def row_kernel(
    count_ref, temps_hbm, absorb_ref, peak_ref, width_ref, out_hbm, temps_ref, out_ref, pair_ref, rhigh_ref, rlow_ref,
    temps_sem, out_sem,
):
    levels = absorb_ref.shape[1]
    points = temps_ref.shape[0]
    chunk = pair_ref.shape[0] // 2
    steps = points // chunk
    piece = chunk // PARTS

    def come(step):
        at = pl.ds(pl.multiple_of(step * chunk, chunk), chunk)
        return pltpu.make_async_copy(temps_hbm.at[at, :], temps_ref.at[at, :], temps_sem.at[step])

    for step in range(steps):
        come(step).start()
    height = lax.broadcasted_iota(jnp.int32, rlow_ref.shape, 0)
    offsets = (height - peak_ref[...]).astype(F32) / width_ref[...]
    shape = jnp.exp(-offsets * offsets)
    high, low = split(shape / jnp.sum(shape, axis=0, keepdims=True))
    rhigh_ref[pl.ds(0, levels), :] = high
    rhigh_ref[pl.ds(levels, levels), :] = high
    rlow_ref[...] = low

    @pl.loop(0, steps)
    def _(step):
        come(step).wait()
        first = pl.multiple_of(step * chunk, chunk)
        temps = temps_ref[pl.ds(first, chunk), :]
        temps = jnp.concatenate((temps[:, :levels], temps[:, levels:]), axis=0)
        source = jnp.exp(0.5 * temps)
        layers = absorb_ref[...] * source
        before = lax.broadcasted_iota(jnp.int32, (2 * levels, levels), 0) % levels
        after = lax.broadcasted_iota(jnp.int32, (2 * levels, levels), 1)
        upper = jnp.where(before < after, 1.0, 0.0).astype(BF16)
        layers_high, layers_low = split(layers)
        above = dot(jnp.concatenate((layers_high, layers_low), axis=1), upper)
        emitted = source * jnp.exp(-above) * (1.0 - jnp.exp(-layers))
        place = first + lax.broadcasted_iota(jnp.int32, (2 * chunk, levels), 0) % chunk
        emitted = jnp.where(place < count_ref[0], emitted, 0.0)
        pair_ref[...] = jnp.concatenate(split(emitted), axis=1)
        for half in range(2):
            for part in range(PARTS):
                pair = pair_ref[pl.ds(half * chunk + part * piece, piece), :]
                bright = dot(pair, rhigh_ref[...]) + dot(pair[:, :levels], rlow_ref[...])
                at = pl.ds(pl.multiple_of(first + part * piece, piece), piece)
                out_ref[0, half, at, :] = bright
                pltpu.make_async_copy(out_ref.at[0, half, at, :], out_hbm.at[0, half, at, :], out_sem).start()

    pltpu.make_async_copy(out_ref, out_hbm, out_sem).wait()


def radiate_row(temps, row_counts, absorb, peak_level, width):
    points = temps.shape[0]
    levels, channels = absorb.shape[0], width.shape[0]
    span = SPAN if points % SPAN == 0 else FINE
    vmem = pl.BlockSpec(memory_space=pltpu.VMEM)
    return pl.pallas_call(
        row_kernel,
        out_shape=jax.ShapeDtypeStruct((1, 2, points, channels), F32),
        in_specs=[pl.BlockSpec(memory_space=pltpu.SMEM), pl.BlockSpec(memory_space=pl.ANY), vmem, vmem, vmem],
        out_specs=pl.BlockSpec(memory_space=pl.ANY),
        scratch_shapes=[
            pltpu.VMEM(temps.shape, F32),
            pltpu.VMEM((1, 2, points, channels), F32),
            pltpu.VMEM((2 * span, 2 * levels), BF16),
            pltpu.VMEM((2 * levels, channels), BF16),
            pltpu.VMEM((levels, channels), BF16),
            pltpu.SemaphoreType.DMA((points // span,)),
            pltpu.SemaphoreType.DMA,
        ],
        name="row_radiance",
    )(row_counts, temps, absorb[None, :], peak_level[None, :], width[None, :])


def moved_coefficients(coefficients, legendre):
    waves, _, slots, _ = coefficients.shape
    first = lax.axis_index("spec") * slots
    spread = prior_spread(jnp.arange(waves, dtype=jnp.int32), first + jnp.arange(slots, dtype=jnp.int32), waves)
    scaled = coefficients.astype(F32) * spread[..., None]
    spectral = lax.all_to_all(scaled, "spec", split_axis=0, concat_axis=2, tiled=True)
    sums = jnp.einsum("mpsj,mpsc->mpjc", legendre, spectral, precision=PRECISE)
    sums = lax.all_to_all(sums, "spec", split_axis=2, concat_axis=0, tiled=True)
    return sums.reshape(2 * waves, sums.shape[-1])


def on_device(coefficients, legendre, row_counts, basis, absorb, peak_level, width):
    own, _, every, rows = legendre.shape
    waves, _, slots, columns = coefficients.shape
    n = waves // own
    fits = n == rows and n % 8 == 0 and LANES % n == 0 and every == n * slots and columns == LANES
    fits = fits and (LANES // n) % 8 == 0 and own % (LANES // n) == 0 and slots % 4 == 0 and waves % LANES == 0
    if fits and (slots * LANES // n) % 16 == 0 and 2 * waves >= 2 * slots * n:
        temps = exchanged_temps(coefficients, legendre, row_counts, basis, n, NLON)
    else:
        spectra = moved_coefficients(coefficients, legendre)
        temps = plain_temps(spectra, row_counts, basis, NLON)
    return radiate_row(temps, row_counts, absorb, peak_level, width)


def solution(mesh):
    placed = (
        P("draws", None, "spec", None),
        P("spec", None, None, None),
        P("spec"),
        P(),
        P(),
        P(),
        P(),
    )
    return jax.shard_map(
        on_device,
        mesh=mesh,
        in_specs=placed,
        out_specs=P(("draws", "spec"), None, None, None),
        check_vma=False,
    )
```
